256 devices in a mesh: member: 16 (over y, x), section: 8 (over z), tensor: 2 (over core).
Axes of the slice: x: 4, y: 4, z: 8, core: 2. Of those that a mesh axis runs over, the one named last changes fastest.
Arguments:
- hidden_input: bfloat16 [16, 8, 2, 128, 4096], P('member', 'section'), may hold values from -6 to 6
- document_index: int32 [8, 2, 128], P('section'), may hold values from 0 to 7, never falling along the last dimension, each value on 1 to 32 neighbouring positions
- query_key_value_weight: bfloat16 [8, 4096, 4, 768], P('section', 'member', 'tensor'), may hold values from -0.09375 to 0.09375
- output_weight: bfloat16 [8, 2048, 4096], P('section', 'tensor', 'member'), may hold values from -0.125 to 0.125
- adapter_down: bfloat16 [16, 8, 2048, 16], P('member', 'section', 'tensor'), may hold values from -0.125 to 0.125
- adapter_up: bfloat16 [16, 8, 16, 4096], P('member', 'section'), may hold values from -1.5 to 1.5
- attention_gain: float32 [16, 8, 4096], P('member', 'section'), may hold values from 0.6 to 5, as said below
- final_norm_gain: float32 [16, 4096], P('member', 'tensor'), may hold values from 0.25 to 1.75
Outputs:
- averaged: bfloat16 [8, 2, 128, 4096], P('section', None, None, 'tensor')
The draws below stay inside these ranges and needn't reach their ends.
Inputs may be any that keep to these rules, and one draw needn't show every extreme that they name: `document_index`: along each micro-batch the document number never falls; each document spans at most 32 positions and one spans exactly that many. `attention_gain`: positive gains.
All inputs are finite; a program needn't handle non-finite values.
Results may differ from the reference program's by a relative error of at most 0.038.
The reference program's roundings to bfloat16 on the way count: a program that leaves them out, or rounds other values in their place, can miss the bound.
Values may be sent and summed in bfloat16 or wider, within the bound.
A program may use at most 128 MiB of HBM per device.

```python
import math
import jax
import jax.numpy as jnp
import numpy as np
from jax import lax

MODEL_WIDTH = 4096
QUERY_HEADS = 16
KV_HEADS = 4
HEAD_WIDTH = 128
ADAPTER_RANK = 16
SEQ = 128
MB = 2
TICKS = 2
GROUP = 4
TEACHER_COUNT = 16
LOOP_SECTIONS = 8
N_MEMBER = 16
N_TENSOR = 2


def draw_attention_gain(key, part):
    uniform_draw = jax.random.uniform(key, (TEACHER_COUNT, LOOP_SECTIONS, MODEL_WIDTH), jnp.float32)
    return 0.6 + 0.8 * uniform_draw


def steps_of(stream_key, dims, split, low, top_value):
    loudness = 1.0
    for dim, blocks in split:
        steps = jax.random.uniform(jax.random.fold_in(jax.random.fold_in(stream_key, 6), dim), (blocks,), jnp.float32, low / len(split), top_value / len(split))
        loudness = loudness * jnp.repeat(jnp.exp(steps), dims[dim] // blocks).reshape((-1,) + (1,) * (len(dims) - 1 - dim))
    return loudness


def length_profile(number_of, total, most, slope):
    weights = [(1 << 20) // math.isqrt(rank ** slope) + 1 for rank in range(2, number_of + 1)]
    spare, counts = total - most - (number_of - 1), [1] * (number_of - 1)
    while spare > 0:
        candidates = [i for i in range(number_of - 1) if counts[i] < most]
        mass, remaining = sum([weights[i] for i in candidates]), spare
        for i in candidates:
            more = min(most - counts[i], max(1, remaining * weights[i] // mass), spare)
            counts[i] = counts[i] + more
            spare = spare - more
    return np.array([most] + counts)


def uneven_parts(own_key, amount, total, most, skew):
    if amount == 2:
        one = jax.random.randint(own_key, (), max(1, total - most), min(most, total - 1) + 1)
        return jnp.stack([one, total - one])
    sizes = jnp.asarray(length_profile(amount, total, most, skew), jnp.int32)
    couples = (amount - 1) // 2
    donor, taker = sizes[1:1 + 2 * couples:2], sizes[2:2 + 2 * couples:2]
    slack = jnp.minimum(donor - 1, most - taker)
    moved = jax.random.randint(jax.random.fold_in(own_key, 1), (couples,), 0, 1 << 20) % (slack + 1)
    sizes = sizes.at[1:1 + 2 * couples:2].set(donor - moved).at[2:2 + 2 * couples:2].set(taker + moved)
    return sizes[jax.random.permutation(jax.random.fold_in(own_key, 2), amount)]


def bell_draw(stream_key, dims, width, reach, cuts=(), kind=jnp.bfloat16):
    gain = steps_of(stream_key, dims, cuts, -0.22, 0.18) if cuts else 1.0
    drawn = jax.random.normal(stream_key, dims, jnp.float32) * width * gain
    return jnp.minimum(jnp.maximum(drawn, -reach), reach).astype(kind)


def setup_inputs(seed: int = 0) -> dict:
    keys = jax.random.split(jax.random.key(seed), 9)
    hidden_input = bell_draw(keys[0], (TEACHER_COUNT, LOOP_SECTIONS, MB, SEQ, MODEL_WIDTH), 1.0, 6.0, ((0, 16), (1, 8)))
    document_index = jax.vmap(lambda own: jnp.searchsorted(jnp.cumsum(uneven_parts(own, 8, SEQ, SEQ // 4, 0)), jnp.arange(SEQ), side="right"))(jax.random.split(keys[1], LOOP_SECTIONS * MB)).reshape((LOOP_SECTIONS, MB, SEQ)).astype(jnp.int32)
    query_key_value_weight = bell_draw(keys[2], (LOOP_SECTIONS, MODEL_WIDTH, KV_HEADS, (GROUP + 2) * HEAD_WIDTH), MODEL_WIDTH ** -0.5, 0.09375, ((0, 8), (1, 16), (2, 2)))
    output_weight = bell_draw(keys[3], (LOOP_SECTIONS, QUERY_HEADS * HEAD_WIDTH, MODEL_WIDTH), (QUERY_HEADS * HEAD_WIDTH) ** -0.5, 0.125, ((0, 8), (1, 2), (2, 16)))
    adapter_down = bell_draw(keys[4], (TEACHER_COUNT, LOOP_SECTIONS, QUERY_HEADS * HEAD_WIDTH, ADAPTER_RANK), (QUERY_HEADS * HEAD_WIDTH) ** -0.5, 0.125, ((0, 16), (1, 8), (2, 2)))
    adapter_up = bell_draw(keys[5], (TEACHER_COUNT, LOOP_SECTIONS, ADAPTER_RANK, MODEL_WIDTH), ADAPTER_RANK ** -0.5, 1.5, ((0, 16), (1, 8)))
    attention_gain = draw_attention_gain(jax.random.fold_in(keys[8], 71), 0)
    final_norm_gain = jnp.clip(1.0 + 0.15 * jax.random.normal(keys[7], (TEACHER_COUNT, MODEL_WIDTH), jnp.float32), 0.25, 1.75)
    return dict(hidden_input=hidden_input, document_index=document_index, query_key_value_weight=query_key_value_weight, output_weight=output_weight, adapter_down=adapter_down, adapter_up=adapter_up, attention_gain=attention_gain, final_norm_gain=final_norm_gain)


def norm_rows(values, gain_row):
    return values * lax.rsqrt(lax.optimization_barrier(jnp.mean(values * values, axis=-1, keepdims=True)) + 1e-05) * gain_row

def rope_tables(seq_len, head_dim):
    position = jnp.arange(seq_len, dtype=jnp.float32)
    frequency = jnp.exp(jnp.arange(head_dim // 2, dtype=jnp.float32) * (-2.0 * math.log(500000.0) / head_dim))
    angles = position[:, None] * frequency[None, :]
    return (jnp.cos(angles), jnp.sin(angles))

def rotate(values, cosine_table, sine_table):
    half_dim = values.shape[-1] // 2
    first_half = values[..., :half_dim]
    second_half = values[..., half_dim:]
    bcast_shape = (1, values.shape[1]) + (1,) * (values.ndim - 3) + (half_dim,)
    cosine_part = cosine_table.reshape(bcast_shape)
    sine_part = sine_table.reshape(bcast_shape)
    return jnp.concatenate([first_half * cosine_part - second_half * sine_part, second_half * cosine_part + first_half * sine_part], axis=-1)

def attention(projected, doc_rows):
    group_size = projected.shape[3] - 2
    seq_len = projected.shape[1]
    head_dim = projected.shape[-1]
    cosine_table, sine_table = rope_tables(seq_len, head_dim)
    queries = rotate(projected[:, :, :, :group_size, :], cosine_table, sine_table).astype(jnp.bfloat16)
    key_rows = rotate(projected[:, :, :, group_size, :], cosine_table, sine_table).astype(jnp.bfloat16)
    value_rows = projected[:, :, :, group_size + 1, :].astype(jnp.bfloat16)
    scores = jnp.einsum('bskgd,btkd->bkgst', queries.astype(jnp.float32), key_rows.astype(jnp.float32)) / math.sqrt(head_dim)
    position = jnp.arange(seq_len)
    causal = position[:, None] >= position[None, :]
    same_doc = doc_rows[:, :, None] == doc_rows[:, None, :]
    allowed = (causal[None] & same_doc)[:, None, None]
    scores = jnp.where(allowed, scores, -1e+30)
    row_max = lax.optimization_barrier(jnp.max(scores, axis=-1, keepdims=True))
    weights = jnp.exp(scores - row_max)
    weights = (weights / lax.optimization_barrier(jnp.sum(weights, axis=-1, keepdims=True))).astype(jnp.bfloat16)
    context = jnp.einsum('bkgst,btkd->bskgd', weights.astype(jnp.float32), value_rows.astype(jnp.float32))
    return context.astype(jnp.bfloat16).reshape(doc_rows.shape[0] * seq_len, -1)

def apply_layer(hidden, doc_rows, qkv_weight, out_weight, down_matrix, up_matrix, gain_row):
    hidden_f = hidden.astype(jnp.float32)
    normed = norm_rows(hidden_f, gain_row).astype(jnp.bfloat16)
    model_dim = hidden.shape[-1]
    batch_count, seq_len = doc_rows.shape
    projected = jnp.dot(normed.reshape(-1, model_dim), qkv_weight.reshape(model_dim, -1), preferred_element_type=jnp.float32)
    projected = projected.reshape(batch_count, seq_len, qkv_weight.shape[1], -1, HEAD_WIDTH)
    context = attention(projected, doc_rows)
    shard_width = context.shape[1] // N_TENSOR
    summed = jnp.zeros((context.shape[0], model_dim), jnp.float32)
    for shard_index in range(N_TENSOR):
        lower = shard_index * shard_width
        upper = lower + shard_width
        piece_cols = context[:, lower:upper]
        main_term = jnp.dot(piece_cols, out_weight[lower:upper], preferred_element_type=jnp.float32)
        low_rank = jnp.dot(piece_cols, down_matrix[lower:upper], preferred_element_type=jnp.float32).astype(jnp.bfloat16)
        partial_value = (main_term + jnp.dot(low_rank, up_matrix, preferred_element_type=jnp.float32)).astype(jnp.bfloat16)
        partial_value = lax.optimization_barrier(partial_value)
        summed = summed + partial_value.astype(jnp.float32)
    return (hidden_f + summed.reshape(hidden.shape)).astype(jnp.bfloat16)

def reference(hidden_input, document_index, query_key_value_weight, output_weight, adapter_down, adapter_up, attention_gain, final_norm_gain):
    total = jnp.zeros(hidden_input.shape[1:], jnp.float32)
    for teacher_member in range(N_MEMBER):
        relay_states = hidden_input[teacher_member]
        document_state = document_index

        def section_block_layer(inputs):
            return apply_layer(*inputs)
        for tick_step in range(TICKS):
            relay_states = lax.map(section_block_layer, (relay_states, document_state, query_key_value_weight, output_weight, adapter_down[teacher_member], adapter_up[teacher_member], attention_gain[teacher_member]))
            relay_states = jnp.roll(relay_states, 1, axis=0)
            document_state = jnp.roll(document_state, 1, axis=0)
        total = total + norm_rows(relay_states.astype(jnp.float32), final_norm_gain[teacher_member])
    return (total / N_MEMBER).astype(jnp.bfloat16)
```

```python
import math

import jax
import jax.numpy as jnp
import numpy as np
from jax import lax
from jax.experimental import pallas as pl
from jax.experimental.pallas import tpu as pltpu
from jax.sharding import PartitionSpec as P

HEAD_WIDTH = 128
GROUP = 4
WIDTH = 4096
ROWS = 256
SEQ = 128
MEMBERS = 16
SIDE = 4
EPS = 1e-05
MESH = pl.DeviceIdType.MESH
F32 = jnp.float32
BF16 = jnp.bfloat16


def rope_tables():
    position = np.arange(SEQ, dtype=np.float32)
    frequency = np.exp(
        np.arange(HEAD_WIDTH // 2, dtype=np.float32)
        * np.float32(-2.0 * math.log(500000.0) / HEAD_WIDTH)
    ).astype(np.float32)
    angles = (position[:, None] * frequency[None, :]).astype(np.float32)
    cosine, sine = np.cos(angles), np.sin(angles)
    return (
        np.concatenate([cosine, cosine], axis=1).astype(np.float32),
        np.concatenate([-sine, sine], axis=1).astype(np.float32),
    )


def wrap(value):
    return lax.rem(value + 2 * SIDE, SIDE)


class Torus:
    def __init__(self):
        self.member = lax.axis_index("member")
        self.x = lax.rem(self.member, SIDE)
        self.y = self.member // SIDE

    def at(self, part, du, dv):
        dx, dy = (du, dv) if part == 0 else (dv, du)
        return wrap(self.y + dy) * SIDE + wrap(self.x + dx)


class Gather:
    order = (0, -1, 1, 2)

    def __init__(self, torus, own, slot, whole, send_sem, recv_sem):
        self.torus, self.own, self.slot, self.whole = torus, own, slot, whole
        self.send_sem, self.recv_sem = send_sem, recv_sem

    def start(self, src, dst, part, du, dv, index):
        pltpu.make_async_remote_copy(
            src_ref=src,
            dst_ref=dst,
            send_sem=self.send_sem.at[part],
            recv_sem=self.recv_sem.at[part, index],
            device_id={"member": self.torus.at(part, du, dv)},
            device_id_type=MESH,
        ).start()

    def wait(self, part, du, dv, index):
        ref = self.slot(part, self.torus.at(part, du, dv), None)
        pltpu.make_async_remote_copy(
            src_ref=ref,
            dst_ref=ref,
            send_sem=self.send_sem.at[part],
            recv_sem=self.recv_sem.at[part, index],
            device_id={"member": self.torus.at(part, 1, 0)},
            device_id_type=MESH,
        ).wait_recv()

    def full(self, part, du, dv):
        return self.slot(part, self.torus.at(part, du, dv), None)

    def half(self, part, du, dv, which):
        return self.slot(part, self.torus.at(part, du, dv), which)

    def spread(self, part, q):
        du = self.order[q]
        here = self.full(part, du, 0)
        src = self.own(part) if q == 0 else here
        self.start(src, here, part, 0, 1, 3 + q)
        self.start(src, here, part, 0, -1, 7 + q)

    def first(self, part):
        here = self.full(part, 0, 0)
        self.start(self.own(part), here, part, 1, 0, 0)
        self.start(self.own(part), here, part, -1, 0, 1)

    def line(self, part):
        self.wait(part, -1, 0, 0)
        ref = self.half(part, -1, 0, 0)
        self.start(ref, ref, part, 1, 0, 2)
        self.spread(part, 1)
        self.wait(part, 1, 0, 1)
        ref = self.half(part, 1, 0, 1)
        self.start(ref, ref, part, -1, 0, 2)
        self.spread(part, 2)

    def far(self, part):
        self.wait(part, 2, 0, 2)
        self.spread(part, 3)

    def cross(self, part, q):
        du = self.order[q]
        self.wait(part, du, -1, 3 + q)
        ref = self.half(part, du, -1, 0)
        self.start(ref, ref, part, 0, 1, 11 + q)
        self.wait(part, du, 1, 7 + q)
        ref = self.half(part, du, 1, 1)
        self.start(ref, ref, part, 0, -1, 11 + q)

    def last(self, part, q):
        self.wait(part, self.order[q], 2, 11 + q)

    def sent(self, part):
        ref = self.whole(part)
        pltpu.make_async_remote_copy(
            src_ref=ref,
            dst_ref=ref,
            send_sem=self.send_sem.at[part],
            recv_sem=self.recv_sem.at[part, 0],
            device_id={"member": self.torus.at(part, 1, 0)},
            device_id_type=MESH,
        ).wait_send()


def rotate(values, cosine, sine):
    return (values * cosine + pltpu.roll(values, HEAD_WIDTH // 2, 1) * sine).astype(BF16)


def kernel(
    hidden_in, docs_in, qkv_in, out_in, down_ref, up_ref, gain_ref, final_ref, cos_ref, sin_ref,
    out_ref,
    wq, wo, hv, nrm, proj, ctx, low, docs_next,
    own_part, peer_send, peer_recv, h_send, h_next,
    part2, send2, recv2, h_last, square, square_peer, rows_out, rows_in, mean_own, mean_in,
    ag_send, ag_recv, local_sem, peer_s, peer_r, hop_s, hop_r, fwd_s, fwd_r,
    two_s, two_r, misc_s, misc_r, scatter_s, scatter_r,
):
    torus = Torus()
    member = torus.member
    section = lax.axis_index("section")
    tensor = lax.axis_index("tensor")
    other = 1 - tensor
    sections = 8
    after = lax.rem(section + 1, sections)
    before = lax.rem(section + sections - 1, sections)

    barrier = pltpu.get_barrier_semaphore()

    def greet(i, carry):
        pl.semaphore_signal(
            barrier, inc=1, device_id={"member": lax.rem(member + i, MEMBERS)}, device_id_type=MESH
        )
        return carry

    lax.fori_loop(1, MEMBERS, greet, 0)
    pl.semaphore_signal(barrier, inc=1, device_id={"tensor": other}, device_id_type=MESH)
    pl.semaphore_signal(barrier, inc=1, device_id={"section": after}, device_id_type=MESH)
    pl.semaphore_signal(barrier, inc=1, device_id={"section": before}, device_id_type=MESH)

    load_h = pltpu.make_async_copy(hidden_in, hv, local_sem.at[0])
    load_h.start()
    pl.semaphore_wait(barrier, MEMBERS + 2)

    def qkv_slot(part, slot, which):
        lower = pl.multiple_of(slot * 256 + part * 128 + (64 if which == 1 else 0), 64)
        return wq.at[pl.ds(lower, 128 if which is None else 64)]

    qkv = Gather(
        torus,
        lambda part: qkv_in.at[pl.ds(part * 128, 128)],
        qkv_slot,
        lambda part: wq.at[pl.ds(0, 15 * 128)],
        ag_send.at[0],
        ag_recv.at[0],
    )

    def out_slot(part, slot, which):
        if which is None:
            return wo.at[slot, part]
        return wo.at[slot, part, pl.ds(which * 512, 512)]

    outw = Gather(
        torus,
        lambda part: out_in.at[:, pl.ds(part * 128, 128)],
        out_slot,
        lambda part: wo.at[pl.ds(0, 15), part],
        ag_send.at[1],
        ag_recv.at[1],
    )
    both = (0, 1)
    for part in both:
        qkv.first(part)
    for part in both:
        qkv.spread(part, 0)

    own_rows = pl.ds(pl.multiple_of(member * 256, 256), 256)
    load_q = pltpu.make_async_copy(qkv_in, wq.at[own_rows], local_sem.at[1])
    load_q.start()
    load_o = [
        pltpu.make_async_copy(
            out_in.at[:, pl.ds(part * 128, 128)], wo.at[member, part], local_sem.at[2 + part]
        )
        for part in both
    ]
    for copy in load_o:
        copy.start()
    pass_docs = pltpu.make_async_remote_copy(
        docs_in, docs_next, misc_s.at[0], misc_r.at[0], {"section": after}, MESH
    )
    pass_docs.start()
    load_h.wait()

    def norm_first(i, carry):
        rows = pl.ds(pl.multiple_of(i * 16, 16), 16)
        h = hv[rows, :].astype(F32)
        scale = lax.rsqrt(jnp.mean(h * h, axis=-1, keepdims=True) + EPS)
        nrm[rows, :] = (h * scale * gain_ref[...]).astype(BF16)
        return carry

    lax.fori_loop(0, ROWS // 16, norm_first, 0)

    def project():
        def block(n, carry):
            columns = pl.ds(pl.multiple_of(n * 256, 256), 256)
            proj[:, columns] = jnp.dot(nrm[...], wq[:, columns], preferred_element_type=F32)
            return carry

        lax.fori_loop(0, 6, block, 0)

    ahead = lax.broadcasted_iota(jnp.int32, (SEQ, SEQ), 0) >= lax.broadcasted_iota(
        jnp.int32, (SEQ, SEQ), 1
    )

    def attend(docs_ref):
        for batch in range(2):
            numbers = jnp.broadcast_to(docs_ref[batch : batch + 1, :], (SEQ, SEQ)).astype(F32)
            allowed = ahead & (numbers == numbers.T)
            allowed = jnp.concatenate([allowed.astype(F32)] * GROUP, axis=0) > 0.5
            rows = slice(batch * SEQ, (batch + 1) * SEQ)
            cosine, sine = cos_ref[...], sin_ref[...]

            def head(k, carry):
                base = k * (GROUP + 2) * HEAD_WIDTH

                def piece(g):
                    return proj[rows, pl.ds(pl.multiple_of(base + g * 128, 128), 128)]

                queries = jnp.concatenate(
                    [rotate(piece(g), cosine, sine) for g in range(GROUP)], axis=0
                )
                keys = rotate(piece(GROUP), cosine, sine)
                values = piece(GROUP + 1).astype(BF16)
                scores = lax.dot_general(
                    queries, keys, (((1,), (1,)), ((), ())), preferred_element_type=F32
                ) * (1.0 / math.sqrt(HEAD_WIDTH))
                scores = jnp.where(allowed, scores, -1e30)
                weights = jnp.exp(scores - jnp.max(scores, axis=-1, keepdims=True))
                weights = (weights / jnp.sum(weights, axis=-1, keepdims=True)).astype(BF16)
                context = jnp.dot(weights, values, preferred_element_type=F32).astype(BF16)
                for g in range(GROUP):
                    columns = pl.ds(pl.multiple_of(k * 512 + g * 128, 128), 128)
                    ctx[rows, columns] = context[g * SEQ : (g + 1) * SEQ]
                return carry

            lax.fori_loop(0, 2, head, 0)
        low[...] = lax.dot_general(
            ctx[...], down_ref[...], (((1,), (1,)), ((), ())), preferred_element_type=F32
        ).astype(BF16)

    for part in both:
        qkv.line(part)
    for part in both:
        qkv.cross(part, 0)
    for part in both:
        qkv.far(part)
    for q in (1, 2, 3):
        for part in both:
            qkv.cross(part, q)
    for part in both:
        outw.first(part)
    for part in both:
        outw.spread(part, 0)
    for q in range(SIDE):
        for part in both:
            qkv.last(part, q)
    load_q.wait()
    project()
    for part in both:
        outw.line(part)
    attend(docs_in)
    for copy in load_o:
        copy.wait()

    def slot_of(part, du, dv):
        dx = jnp.where(part == 0, du, dv)
        dy = jnp.where(part == 0, dv, du)
        return wrap(torus.y + dy) * SIDE + wrap(torus.x + dx)

    def column_of(part, slot):
        return pl.ds(pl.multiple_of(slot * 256 + part * 128, 128), 128)

    def partial(part, slot):
        main = jnp.dot(ctx[...], wo[slot, part], preferred_element_type=F32)
        return (
            main + jnp.dot(low[...], up_ref[:, column_of(part, slot)], preferred_element_type=F32)
        ).astype(BF16)

    def peer_copy(i):
        return pltpu.make_async_remote_copy(
            peer_send.at[i], peer_recv.at[i], peer_s.at[i], peer_r.at[i], {"tensor": other}, MESH
        )

    def hop_copy(i, slot):
        return pltpu.make_async_remote_copy(
            h_send.at[i], h_next.at[tensor, slot], hop_s.at[i], hop_r.at[i], {"section": after}, MESH
        )

    def forward_copy(i, part, slot):
        ref = h_next.at[part, slot]
        return pltpu.make_async_remote_copy(
            ref, ref, fwd_s.at[i], fwd_r.at[i], {"tensor": other}, MESH
        )

    def start_block(i, du, dv):
        peer_send[i] = partial(other, slot_of(other, du, dv))
        peer_copy(i).start()
        own_part[i] = partial(tensor, slot_of(tensor, du, dv))

    def finish_block(i, du, dv):
        slot = slot_of(tensor, du, dv)
        peer_copy(i).wait_recv()
        total = own_part[i].astype(F32) + peer_recv[i].astype(F32)
        h_send[i] = (hv[:, column_of(tensor, slot)].astype(F32) + total).astype(BF16)
        hop_copy(i, slot).start()

    def arrive(i, du, dv):
        slot = slot_of(tensor, du, dv)
        hop_copy(i, slot).wait_recv()
        forward_copy(i, tensor, slot).start()

    order = Gather.order
    blocks = [(q, 0) for q in range(4)]
    for q in range(4):
        blocks += [(q, -1), (q, 1)]
    blocks += [(q, 2) for q in range(4)]
    progress = [0, 0]

    def run(count):
        for i in range(count[0], count[1]):
            q, dv = blocks[i]
            start_block(i, order[q], dv)
            if i >= 1:
                q, dv = blocks[i - 1]
                finish_block(i - 1, order[q], dv)
            if i >= 4:
                q, dv = blocks[i - 4]
                arrive(i - 4, order[q], dv)

    run((0, 1))
    for part in both:
        outw.cross(part, 0)
    run((1, 3))
    for part in both:
        outw.far(part)
    run((3, 4))
    for q in (1, 2, 3):
        for part in both:
            outw.cross(part, q)
        run((4 + 2 * (q - 1), 6 + 2 * (q - 1)))
    run((10, 12))
    for q in range(SIDE):
        for part in both:
            outw.last(part, q)
        run((12 + q, 13 + q))
    q, dv = blocks[15]
    finish_block(15, order[q], dv)
    for i in range(12, 16):
        q, dv = blocks[i]
        arrive(i, order[q], dv)
    for i in range(16):
        q, dv = blocks[i]
        forward_copy(i, other, slot_of(other, order[q], dv)).wait_recv()
    pass_docs.wait_recv()

    def norm_second(i, carry):
        rows = pl.ds(pl.multiple_of(i * 32, 32), 32)
        total = jnp.zeros((32, 128), F32)
        for slot in range(MEMBERS):
            for part in both:
                h = h_next[part, slot, rows, :].astype(F32)
                total = total + h * h
        scale = lax.rsqrt(jnp.sum(total, axis=-1, keepdims=True) * (1.0 / WIDTH) + EPS)
        scale = jnp.broadcast_to(scale, (32, 128))
        for slot in range(MEMBERS):
            for part in both:
                columns = slice(slot * 256 + part * 128, slot * 256 + part * 128 + 128)
                h = h_next[part, slot, rows, :].astype(F32)
                nrm[rows, columns] = (h * scale * gain_ref[:, columns]).astype(BF16)
        return carry

    lax.fori_loop(0, ROWS // 32, norm_second, 0)
    project()
    attend(docs_next)

    def partial_pair(slot):
        weights = jnp.concatenate([wo[slot, 0], wo[slot, 1]], axis=1)
        columns = pl.ds(pl.multiple_of(slot * 256, 256), 256)
        main = jnp.dot(ctx[...], weights, preferred_element_type=F32)
        return (main + jnp.dot(low[...], up_ref[:, columns], preferred_element_type=F32)).astype(BF16)

    def two_copy(i):
        return pltpu.make_async_remote_copy(
            send2.at[i], recv2.at[i], two_s.at[i], two_r.at[i], {"tensor": other}, MESH
        )

    def give(i, carry):
        send2[i] = partial_pair(other * 8 + i)
        two_copy(i).start()
        return carry

    lax.fori_loop(0, 8, give, 0)

    def keep(i, carry):
        part2[i] = partial_pair(tensor * 8 + i)
        return carry

    lax.fori_loop(0, 8, keep, 0)
    square[...] = jnp.zeros_like(square)

    def settle(i, carry):
        two_copy(i).wait_recv()
        slot = tensor * 8 + i
        for part in both:
            cols = slice(part * 128, part * 128 + 128)
            total = part2[i, :, cols].astype(F32) + recv2[i, :, cols].astype(F32)
            h = (h_next[part, slot].astype(F32) + total).astype(BF16)
            h_last[i, :, cols] = h
            h = h.astype(F32)
            square[...] += h * h
        return carry

    lax.fori_loop(0, 8, settle, 0)
    swap = pltpu.make_async_remote_copy(
        square, square_peer, misc_s.at[1], misc_r.at[1], {"tensor": other}, MESH
    )
    swap.start()
    swap.wait()

    def norm_last(i, carry):
        rows = pl.ds(pl.multiple_of(i * 32, 32), 32)
        total = square[rows, :] + square_peer[rows, :]
        scale = lax.rsqrt(jnp.sum(total, axis=-1, keepdims=True) * (1.0 / WIDTH) + EPS)
        scale = jnp.broadcast_to(scale, (32, 256))
        for j in range(8):
            columns = slice(j * 256, j * 256 + 256)
            h = h_last[j, rows, :].astype(F32)
            rows_out[rows, columns] = (h * scale * final_ref[:, columns]).astype(BF16)
        return carry

    lax.fori_loop(0, ROWS // 32, norm_last, 0)

    def scatter_copy(i):
        target = lax.rem(member + i, MEMBERS)
        return pltpu.make_async_remote_copy(
            rows_out.at[pl.ds(pl.multiple_of(target * 16, 16), 16)],
            rows_in.at[member],
            scatter_s,
            scatter_r,
            {"member": target},
            MESH,
        )

    def scatter(i, carry):
        scatter_copy(i).start()
        return carry

    lax.fori_loop(1, MEMBERS, scatter, 0)
    pltpu.make_async_copy(
        rows_out.at[pl.ds(pl.multiple_of(member * 16, 16), 16)], rows_in.at[member], local_sem.at[4]
    ).start()
    pltpu.make_async_copy(
        rows_out.at[pl.ds(pl.multiple_of(member * 16, 16), 16)], rows_in.at[member], local_sem.at[4]
    ).wait()
    fifteen = pltpu.make_async_remote_copy(
        rows_in.at[pl.ds(0, 15)], rows_in.at[pl.ds(0, 15)], scatter_s, scatter_r,
        {"tensor": other}, MESH,
    )
    fifteen.wait_recv()
    total = rows_in[0].astype(F32)
    for m in range(1, MEMBERS):
        total = total + rows_in[m].astype(F32)
    mean_own[...] = (total * (1.0 / MEMBERS)).astype(BF16)
    hop = pltpu.make_async_remote_copy(
        mean_own, mean_in, misc_s.at[2], misc_r.at[2], {"section": after}, MESH
    )
    hop.start()
    hop.wait_recv()

    def mean_slot(part, slot, which):
        rows = pl.ds(pl.multiple_of(slot * 16, 16), 16)
        lower = part * 1024 + (512 if which == 1 else 0)
        return out_ref.at[rows, pl.ds(lower, 1024 if which is None else 512)]

    final = Gather(
        torus,
        lambda part: mean_in.at[:, pl.ds(part * 1024, 1024)],
        mean_slot,
        lambda part: out_ref.at[pl.ds(0, 240), pl.ds(0, 1024)],
        ag_send.at[2],
        ag_recv.at[2],
    )
    for part in both:
        final.first(part)
    for part in both:
        final.spread(part, 0)
    out_ref[pl.ds(pl.multiple_of(member * 16, 16), 16), :] = mean_in[...]
    for part in both:
        final.line(part)
    for part in both:
        final.cross(part, 0)
    for part in both:
        final.far(part)
    for q in (1, 2, 3):
        for part in both:
            final.cross(part, q)
    for q in range(SIDE):
        for part in both:
            final.last(part, q)

    for gather in (qkv, outw, final):
        for part in both:
            gather.sent(part)
    for i in range(16):
        q, dv = blocks[i]
        peer_copy(i).wait_send()
        slot = slot_of(tensor, order[q], dv)
        hop_copy(i, slot).wait_send()
        forward_copy(i, tensor, slot).wait_send()
    for i in range(8):
        two_copy(i).wait_send()
    pass_docs.wait_send()
    hop.wait_send()
    fifteen.wait_send()


def per_device(
    hidden_input,
    document_index,
    query_key_value_weight,
    output_weight,
    adapter_down,
    adapter_up,
    attention_gain,
    final_norm_gain,
):
    cosine, sine = rope_tables()
    vmem = pl.BlockSpec(memory_space=pltpu.VMEM)
    anywhere = pl.BlockSpec(memory_space=pl.ANY)
    dma = pltpu.SemaphoreType.DMA
    averaged = pl.pallas_call(
        kernel,
        out_shape=jax.ShapeDtypeStruct((ROWS, WIDTH // 2), BF16),
        in_specs=[anywhere, vmem, anywhere, anywhere] + [vmem] * 6,
        out_specs=vmem,
        scratch_shapes=[
            pltpu.VMEM((WIDTH, 1536), BF16),
            pltpu.VMEM((MEMBERS, 2, 1024, 128), BF16),
            pltpu.VMEM((ROWS, WIDTH), BF16),
            pltpu.VMEM((ROWS, WIDTH), BF16),
            pltpu.VMEM((ROWS, 1536), F32),
            pltpu.VMEM((ROWS, 1024), BF16),
            pltpu.VMEM((ROWS, 16), BF16),
            pltpu.VMEM((2, SEQ), jnp.int32),
            pltpu.VMEM((16, ROWS, 128), BF16),
            pltpu.VMEM((16, ROWS, 128), BF16),
            pltpu.VMEM((16, ROWS, 128), BF16),
            pltpu.VMEM((16, ROWS, 128), BF16),
            pltpu.VMEM((2, MEMBERS, ROWS, 128), BF16),
            pltpu.VMEM((8, ROWS, 256), BF16),
            pltpu.VMEM((8, ROWS, 256), BF16),
            pltpu.VMEM((8, ROWS, 256), BF16),
            pltpu.VMEM((8, ROWS, 256), BF16),
            pltpu.VMEM((ROWS, 128), F32),
            pltpu.VMEM((ROWS, 128), F32),
            pltpu.VMEM((ROWS, WIDTH // 2), BF16),
            pltpu.VMEM((MEMBERS, 16, WIDTH // 2), BF16),
            pltpu.VMEM((16, WIDTH // 2), BF16),
            pltpu.VMEM((16, WIDTH // 2), BF16),
            dma((3, 2)),
            dma((3, 2, 15)),
            dma((5,)),
            dma((16,)),
            dma((16,)),
            dma((16,)),
            dma((16,)),
            dma((16,)),
            dma((16,)),
            dma((8,)),
            dma((8,)),
            dma((3,)),
            dma((3,)),
            dma,
            dma,
        ],
        compiler_params=pltpu.CompilerParams(
            collective_id=0, has_side_effects=True, vmem_limit_bytes=58 * 1024 * 1024
        ),
        name="relay",
    )(
        hidden_input.reshape(ROWS, WIDTH),
        document_index[0],
        query_key_value_weight[0].reshape(256, 1536),
        output_weight[0],
        adapter_down[0, 0].T,
        adapter_up[0, 0],
        attention_gain[0],
        final_norm_gain,
        jnp.asarray(cosine),
        jnp.asarray(sine),
    )
    return averaged.reshape(1, 2, SEQ, WIDTH // 2)


def solution(mesh):
    return jax.shard_map(
        per_device,
        mesh=mesh,
        in_specs=(
            P("member", "section", None, None, None),
            P("section", None, None),
            P("section", "member", "tensor", None),
            P("section", "tensor", "member"),
            P("member", "section", "tensor", None),
            P("member", "section", None, None),
            P("member", "section", None),
            P("member", "tensor"),
        ),
        out_specs=P("section", None, None, "tensor"),
        check_vma=False,
    )
```

```python
import math

import jax
import jax.numpy as jnp
import numpy as np
from jax import lax
from jax.experimental import pallas as pl
from jax.experimental.pallas import tpu as pltpu
from jax.sharding import PartitionSpec as P

HEAD_WIDTH = 128
GROUP = 4
WIDTH = 4096
ROWS = 256
SEQ = 128
MEMBERS = 16
SIDE = 4
EPS = 1e-05
MESH = pl.DeviceIdType.MESH
F32 = jnp.float32
BF16 = jnp.bfloat16


def rope_tables():
    position = np.arange(SEQ, dtype=np.float32)
    frequency = np.exp(
        np.arange(HEAD_WIDTH // 2, dtype=np.float32)
        * np.float32(-2.0 * math.log(500000.0) / HEAD_WIDTH)
    ).astype(np.float32)
    angles = (position[:, None] * frequency[None, :]).astype(np.float32)
    cosine, sine = np.cos(angles), np.sin(angles)
    return (
        np.concatenate([cosine, cosine], axis=1).astype(np.float32),
        np.concatenate([-sine, sine], axis=1).astype(np.float32),
    )


def wrap(value):
    return lax.rem(value + 2 * SIDE, SIDE)


class Torus:
    def __init__(self):
        self.member = lax.axis_index("member")
        self.x = lax.rem(self.member, SIDE)
        self.y = self.member // SIDE

    def at(self, part, du, dv):
        dx, dy = (du, dv) if part == 0 else (dv, du)
        return wrap(self.y + dy) * SIDE + wrap(self.x + dx)


class Place(Torus):
    def __init__(self):
        super().__init__()
        self.kind = lax.rem((self.x + 1) // 2, 2)
        self.parity = lax.rem(self.x, 2)
        self.pair_x = self.x + 1 - 2 * self.parity
        self.pair = self.y * SIDE + self.pair_x
        self.index = self.y * 2 + self.x // 2

    def column(self, f):
        return self.x + f * (3 - 2 * self.x)

    def row(self, dy):
        return wrap(self.y + dy)

    def near(self, f, dy):
        return self.row(dy) * SIDE + self.column(f)

    def pair_near(self, f, dy):
        return self.row(dy) * SIDE + self.pair_x + f * (3 - 2 * self.pair_x)


class PairGather:
    def __init__(self, place, own, slot, whole, send_sem, recv_sem):
        self.place, self.own, self.slot, self.whole = place, own, slot, whole
        self.send_sem, self.recv_sem = send_sem, recv_sem

    def copy(self, src, dst, part, f, dy, index):
        return pltpu.make_async_remote_copy(
            src_ref=src,
            dst_ref=dst,
            send_sem=self.send_sem.at[part],
            recv_sem=self.recv_sem.at[part, index],
            device_id={"member": self.place.near(f, dy)},
            device_id_type=MESH,
        )

    def ref(self, part, f, dy, which=None):
        return self.slot(self.place.column(f), self.place.row(dy), part, which)

    def move(self, part, f, dy, which, to_f, to_dy, index):
        ref = self.ref(part, f, dy, which)
        self.copy(ref, ref, part, to_f, to_dy, index).start()

    def wait(self, part, f, dy, index):
        ref = self.ref(part, f, dy)
        self.copy(ref, ref, part, 1, 0, index).wait_recv()

    def begin(self):
        for part, targets in ((0, ((1, 0), (0, 1), (0, -1))), (1, ((0, 1), (0, -1), (1, 0)))):
            for index, (f, dy) in enumerate(targets):
                self.copy(self.own(part), self.ref(part, 0, 0), part, f, dy, index).start()

    def middle(self):
        self.wait(0, 1, 0, 0)
        self.move(0, 1, 0, None, 0, 1, 3)
        self.move(0, 1, 0, None, 0, -1, 4)
        self.wait(1, 0, -1, 0)
        self.move(1, 0, -1, 0, 0, 1, 3)
        self.move(1, 0, -1, None, 1, 0, 4)
        self.wait(1, 0, 1, 1)
        self.move(1, 0, 1, 1, 0, -1, 3)
        self.move(1, 0, 1, None, 1, 0, 5)

    def late(self):
        self.wait(0, 0, -1, 1)
        self.move(0, 0, -1, 0, 0, 1, 5)
        self.wait(0, 0, 1, 2)
        self.move(0, 0, 1, 1, 0, -1, 5)
        self.wait(1, 0, 2, 3)
        self.move(1, 0, 2, None, 1, 0, 6)
        self.wait(0, 1, -1, 3)
        self.move(0, 1, -1, 0, 0, 1, 6)
        self.wait(0, 1, 1, 4)
        self.move(0, 1, 1, 1, 0, -1, 6)

    def end(self, stage):
        if stage == 0:
            self.wait(1, 1, 0, 2)
        elif stage == 1:
            self.wait(1, 1, -1, 4)
            self.wait(1, 1, 1, 5)
        elif stage == 2:
            self.wait(0, 0, 2, 5)
        else:
            self.wait(0, 1, 2, 6)
            self.wait(1, 1, 2, 6)

    def sent(self):
        for part in (0, 1):
            ref = self.whole(part)
            self.copy(ref, ref, part, 1, 0, 0).wait_send()


class Gather:
    order = (0, -1, 1, 2)

    def __init__(self, torus, own, slot, whole, send_sem, recv_sem):
        self.torus, self.own, self.slot, self.whole = torus, own, slot, whole
        self.send_sem, self.recv_sem = send_sem, recv_sem

    def start(self, src, dst, part, du, dv, index):
        pltpu.make_async_remote_copy(
            src_ref=src,
            dst_ref=dst,
            send_sem=self.send_sem.at[part],
            recv_sem=self.recv_sem.at[part, index],
            device_id={"member": self.torus.at(part, du, dv)},
            device_id_type=MESH,
        ).start()

    def wait(self, part, du, dv, index):
        ref = self.slot(part, self.torus.at(part, du, dv), None)
        pltpu.make_async_remote_copy(
            src_ref=ref,
            dst_ref=ref,
            send_sem=self.send_sem.at[part],
            recv_sem=self.recv_sem.at[part, index],
            device_id={"member": self.torus.at(part, 1, 0)},
            device_id_type=MESH,
        ).wait_recv()

    def full(self, part, du, dv):
        return self.slot(part, self.torus.at(part, du, dv), None)

    def half(self, part, du, dv, which):
        return self.slot(part, self.torus.at(part, du, dv), which)

    def spread(self, part, q):
        du = self.order[q]
        here = self.full(part, du, 0)
        src = self.own(part) if q == 0 else here
        self.start(src, here, part, 0, 1, 3 + q)
        self.start(src, here, part, 0, -1, 7 + q)

    def first(self, part):
        here = self.full(part, 0, 0)
        self.start(self.own(part), here, part, 1, 0, 0)
        self.start(self.own(part), here, part, -1, 0, 1)

    def line(self, part):
        self.wait(part, -1, 0, 0)
        ref = self.half(part, -1, 0, 0)
        self.start(ref, ref, part, 1, 0, 2)
        self.spread(part, 1)
        self.wait(part, 1, 0, 1)
        ref = self.half(part, 1, 0, 1)
        self.start(ref, ref, part, -1, 0, 2)
        self.spread(part, 2)

    def far(self, part):
        self.wait(part, 2, 0, 2)
        self.spread(part, 3)

    def cross(self, part, q):
        du = self.order[q]
        self.wait(part, du, -1, 3 + q)
        ref = self.half(part, du, -1, 0)
        self.start(ref, ref, part, 0, 1, 11 + q)
        self.wait(part, du, 1, 7 + q)
        ref = self.half(part, du, 1, 1)
        self.start(ref, ref, part, 0, -1, 11 + q)

    def last(self, part, q):
        self.wait(part, self.order[q], 2, 11 + q)

    def sent(self, part):
        ref = self.whole(part)
        pltpu.make_async_remote_copy(
            src_ref=ref,
            dst_ref=ref,
            send_sem=self.send_sem.at[part],
            recv_sem=self.recv_sem.at[part, 0],
            device_id={"member": self.torus.at(part, 1, 0)},
            device_id_type=MESH,
        ).wait_send()


def rotate(values, cosine, sine):
    return (values * cosine + pltpu.roll(values, HEAD_WIDTH // 2, 1) * sine).astype(BF16)


QKV_SPLIT = (((0, 144), (0, 80), (80, 64)), ((144, 112), (144, 64), (208, 48)))
OUT_SPLIT = (((0, 1152), (0, 576), (576, 576)), ((1152, 896), (1152, 448), (1600, 448)))


def cut(split, part, which):
    return split[part][0 if which is None else which + 1]


BLOCKS = ((0, 0), (1, 0), (0, -1), (0, 1), (1, -1), (1, 1), (0, 2), (1, 2))


def kernel(
    hidden_in, docs_in, qkv_in, out_in, down_in, up_in, gain_in, final_in, cos_ref, sin_ref,
    out_ref,
    wq, wo, h_all, nrm, proj, ctx_one, ctx_two, low, docs_next, gain_all, down_all, up_all, final_all,
    h_send, h_next, h_last, square, stat_own, stat_in, rows_out, rows_in, mean_own, mean_in, fin,
    pg_send, pg_recv, ag_send, ag_recv, local_sem, ctx_s, ctx_r, hop_s, hop_r, fwd_s, fwd_r,
    misc_s, misc_r, scatter_s, scatter_r,
):
    place = Place()
    member, kind, parity, index8 = place.member, place.kind, place.parity, place.index
    section = lax.axis_index("section")
    tensor = lax.axis_index("tensor")
    other = 1 - tensor
    sections = 8
    after = lax.rem(section + 1, sections)
    before = lax.rem(section + sections - 1, sections)
    both = (0, 1)

    barrier = pltpu.get_barrier_semaphore()

    def signal(device):
        pl.semaphore_signal(barrier, inc=1, device_id=device, device_id_type=MESH)

    def greet(i, carry):
        signal({"member": lax.rem(member + i, MEMBERS)})
        return carry

    lax.fori_loop(1, MEMBERS, greet, 0)
    signal({"tensor": other})
    signal({"member": place.pair, "tensor": other})
    for near in (after, before):
        signal({"section": near})
        signal({"section": near, "tensor": other})

    pending = []

    def local(src, dst, index):
        copy = pltpu.make_async_copy(src, dst, local_sem.at[index])
        copy.start()
        return copy

    def misc(src, dst, index, device):
        copy = pltpu.make_async_remote_copy(
            src, dst, misc_s.at[index], misc_r.at[index], device, MESH
        )
        pending.append(copy)
        return copy

    load_h = local(hidden_in, h_all.at[parity], 0)
    loads = [
        local(gain_in, gain_all.at[parity], 1),
        local(down_in, down_all.at[parity, tensor], 2),
        local(up_in, up_all.at[parity], 3),
        local(final_in, final_all.at[parity, tensor], 4),
        local(
            qkv_in.at[:, pl.ds(pl.multiple_of(kind * 768, 256), 768)],
            wq.at[pl.ds(pl.multiple_of(member * 256, 256), 256)],
            5,
        ),
    ]
    load_o = local(
        out_in.at[:, pl.ds(pl.multiple_of(tensor * 128, 128), 128)],
        wo.at[index8, pl.ds(pl.multiple_of(tensor * 1024, 1024), 1024)],
        6,
    )
    pl.semaphore_wait(barrier, MEMBERS - 1 + 6)

    def qkv_slot(of_pair):
        def slot(x, y, part, which):
            if of_pair:
                x = x + 1 - 2 * lax.rem(x, 2)
            lower, size = cut(QKV_SPLIT, part, which)
            return wq.at[pl.ds(pl.multiple_of((y * SIDE + x) * 256 + lower, 16), size)]

        return slot

    def own_qkv(part):
        lower, size = cut(QKV_SPLIT, part, None)
        return qkv_in.at[pl.ds(lower, size), pl.ds(pl.multiple_of(kind * 768, 256), 768)]

    def whole_qkv(part):
        return wq.at[pl.ds(0, 7 * cut(QKV_SPLIT, part, None)[1])]

    def out_slot(x, y, part, which):
        lower, size = cut(OUT_SPLIT, part, which)
        return wo.at[y * 2 + x // 2, pl.ds(lower, size)]

    def whole_out(part):
        return wo.at[pl.ds(0, 7), pl.ds(0, cut(OUT_SPLIT, part, None)[1])]

    wave_one = PairGather(place, own_qkv, qkv_slot(False), whole_qkv, pg_send.at[0], pg_recv.at[0])
    pair_slot = qkv_slot(True)
    wave_two = PairGather(
        place,
        lambda part: pair_slot(place.x, place.y, part, None),
        pair_slot,
        whole_qkv,
        pg_send.at[1],
        pg_recv.at[1],
    )
    wave_out = PairGather(
        place,
        lambda part: out_slot(place.x, place.y, part, None),
        out_slot,
        whole_out,
        pg_send.at[2],
        pg_recv.at[2],
    )

    to_pair = {"member": place.pair}
    to_pair_other = {"member": place.pair, "tensor": other}
    to_other = {"tensor": other}

    rows_of = lambda m: wq.at[pl.ds(pl.multiple_of(m * 256, 256), 256)]
    seed = misc(
        qkv_in.at[:, pl.ds(pl.multiple_of((1 - kind) * 768, 256), 768)], rows_of(member), 0, to_pair
    )
    seed.start()
    wave_one.begin()
    half_of = lambda a, t: h_all.at[a, pl.ds(pl.multiple_of(t * 128, 128), 128)]
    share_h = misc(
        hidden_in.at[pl.ds(pl.multiple_of(tensor * 128, 128), 128)], half_of(parity, tensor), 1, to_pair
    )
    share_h.start()
    share_out = misc(
        out_in.at[:, pl.ds(pl.multiple_of(other * 128, 128), 128)],
        wo.at[index8, pl.ds(pl.multiple_of(tensor * 1024, 1024), 1024)],
        2,
        to_other,
    )
    share_out.start()
    small = [misc(gain_in, gain_all.at[parity], 3, to_pair), misc(up_in, up_all.at[parity], 4, to_pair)]
    for k, device in enumerate((to_other, to_pair, to_pair_other)):
        small.append(misc(down_in, down_all.at[parity, tensor], 5 + k, device))
        small.append(misc(final_in, final_all.at[parity, tensor], 8 + k, device))
    small.append(misc(docs_in, docs_next, 11, {"section": after}))
    for copy in small:
        copy.start()
    load_h.wait()
    loads[0].wait()

    def norm_first(a):
        def block(i, carry):
            rows = pl.ds(pl.multiple_of(i * 16, 16), 16)
            h = h_all[a, rows, :].astype(F32)
            scale = lax.rsqrt(jnp.mean(h * h, axis=-1, keepdims=True) + EPS)
            nrm[pl.ds(pl.multiple_of(a * 256 + i * 16, 16), 16), :] = (
                h * scale * gain_all[a]
            ).astype(BF16)
            return carry

        lax.fori_loop(0, ROWS // 16, block, 0)

    norm_first(parity)

    def project():
        def block(n, carry):
            rows = pl.ds(pl.multiple_of(lax.rem(n, 2) * 256, 256), 256)
            columns = pl.ds(pl.multiple_of(n // 2 * 256, 256), 256)
            proj[rows, columns] = jnp.dot(nrm[rows, :], wq[:, columns], preferred_element_type=F32)
            return carry

        lax.fori_loop(0, 6, block, 0)

    ahead = lax.broadcasted_iota(jnp.int32, (SEQ, SEQ), 0) >= lax.broadcasted_iota(
        jnp.int32, (SEQ, SEQ), 1
    )
    head = 2 * tensor + kind

    def ctx_copy(ctx, tick, s, which):
        owner = 2 * tensor + (1 - kind if which == 2 else kind)
        ref = ctx.at[
            pl.ds(pl.multiple_of(s * SEQ, SEQ), SEQ), pl.ds(pl.multiple_of(owner * 512, 512), 512)
        ]
        return pltpu.make_async_remote_copy(
            ref, ref, ctx_s.at[tick, which, s], ctx_r.at[tick, which, s],
            to_pair if which == 1 else to_other, MESH,
        )

    def ctx_arrived(ctx, tick, s, which):
        t = tensor if which == 1 else other
        owner = 2 * t + (kind if which == 0 else 1 - kind)
        ref = ctx.at[
            pl.ds(pl.multiple_of(s * SEQ, SEQ), SEQ), pl.ds(pl.multiple_of(owner * 512, 512), 512)
        ]
        pltpu.make_async_remote_copy(
            ref, ref, ctx_s.at[tick, which, s], ctx_r.at[tick, which, s], to_other, MESH
        ).wait_recv()

    def attend(docs_ref, ctx, tick):
        def sequence(s, carry):
            rows = pl.ds(pl.multiple_of(s * SEQ, SEQ), SEQ)
            numbers = docs_ref[pl.ds(lax.rem(s, 2), 1), :]
            numbers = jnp.broadcast_to(numbers, (SEQ, SEQ)).astype(F32)
            allowed = ahead & (numbers == numbers.T)
            allowed = jnp.concatenate([allowed.astype(F32)] * GROUP, axis=0) > 0.5
            cosine, sine = cos_ref[...], sin_ref[...]

            def piece(g):
                return proj[rows, g * 128 : g * 128 + 128]

            queries = jnp.concatenate(
                [rotate(piece(g), cosine, sine) for g in range(GROUP)], axis=0
            )
            keys = rotate(piece(GROUP), cosine, sine)
            values = piece(GROUP + 1).astype(BF16)
            scores = lax.dot_general(
                queries, keys, (((1,), (1,)), ((), ())), preferred_element_type=F32
            ) * (1.0 / math.sqrt(HEAD_WIDTH))
            scores = jnp.where(allowed, scores, -1e30)
            weights = jnp.exp(scores - jnp.max(scores, axis=-1, keepdims=True))
            weights = (weights / jnp.sum(weights, axis=-1, keepdims=True)).astype(BF16)
            context = jnp.dot(weights, values, preferred_element_type=F32).astype(BF16)
            for g in range(GROUP):
                columns = pl.ds(pl.multiple_of(head * 512 + g * 128, 128), 128)
                ctx[rows, columns] = context[g * SEQ : (g + 1) * SEQ]
            ctx_copy(ctx, tick, s, 1).start()
            ctx_copy(ctx, tick, s, 0).start()
            return carry

        lax.fori_loop(0, 4, sequence, 0)

    def collect(ctx, tick, a):
        for s in (2 * a, 2 * a + 1):
            ctx_arrived(ctx, tick, s, 1)
            ctx_copy(ctx, tick, s, 2).start()
        for s in (2 * a, 2 * a + 1):
            ctx_arrived(ctx, tick, s, 0)
            ctx_arrived(ctx, tick, s, 2)
        for block in both:
            low[a, block] = lax.dot_general(
                ctx[a * 256 : a * 256 + 256, block * 1024 : block * 1024 + 1024],
                down_all[a, block],
                (((1,), (1,)), ((), ())),
                preferred_element_type=F32,
            ).astype(BF16)

    wave_one.middle()
    seed_in = pltpu.make_async_remote_copy(
        rows_of(place.pair), rows_of(place.pair), misc_s.at[0], misc_r.at[0], to_pair, MESH
    )
    seed_in.wait_recv()
    wave_two.begin()
    wave_one.late()
    pltpu.make_async_remote_copy(
        half_of(1 - parity, tensor), half_of(1 - parity, tensor), misc_s.at[1], misc_r.at[1],
        to_pair, MESH,
    ).wait_recv()
    pass_h = misc(half_of(1 - parity, tensor), half_of(1 - parity, tensor), 12, to_other)
    pass_h.start()
    wave_two.middle()
    load_o.wait()
    share_in = wo.at[index8, pl.ds(pl.multiple_of(other * 1024, 1024), 1024)]
    pltpu.make_async_remote_copy(
        share_in, share_in, misc_s.at[2], misc_r.at[2], to_other, MESH
    ).wait_recv()
    wave_out.begin()
    pltpu.make_async_remote_copy(
        half_of(1 - parity, other), half_of(1 - parity, other), misc_s.at[12], misc_r.at[12],
        to_other, MESH,
    ).wait_recv()
    small[0].wait_recv()
    norm_first(1 - parity)
    wave_two.late()
    for copy in small[1:]:
        copy.wait_recv()
    for copy in loads[1:]:
        copy.wait()
    for stage in range(4):
        wave_one.end(stage)
        wave_two.end(stage)
    project()
    wave_out.middle()
    attend(docs_in, ctx_one, 0)
    wave_out.late()

    def block_member(i, pair=False):
        f, dy = BLOCKS[i]
        return place.pair_near(f, dy) if pair else place.near(f, dy)

    def columns_of(m):
        return pl.ds(pl.multiple_of(m * 256 + tensor * 128, 128), 128)

    def summed(ctx, a, weights_of, up):
        total = None
        for block in both:
            main = jnp.dot(
                ctx[a * 256 : a * 256 + 256, block * 1024 : block * 1024 + 1024],
                weights_of(block),
                preferred_element_type=F32,
            )
            value = main + jnp.dot(low[a, block], up, preferred_element_type=F32)
            value = value.astype(BF16).astype(F32)
            total = value if total is None else total + value
        return total

    def block_copy(ref, dst, kind_of, n, device):
        send, recv = (hop_s.at[n], hop_r.at[n]) if kind_of == 3 else (
            fwd_s.at[kind_of, n], fwd_r.at[kind_of, n]
        )
        return pltpu.make_async_remote_copy(ref, dst, send, recv, device, MESH)

    steps = [(i, 0) for i in range(4)] + [(i, 1) for i in range(4)]
    for i in range(4, 8):
        steps += [(i, 0), (i, 1)]

    def own_ref(n):
        i, a = steps[n]
        return h_next.at[block_member(i) * 2 + tensor, a]

    def hop_copy(n):
        return block_copy(h_send.at[n], own_ref(n), 3, n, {"section": after})

    def start_block(n):
        i, a = steps[n]
        f, dy = BLOCKS[i]
        slot = place.row(dy) * 2 + place.column(f) // 2
        columns = columns_of(block_member(i))
        total = summed(
            ctx_one, a, lambda block: wo[slot, block * 1024 : block * 1024 + 1024],
            up_all[a, :, columns],
        )
        h_send[n] = (h_all[a, :, columns].astype(F32) + total).astype(BF16)
        hop_copy(n).start()

    def pair_ref(n):
        i, a = steps[n]
        return h_next.at[block_member(i, True) * 2 + tensor, a]

    def pass_own(n, device, kind_of):
        return block_copy(own_ref(n), own_ref(n), kind_of, n, device)

    def pass_pair(n):
        return block_copy(pair_ref(n), pair_ref(n), 2, n, to_other)

    def arrive(n):
        hop_copy(n).wait_recv()
        pass_own(n, to_pair, 0).start()
        pass_own(n, to_other, 1).start()

    def relay(n):
        block_copy(pair_ref(n), pair_ref(n), 0, n, to_pair).wait_recv()
        pass_pair(n).start()

    def other_ref(n, pair):
        i, a = steps[n]
        return h_next.at[block_member(i, pair) * 2 + other, a]

    def run(lower, upper):
        for n in range(lower, upper):
            start_block(n)
            if n >= 2:
                arrive(n - 2)
            if n >= 5:
                relay(n - 5)

    collect(ctx_one, 0, 0)
    wave_out.end(0)
    run(0, 4)
    collect(ctx_one, 0, 1)
    run(4, 8)
    wave_out.end(1)
    run(8, 12)
    wave_out.end(2)
    run(12, 14)
    wave_out.end(3)
    run(14, 16)
    for n in (14, 15):
        arrive(n)
    for n in range(11, 16):
        relay(n)
    for n in range(16):
        ref = other_ref(n, False)
        block_copy(ref, ref, 1, n, to_other).wait_recv()
        ref = other_ref(n, True)
        block_copy(ref, ref, 2, n, to_other).wait_recv()

    def norm_second(i, carry):
        a = i // 8
        rows = pl.ds(pl.multiple_of(lax.rem(i, 8) * 32, 32), 32)
        total = jnp.zeros((32, 128), F32)
        for block in range(32):
            h = h_next[block, a, rows, :].astype(F32)
            total = total + h * h
        scale = lax.rsqrt(jnp.sum(total, axis=-1, keepdims=True) * (1.0 / WIDTH) + EPS)
        scale = jnp.broadcast_to(scale, (32, 128))
        for block in range(32):
            columns = slice(block * 128, block * 128 + 128)
            h = h_next[block, a, rows, :].astype(F32)
            nrm[pl.ds(pl.multiple_of(i * 32, 32), 32), columns] = (
                h * scale * gain_all[a, :, columns]
            ).astype(BF16)
        return carry

    lax.fori_loop(0, 16, norm_second, 0)
    project()
    attend(docs_next, ctx_two, 1)

    def pair_members(y):
        return y * SIDE + kind, y * SIDE + 3 - kind

    def pair_columns(ref, a, y, half):
        parts = []
        for m in pair_members(y):
            lower = (m - half * 8) * 256 + tensor * 128
            parts.append(ref[a, :, pl.ds(pl.multiple_of(lower, 128), 128)])
        return jnp.concatenate(parts, axis=1)

    for a in both:
        collect(ctx_two, 1, a)
        square[a] = jnp.zeros((ROWS, 128), F32)

        def last_block(y, carry):
            total = summed(
                ctx_two,
                a,
                lambda block: jnp.concatenate(
                    [wo[2 * y + k, block * 1024 : block * 1024 + 1024] for k in both], axis=1
                ),
                pair_columns(up_all, a, y, 0),
            )
            for k, m in enumerate(pair_members(y)):
                columns = slice(k * 128, k * 128 + 128)
                h = h_next[m * 2 + tensor, a].astype(F32) + total[:, columns]
                h = h.astype(BF16)
                h_last[a, y, :, columns] = h
                h = h.astype(F32)
                square[a] += h * h
            return carry

        lax.fori_loop(0, SIDE, last_block, 0)

    stat_own[...] = jnp.zeros_like(stat_own)
    for a in both:
        for r in both:
            stat_own[2 * a + r : 2 * a + r + 1, :] = jnp.sum(
                square[a, r * 128 : r * 128 + 128].T, axis=0, keepdims=True
            )
    stats = [
        misc(stat_own, stat_in.at[k], 13 + k, device)
        for k, device in enumerate((to_other, to_pair, to_pair_other))
    ]
    for copy in stats:
        copy.start()
    for copy in stats:
        copy.wait_recv()
    total = stat_own[...] + stat_in[0] + stat_in[1] + stat_in[2]
    scales = lax.rsqrt(total * (1.0 / WIDTH) + EPS)
    column_scale = [jnp.broadcast_to(scales[s : s + 1], (128, 128)).T for s in range(4)]
    for y in range(SIDE):
        for k, m in enumerate((y * SIDE + kind, y * SIDE + 3 - kind)):
            lower = (m - (y // 2) * 8) * 256 + tensor * 128
            gains = [
                final_all[a, y // 2, :, pl.ds(pl.multiple_of(lower, 128), 128)] for a in both
            ]
            columns = slice(k * 128, k * 128 + 128)
            for r in both:
                rows = slice(r * 128, r * 128 + 128)
                value = sum(
                    h_last[a, y, rows, columns].astype(F32) * column_scale[2 * a + r] * gains[a]
                    for a in both
                )
                rows_out[rows, (2 * y + k) * 128 : (2 * y + k + 1) * 128] = value.astype(BF16)

    def rows_at(i):
        return rows_out.at[pl.ds(pl.multiple_of(i * 32, 32), 32)]

    def scatter(i, carry):
        f, dy = lax.rem(i, 2), i // 2
        x, y = place.column(f), place.row(dy)
        pltpu.make_async_remote_copy(
            rows_at(y * 2 + x // 2), rows_in.at[index8], scatter_s, scatter_r,
            {"member": y * SIDE + x}, MESH,
        ).start()
        return carry

    lax.fori_loop(1, 8, scatter, 0)
    keep = local(rows_at(index8), rows_in.at[index8], 7)
    keep.wait()
    seven = pltpu.make_async_remote_copy(
        rows_in.at[pl.ds(0, 7)], rows_in.at[pl.ds(0, 7)], scatter_s, scatter_r, to_other, MESH
    )
    seven.wait_recv()
    total = rows_in[0].astype(F32)
    for i in range(1, 8):
        total = total + rows_in[i].astype(F32)
    total = (total * (1.0 / MEMBERS)).astype(BF16)
    for half in both:
        mean_own[half] = total[:, half * 512 : half * 512 + 512]
    hops = [
        misc(mean_own.at[tensor], mean_in.at[tensor], 16, {"section": after}),
        misc(mean_own.at[other], mean_in.at[tensor], 17, {"section": after, "tensor": other}),
    ]
    for copy in hops:
        copy.start()
    hops[0].wait_recv()
    pltpu.make_async_remote_copy(
        mean_own.at[other], mean_in.at[other], misc_s.at[17], misc_r.at[17],
        {"section": after, "tensor": other}, MESH,
    ).wait_recv()

    def mean_slot(part, slot, which):
        if which is None:
            return fin.at[slot, part]
        return fin.at[slot, part, :, pl.ds(which * 256, 256)]

    final = Gather(
        place,
        lambda part: mean_in.at[part],
        mean_slot,
        lambda part: fin.at[pl.ds(0, 15), part],
        ag_send,
        ag_recv,
    )
    for part in both:
        final.first(part)
    for part in both:
        final.spread(part, 0)
    fin[member] = mean_in[...]
    for part in both:
        final.line(part)
    for part in both:
        final.cross(part, 0)
    for part in both:
        final.far(part)
    for q in (1, 2, 3):
        for part in both:
            final.cross(part, q)
    for q in range(SIDE):
        for part in both:
            final.last(part, q)
    for m in range(MEMBERS):
        x, y = m % SIDE, m // SIDE
        side = ((x + 1) // 2) % 2
        rows = slice((y * 2 + x // 2) * 32, (y * 2 + x // 2) * 32 + 32)
        for part in both:
            for s in range(4):
                column = (s // 2 * SIDE + (side if s % 2 == 0 else 3 - side)) * 256 + part * 128
                out_ref[rows, column : column + 128] = fin[m, part, :, s * 128 : s * 128 + 128]

    for wave in (wave_one, wave_two, wave_out):
        wave.sent()
    for part in both:
        final.sent(part)
    for tick, ctx in enumerate((ctx_one, ctx_two)):
        for which in range(3):
            for s in range(4):
                ctx_copy(ctx, tick, s, which).wait_send()
    for n in range(16):
        hop_copy(n).wait_send()
        pass_own(n, to_pair, 0).wait_send()
        pass_own(n, to_other, 1).wait_send()
        pass_pair(n).wait_send()
    for copy in pending:
        copy.wait_send()
    seven.wait_send()


def per_device(
    hidden_input,
    document_index,
    query_key_value_weight,
    output_weight,
    adapter_down,
    adapter_up,
    attention_gain,
    final_norm_gain,
):
    cosine, sine = rope_tables()
    vmem = pl.BlockSpec(memory_space=pltpu.VMEM)
    anywhere = pl.BlockSpec(memory_space=pl.ANY)
    dma = pltpu.SemaphoreType.DMA
    averaged = pl.pallas_call(
        kernel,
        out_shape=jax.ShapeDtypeStruct((ROWS, WIDTH // 2), BF16),
        in_specs=[anywhere, vmem, anywhere, anywhere] + [vmem] * 6,
        out_specs=vmem,
        scratch_shapes=[
            pltpu.VMEM((WIDTH, 768), BF16),
            pltpu.VMEM((8, 2048, 128), BF16),
            pltpu.VMEM((2, ROWS, WIDTH), BF16),
            pltpu.VMEM((2 * ROWS, WIDTH), BF16),
            pltpu.VMEM((2 * ROWS, 768), F32),
            pltpu.VMEM((2 * ROWS, 2048), BF16),
            pltpu.VMEM((2 * ROWS, 2048), BF16),
            pltpu.VMEM((2, 2, ROWS, 16), BF16),
            pltpu.VMEM((2, SEQ), jnp.int32),
            pltpu.VMEM((2, 1, WIDTH), F32),
            pltpu.VMEM((2, 2, 16, 1024), BF16),
            pltpu.VMEM((2, 16, WIDTH), BF16),
            pltpu.VMEM((2, 2, 1, WIDTH // 2), F32),
            pltpu.VMEM((16, ROWS, 128), BF16),
            pltpu.VMEM((32, 2, ROWS, 128), BF16),
            pltpu.VMEM((2, SIDE, ROWS, 256), BF16),
            pltpu.VMEM((2, ROWS, 128), F32),
            pltpu.VMEM((8, 128), F32),
            pltpu.VMEM((3, 8, 128), F32),
            pltpu.VMEM((ROWS, 1024), BF16),
            pltpu.VMEM((8, 32, 1024), BF16),
            pltpu.VMEM((2, 32, 512), BF16),
            pltpu.VMEM((2, 32, 512), BF16),
            pltpu.VMEM((MEMBERS, 2, 32, 512), BF16),
            dma((3, 2)),
            dma((3, 2, 7)),
            dma((2,)),
            dma((2, 15)),
            dma((8,)),
            dma((2, 3, 4)),
            dma((2, 3, 4)),
            dma((16,)),
            dma((16,)),
            dma((3, 16)),
            dma((3, 16)),
            dma((18,)),
            dma((18,)),
            dma,
            dma,
        ],
        compiler_params=pltpu.CompilerParams(
            collective_id=0, has_side_effects=True, vmem_limit_bytes=58 * 1024 * 1024
        ),
        name="relay",
    )(
        hidden_input.reshape(ROWS, WIDTH),
        document_index[0],
        query_key_value_weight[0].reshape(256, 1536),
        output_weight[0],
        adapter_down[0, 0].T,
        adapter_up[0, 0],
        attention_gain[0],
        final_norm_gain,
        jnp.asarray(cosine),
        jnp.asarray(sine),
    )
    return averaged.reshape(1, 2, SEQ, WIDTH // 2)


def solution(mesh):
    return jax.shard_map(
        per_device,
        mesh=mesh,
        in_specs=(
            P("member", "section", None, None, None),
            P("section", None, None),
            P("section", "member", "tensor", None),
            P("section", "tensor", "member"),
            P("member", "section", "tensor", None),
            P("member", "section", None, None),
            P("member", "section", None),
            P("member", "tensor"),
        ),
        out_specs=P("section", None, None, "tensor"),
        check_vma=False,
    )
```

```python
import math

import jax
import jax.numpy as jnp
import numpy as np
from jax import lax
from jax.experimental import pallas as pl
from jax.experimental.pallas import tpu as pltpu
from jax.sharding import PartitionSpec as P

HEAD_WIDTH = 128
GROUP = 4
WIDTH = 4096
ROWS = 256
SEQ = 128
MEMBERS = 16
SIDE = 4
EPS = 1e-05
MESH = pl.DeviceIdType.MESH
F32 = jnp.float32
BF16 = jnp.bfloat16


def rope_tables():
    position = np.arange(SEQ, dtype=np.float32)
    frequency = np.exp(
        np.arange(HEAD_WIDTH // 2, dtype=np.float32)
        * np.float32(-2.0 * math.log(500000.0) / HEAD_WIDTH)
    ).astype(np.float32)
    angles = (position[:, None] * frequency[None, :]).astype(np.float32)
    cosine, sine = np.cos(angles), np.sin(angles)
    return (
        np.concatenate([cosine, cosine], axis=1).astype(np.float32),
        np.concatenate([-sine, sine], axis=1).astype(np.float32),
    )


def wrap(value):
    return lax.rem(value + 2 * SIDE, SIDE)


class Torus:
    def __init__(self):
        self.member = lax.axis_index("member")
        self.x = lax.rem(self.member, SIDE)
        self.y = self.member // SIDE

    def at(self, part, du, dv):
        dx, dy = (du, dv) if part == 0 else (dv, du)
        return wrap(self.y + dy) * SIDE + wrap(self.x + dx)


class Place(Torus):
    def __init__(self):
        super().__init__()
        self.kind = lax.rem((self.x + 1) // 2, 2)
        self.parity = lax.rem(self.x, 2)
        self.pair_x = self.x + 1 - 2 * self.parity
        self.pair = self.y * SIDE + self.pair_x
        self.index = self.y * 2 + self.x // 2

    def column(self, f):
        return self.x + f * (3 - 2 * self.x)

    def row(self, dy):
        return wrap(self.y + dy)

    def near(self, f, dy):
        return self.row(dy) * SIDE + self.column(f)

    def pair_near(self, f, dy):
        return self.row(dy) * SIDE + self.pair_x + f * (3 - 2 * self.pair_x)


class PairGather:
    def __init__(self, place, own, slot, whole, send_sem, recv_sem):
        self.place, self.own, self.slot, self.whole = place, own, slot, whole
        self.send_sem, self.recv_sem = send_sem, recv_sem

    def copy(self, src, dst, part, f, dy, index):
        return pltpu.make_async_remote_copy(
            src_ref=src,
            dst_ref=dst,
            send_sem=self.send_sem.at[part],
            recv_sem=self.recv_sem.at[part, index],
            device_id={"member": self.place.near(f, dy)},
            device_id_type=MESH,
        )

    def ref(self, part, f, dy, which=None):
        return self.slot(self.place.column(f), self.place.row(dy), part, which)

    def move(self, part, f, dy, which, to_f, to_dy, index):
        ref = self.ref(part, f, dy, which)
        self.copy(ref, ref, part, to_f, to_dy, index).start()

    def wait(self, part, f, dy, index):
        ref = self.ref(part, f, dy)
        self.copy(ref, ref, part, 1, 0, index).wait_recv()

    def begin(self):
        for part, targets in ((0, ((1, 0), (0, 1), (0, -1))), (1, ((0, 1), (0, -1), (1, 0)))):
            for index, (f, dy) in enumerate(targets):
                self.copy(self.own(part), self.ref(part, 0, 0), part, f, dy, index).start()

    def middle(self):
        self.wait(0, 1, 0, 0)
        self.move(0, 1, 0, None, 0, 1, 3)
        self.move(0, 1, 0, None, 0, -1, 4)
        self.wait(1, 0, -1, 0)
        self.move(1, 0, -1, 0, 0, 1, 3)
        self.move(1, 0, -1, None, 1, 0, 4)
        self.wait(1, 0, 1, 1)
        self.move(1, 0, 1, 1, 0, -1, 3)
        self.move(1, 0, 1, None, 1, 0, 5)

    def late(self):
        self.wait(0, 0, -1, 1)
        self.move(0, 0, -1, 0, 0, 1, 5)
        self.wait(0, 0, 1, 2)
        self.move(0, 0, 1, 1, 0, -1, 5)
        self.wait(1, 0, 2, 3)
        self.move(1, 0, 2, None, 1, 0, 6)
        self.wait(0, 1, -1, 3)
        self.move(0, 1, -1, 0, 0, 1, 6)
        self.wait(0, 1, 1, 4)
        self.move(0, 1, 1, 1, 0, -1, 6)

    def end(self, stage):
        if stage == 0:
            self.wait(1, 1, 0, 2)
        elif stage == 1:
            self.wait(1, 1, -1, 4)
            self.wait(1, 1, 1, 5)
        elif stage == 2:
            self.wait(0, 0, 2, 5)
        else:
            self.wait(0, 1, 2, 6)
            self.wait(1, 1, 2, 6)

    def sent(self):
        for part in (0, 1):
            ref = self.whole(part)
            self.copy(ref, ref, part, 1, 0, 0).wait_send()


class PlaneGather:
    order = (0, -1, 1, 2)

    def __init__(self, torus, own, slot, whole, send_sem, recv_sem):
        self.torus, self.own, self.slot, self.whole = torus, own, slot, whole
        self.send_sem, self.recv_sem = send_sem, recv_sem

    def copy(self, src, dst, part, du, dv, index):
        return pltpu.make_async_remote_copy(
            src_ref=src,
            dst_ref=dst,
            send_sem=self.send_sem.at[part],
            recv_sem=self.recv_sem.at[part, index],
            device_id={"member": self.torus.at(part, du, dv)},
            device_id_type=MESH,
        )

    def ref(self, part, du, dv):
        return self.slot(part, self.torus.at(part, du, dv))

    def begin(self):
        for part in (0, 1):
            for k in (1, 2, 3):
                self.copy(self.own(part), self.ref(part, 0, 0), part, -self.order[k], 0, k - 1).start()
        for part in (0, 1):
            self.spread(part, 0)

    def spread(self, part, q):
        here = self.ref(part, self.order[q], 0)
        src = self.own(part) if q == 0 else here
        for k in (1, 2, 3):
            self.copy(src, here, part, 0, -self.order[k], 3 * q + k + 2).start()

    def wait(self, part, du, dv, index):
        ref = self.ref(part, du, dv)
        self.copy(ref, ref, part, 1, 0, index).wait_recv()

    def middle(self):
        for q in (1, 2, 3):
            for part in (0, 1):
                self.wait(part, self.order[q], 0, q - 1)
                self.spread(part, q)

    def end(self):
        for q in range(SIDE):
            for part in (0, 1):
                for k in (1, 2, 3):
                    self.wait(part, self.order[q], self.order[k], 3 * q + k + 2)

    def sent(self):
        for part in (0, 1):
            ref = self.whole(part)
            self.copy(ref, ref, part, 1, 0, 0).wait_send()


def rotate(values, cosine, sine):
    return (values * cosine + pltpu.roll(values, HEAD_WIDTH // 2, 1) * sine).astype(BF16)


QKV_SPLIT = (((0, 144), (0, 80), (80, 64)), ((144, 112), (144, 64), (208, 48)))
OUT_SPLIT = (((0, 1152), (0, 576), (576, 576)), ((1152, 896), (1152, 448), (1600, 448)))


def cut(split, part, which):
    return split[part][0 if which is None else which + 1]


BLOCKS = ((0, 0), (1, 0), (0, -1), (0, 1), (1, -1), (1, 1), (0, 2), (1, 2))


def kernel(
    hidden_in, docs_in, qkv_in, out_in, down_in, up_in, gain_in, final_in, cos_ref, sin_ref,
    out_ref,
    wq, wo, h_all, nrm, proj, ctx_one, ctx_two, low, docs_next, gain_all, down_all, up_all, final_all,
    h_send, h_next, h_last, square, stat_own, stat_in, rows_out, rows_in, mean_own, mean_in, fin,
    pg_send, pg_recv, ag_send, ag_recv, local_sem, ctx_s, ctx_r, hop_s, hop_r, fwd_s, fwd_r,
    misc_s, misc_r, scatter_s, scatter_r,
):
    place = Place()
    member, kind, parity, index8 = place.member, place.kind, place.parity, place.index
    section = lax.axis_index("section")
    tensor = lax.axis_index("tensor")
    other = 1 - tensor
    sections = 8
    after = lax.rem(section + 1, sections)
    before = lax.rem(section + sections - 1, sections)
    both = (0, 1)

    barrier = pltpu.get_barrier_semaphore()

    def signal(device):
        pl.semaphore_signal(barrier, inc=1, device_id=device, device_id_type=MESH)

    def greet(i, carry):
        signal({"member": lax.rem(member + i, MEMBERS)})
        return carry

    lax.fori_loop(1, MEMBERS, greet, 0)
    signal({"tensor": other})
    signal({"member": place.pair, "tensor": other})
    for near in (after, before):
        signal({"section": near})
        signal({"section": near, "tensor": other})

    pending = []

    def local(src, dst, index):
        copy = pltpu.make_async_copy(src, dst, local_sem.at[index])
        copy.start()
        return copy

    def misc(src, dst, index, device):
        copy = pltpu.make_async_remote_copy(
            src, dst, misc_s.at[index], misc_r.at[index], device, MESH
        )
        pending.append(copy)
        return copy

    load_h = local(hidden_in, h_all.at[:, parity], 0)
    loads = [
        local(gain_in, gain_all.at[parity], 1),
        local(down_in, down_all.at[parity, tensor], 2),
        local(up_in, up_all.at[parity], 3),
        local(final_in, final_all.at[parity, tensor], 4),
        local(
            qkv_in.at[:, pl.ds(pl.multiple_of(kind * 768, 256), 768)],
            wq.at[pl.ds(pl.multiple_of(member * 256, 256), 256)],
            5,
        ),
    ]
    load_o = local(
        out_in.at[:, pl.ds(pl.multiple_of(tensor * 128, 128), 128)],
        wo.at[index8, pl.ds(pl.multiple_of(tensor * 1024, 1024), 1024)],
        6,
    )
    pl.semaphore_wait(barrier, MEMBERS - 1 + 6)

    def qkv_slot(of_pair):
        def slot(x, y, part, which):
            if of_pair:
                x = x + 1 - 2 * lax.rem(x, 2)
            lower, size = cut(QKV_SPLIT, part, which)
            return wq.at[pl.ds(pl.multiple_of((y * SIDE + x) * 256 + lower, 16), size)]

        return slot

    def own_qkv(part):
        lower, size = cut(QKV_SPLIT, part, None)
        return qkv_in.at[pl.ds(lower, size), pl.ds(pl.multiple_of(kind * 768, 256), 768)]

    def whole_qkv(part):
        return wq.at[pl.ds(0, 7 * cut(QKV_SPLIT, part, None)[1])]

    def out_slot(x, y, part, which):
        lower, size = cut(OUT_SPLIT, part, which)
        return wo.at[y * 2 + x // 2, pl.ds(lower, size)]

    def whole_out(part):
        return wo.at[pl.ds(0, 7), pl.ds(0, cut(OUT_SPLIT, part, None)[1])]

    wave_one = PairGather(place, own_qkv, qkv_slot(False), whole_qkv, pg_send.at[0], pg_recv.at[0])
    pair_slot = qkv_slot(True)
    wave_two = PairGather(
        place,
        lambda part: pair_slot(place.x, place.y, part, None),
        pair_slot,
        whole_qkv,
        pg_send.at[1],
        pg_recv.at[1],
    )
    wave_out = PairGather(
        place,
        lambda part: out_slot(place.x, place.y, part, None),
        out_slot,
        whole_out,
        pg_send.at[2],
        pg_recv.at[2],
    )

    to_pair = {"member": place.pair}
    to_pair_other = {"member": place.pair, "tensor": other}
    to_other = {"tensor": other}

    rows_of = lambda m: wq.at[pl.ds(pl.multiple_of(m * 256, 256), 256)]
    seed = misc(
        qkv_in.at[:, pl.ds(pl.multiple_of((1 - kind) * 768, 256), 768)], rows_of(member), 0, to_pair
    )
    seed.start()
    wave_one.begin()
    half_of = lambda a, t: h_all.at[t, a]
    share_h = misc(
        hidden_in.at[tensor], half_of(parity, tensor), 1, to_pair
    )
    share_h.start()
    share_out = misc(
        out_in.at[:, pl.ds(pl.multiple_of(other * 128, 128), 128)],
        wo.at[index8, pl.ds(pl.multiple_of(tensor * 1024, 1024), 1024)],
        2,
        to_other,
    )
    share_out.start()
    small = [misc(gain_in, gain_all.at[parity], 3, to_pair), misc(up_in, up_all.at[parity], 4, to_pair)]
    for k, device in enumerate((to_other, to_pair, to_pair_other)):
        small.append(misc(down_in, down_all.at[parity, tensor], 5 + k, device))
        small.append(misc(final_in, final_all.at[parity, tensor], 8 + k, device))
    small.append(misc(docs_in, docs_next, 11, {"section": after}))
    for copy in small:
        copy.start()
    load_h.wait()
    loads[0].wait()

    def norm_first(a):
        def block(i, carry):
            r, j = i // 8, lax.rem(i, 8)
            h = h_all[r, a, pl.ds(pl.multiple_of(j * 16, 16), 16), :].astype(F32)
            scale = lax.rsqrt(jnp.mean(h * h, axis=-1, keepdims=True) + EPS)
            nrm[pl.ds(pl.multiple_of(r * 256 + a * 128 + j * 16, 16), 16), :] = (
                h * scale * gain_all[a]
            ).astype(BF16)
            return carry

        lax.fori_loop(0, ROWS // 16, block, 0)

    norm_first(parity)

    def project(lower, upper):
        def block(n, carry):
            rows = pl.ds(pl.multiple_of(n // 3 * 256, 256), 256)
            columns = pl.ds(pl.multiple_of(lax.rem(n, 3) * 256, 256), 256)
            proj[rows, columns] = jnp.dot(nrm[rows, :], wq[:, columns], preferred_element_type=F32)
            return carry

        lax.fori_loop(lower, upper, block, 0)

    ahead = lax.broadcasted_iota(jnp.int32, (SEQ, SEQ), 0) >= lax.broadcasted_iota(
        jnp.int32, (SEQ, SEQ), 1
    )
    head = 2 * tensor + kind

    def ctx_copy(ctx, tick, s, which):
        owner = 2 * tensor + (1 - kind if which == 2 else kind)
        ref = ctx.at[
            pl.ds(pl.multiple_of(s * SEQ, SEQ), SEQ), pl.ds(pl.multiple_of(owner * 512, 512), 512)
        ]
        return pltpu.make_async_remote_copy(
            ref, ref, ctx_s.at[tick, which, s], ctx_r.at[tick, which, s],
            to_pair if which == 1 else to_other, MESH,
        )

    def ctx_arrived(ctx, tick, s, which):
        t = tensor if which == 1 else other
        owner = 2 * t + (kind if which == 0 else 1 - kind)
        ref = ctx.at[
            pl.ds(pl.multiple_of(s * SEQ, SEQ), SEQ), pl.ds(pl.multiple_of(owner * 512, 512), 512)
        ]
        pltpu.make_async_remote_copy(
            ref, ref, ctx_s.at[tick, which, s], ctx_r.at[tick, which, s], to_other, MESH
        ).wait_recv()

    def attend(docs_ref, ctx, tick, lower, upper):
        def sequence(s, carry):
            rows = pl.ds(pl.multiple_of(s * SEQ, SEQ), SEQ)
            numbers = docs_ref[pl.ds(s // 2, 1), :]
            numbers = jnp.broadcast_to(numbers, (SEQ, SEQ)).astype(F32)
            allowed = ahead & (numbers == numbers.T)
            allowed = jnp.concatenate([allowed.astype(F32)] * GROUP, axis=0) > 0.5
            cosine, sine = cos_ref[...], sin_ref[...]

            def piece(g):
                return proj[rows, g * 128 : g * 128 + 128]

            queries = jnp.concatenate(
                [rotate(piece(g), cosine, sine) for g in range(GROUP)], axis=0
            )
            keys = rotate(piece(GROUP), cosine, sine)
            values = piece(GROUP + 1).astype(BF16)
            scores = lax.dot_general(
                queries, keys, (((1,), (1,)), ((), ())), preferred_element_type=F32
            ) * (1.0 / math.sqrt(HEAD_WIDTH))
            scores = jnp.where(allowed, scores, -1e30)
            weights = jnp.exp(scores - jnp.max(scores, axis=-1, keepdims=True))
            weights = (weights / jnp.sum(weights, axis=-1, keepdims=True)).astype(BF16)
            context = jnp.dot(weights, values, preferred_element_type=F32).astype(BF16)
            for g in range(GROUP):
                columns = pl.ds(pl.multiple_of(head * 512 + g * 128, 128), 128)
                ctx[rows, columns] = context[g * SEQ : (g + 1) * SEQ]
            ctx_copy(ctx, tick, s, 1).start()
            ctx_copy(ctx, tick, s, 0).start()
            return carry

        lax.fori_loop(lower, upper, sequence, 0)

    def collect(ctx, tick, r):
        for a in both:
            ctx_arrived(ctx, tick, 2 * r + a, 1)
            ctx_copy(ctx, tick, 2 * r + a, 2).start()
        for a in both:
            ctx_arrived(ctx, tick, 2 * r + a, 0)
            ctx_arrived(ctx, tick, 2 * r + a, 2)
        for a in both:
            rows = slice((2 * r + a) * SEQ, (2 * r + a + 1) * SEQ)
            for block in both:
                low[block, rows] = lax.dot_general(
                    ctx[rows, block * 1024 : block * 1024 + 1024],
                    down_all[a, block],
                    (((1,), (1,)), ((), ())),
                    preferred_element_type=F32,
                ).astype(BF16)

    wave_one.middle()
    seed_in = pltpu.make_async_remote_copy(
        rows_of(place.pair), rows_of(place.pair), misc_s.at[0], misc_r.at[0], to_pair, MESH
    )
    seed_in.wait_recv()
    wave_two.begin()
    wave_one.late()
    pltpu.make_async_remote_copy(
        half_of(1 - parity, tensor), half_of(1 - parity, tensor), misc_s.at[1], misc_r.at[1],
        to_pair, MESH,
    ).wait_recv()
    pass_h = misc(half_of(1 - parity, tensor), half_of(1 - parity, tensor), 12, to_other)
    pass_h.start()
    wave_two.middle()
    load_o.wait()
    share_in = wo.at[index8, pl.ds(pl.multiple_of(other * 1024, 1024), 1024)]
    pltpu.make_async_remote_copy(
        share_in, share_in, misc_s.at[2], misc_r.at[2], to_other, MESH
    ).wait_recv()
    wave_two.late()
    pltpu.make_async_remote_copy(
        half_of(1 - parity, other), half_of(1 - parity, other), misc_s.at[12], misc_r.at[12],
        to_other, MESH,
    ).wait_recv()
    small[0].wait_recv()
    norm_first(1 - parity)
    wave_out.begin()
    for copy in small[1:]:
        copy.wait_recv()
    for copy in loads[1:]:
        copy.wait()
    for stage in range(4):
        wave_one.end(stage)
        wave_two.end(stage)
    project(0, 3)
    attend(docs_in, ctx_one, 0, 0, 2)
    wave_out.middle()
    project(3, 6)
    attend(docs_in, ctx_one, 0, 2, 4)
    wave_out.late()

    def block_member(i, pair=False):
        f, dy = BLOCKS[i]
        return place.pair_near(f, dy) if pair else place.near(f, dy)

    def columns_of(m):
        return pl.ds(pl.multiple_of(m * 256 + tensor * 128, 128), 128)

    def summed(ctx, r, weights_of, up_of):
        total = None
        rows = slice(r * 256, r * 256 + 256)
        for block in both:
            main = jnp.dot(
                ctx[rows, block * 1024 : block * 1024 + 1024],
                weights_of(block),
                preferred_element_type=F32,
            )
            extra = jnp.concatenate(
                [
                    jnp.dot(
                        low[block, (2 * r + a) * SEQ : (2 * r + a + 1) * SEQ],
                        up_of(a),
                        preferred_element_type=F32,
                    )
                    for a in both
                ],
                axis=0,
            )
            value = (main + extra).astype(BF16).astype(F32)
            total = value if total is None else total + value
        return total

    def block_copy(ref, dst, kind_of, n, device):
        send, recv = (hop_s.at[n], hop_r.at[n]) if kind_of == 3 else (
            fwd_s.at[kind_of, n], fwd_r.at[kind_of, n]
        )
        return pltpu.make_async_remote_copy(ref, dst, send, recv, device, MESH)

    steps = [(i, 0) for i in range(4)] + [(i, 1) for i in range(4)]
    for i in range(4, 8):
        steps += [(i, 0), (i, 1)]

    def own_ref(n):
        i, r = steps[n]
        return h_next.at[block_member(i) * 2 + tensor, r]

    def hop_copy(n):
        return block_copy(h_send.at[n], own_ref(n), 3, n, {"section": after})

    def start_block(n):
        i, r = steps[n]
        f, dy = BLOCKS[i]
        slot = place.row(dy) * 2 + place.column(f) // 2
        columns = columns_of(block_member(i))
        total = summed(
            ctx_one, r, lambda block: wo[slot, block * 1024 : block * 1024 + 1024],
            lambda a: up_all[a, :, columns],
        )
        for a in both:
            rows = slice(a * SEQ, a * SEQ + SEQ)
            h_send[n, rows] = (h_all[r, a, :, columns].astype(F32) + total[rows]).astype(BF16)
        hop_copy(n).start()

    def pair_ref(n):
        i, r = steps[n]
        return h_next.at[block_member(i, True) * 2 + tensor, r]

    def pass_own(n, device, kind_of):
        return block_copy(own_ref(n), own_ref(n), kind_of, n, device)

    def pass_pair(n):
        return block_copy(pair_ref(n), pair_ref(n), 2, n, to_other)

    def arrive(n):
        hop_copy(n).wait_recv()
        pass_own(n, to_pair, 0).start()
        pass_own(n, to_other, 1).start()

    def relay(n):
        block_copy(pair_ref(n), pair_ref(n), 0, n, to_pair).wait_recv()
        pass_pair(n).start()

    def other_ref(n, pair):
        i, r = steps[n]
        return h_next.at[block_member(i, pair) * 2 + other, r]

    def run(lower, upper):
        for n in range(lower, upper):
            start_block(n)
            if n >= 3:
                arrive(n - 3)
            if n >= 6:
                relay(n - 6)

    collect(ctx_one, 0, 0)
    wave_out.end(0)
    run(0, 4)
    collect(ctx_one, 0, 1)
    run(4, 8)
    wave_out.end(1)
    run(8, 12)
    wave_out.end(2)
    run(12, 14)
    wave_out.end(3)
    run(14, 16)
    for n in range(13, 16):
        arrive(n)
    for n in range(10, 16):
        relay(n)
    for n in range(16):
        ref = other_ref(n, False)
        block_copy(ref, ref, 1, n, to_other).wait_recv()
        ref = other_ref(n, True)
        block_copy(ref, ref, 2, n, to_other).wait_recv()

    def norm_second(i, carry):
        r, j = i // 8, lax.rem(i, 8)
        a = j // 4
        rows = pl.ds(pl.multiple_of(j * 32, 32), 32)
        total = jnp.zeros((32, 128), F32)
        for block in range(32):
            h = h_next[block, r, rows, :].astype(F32)
            total = total + h * h
        scale = lax.rsqrt(jnp.sum(total, axis=-1, keepdims=True) * (1.0 / WIDTH) + EPS)
        scale = jnp.broadcast_to(scale, (32, 128))
        for block in range(32):
            columns = slice(block * 128, block * 128 + 128)
            h = h_next[block, r, rows, :].astype(F32)
            nrm[pl.ds(pl.multiple_of(i * 32, 32), 32), columns] = (
                h * scale * gain_all[a, :, columns]
            ).astype(BF16)
        return carry

    for r in both:
        lax.fori_loop(8 * r, 8 * r + 8, norm_second, 0)
        project(3 * r, 3 * r + 3)
        attend(docs_next, ctx_two, 1, 2 * r, 2 * r + 2)

    def pair_members(y):
        return y * SIDE + kind, y * SIDE + 3 - kind

    def up_pair(a, y):
        return jnp.concatenate([up_all[a, :, columns_of(m)] for m in pair_members(y)], axis=1)

    def last_output(r):
        square[r] = jnp.zeros((ROWS, 128), F32)

        def last_block(y, carry):
            total = summed(
                ctx_two,
                r,
                lambda block: jnp.concatenate(
                    [wo[2 * y + k, block * 1024 : block * 1024 + 1024] for k in both], axis=1
                ),
                lambda a: up_pair(a, y),
            )
            for k, m in enumerate(pair_members(y)):
                columns = slice(k * 128, k * 128 + 128)
                h = h_next[m * 2 + tensor, r].astype(F32) + total[:, columns]
                h = h.astype(BF16)
                h_last[r, y, :, columns] = h
                h = h.astype(F32)
                square[r] += h * h
            return carry

        lax.fori_loop(0, SIDE, last_block, 0)

    def send_stats(r):
        stat_own[r] = jnp.zeros((8, 128), F32)
        for a in both:
            stat_own[r, a : a + 1, :] = jnp.sum(
                square[r, a * SEQ : a * SEQ + SEQ].T, axis=0, keepdims=True
            )
        stats = [
            misc(stat_own.at[r], stat_in.at[r, k], 13 + 3 * r + k, device)
            for k, device in enumerate((to_other, to_pair, to_pair_other))
        ]
        for copy in stats:
            copy.start()
        return stats

    def rows_at(r, i):
        return rows_out.at[r, pl.ds(pl.multiple_of(i * 16, 16), 16)]

    def scatter_rows(r, stats):
        for copy in stats:
            copy.wait_recv()
        total = stat_own[r] + stat_in[r, 0] + stat_in[r, 1] + stat_in[r, 2]
        scales = lax.rsqrt(total * (1.0 / WIDTH) + EPS)
        column_scale = [jnp.broadcast_to(scales[a : a + 1], (128, 128)).T for a in both]
        for y in range(SIDE):
            for k, m in enumerate(pair_members(y)):
                lower = (m - (y // 2) * 8) * 256 + tensor * 128
                gains = [
                    final_all[a, y // 2, :, pl.ds(pl.multiple_of(lower, 128), 128)] for a in both
                ]
                columns = slice(k * 128, k * 128 + 128)
                value = sum(
                    h_last[r, y, a * SEQ : a * SEQ + SEQ, columns].astype(F32)
                    * column_scale[a]
                    * gains[a]
                    for a in both
                )
                rows_out[r, :, (2 * y + k) * 128 : (2 * y + k + 1) * 128] = value.astype(BF16)

        def scatter(i, carry):
            f, dy = lax.rem(i, 2), i // 2
            x, y = place.column(f), place.row(dy)
            pltpu.make_async_remote_copy(
                rows_at(r, y * 2 + x // 2), rows_in.at[r, index8], scatter_s.at[r], scatter_r.at[r],
                {"member": y * SIDE + x}, MESH,
            ).start()
            return carry

        lax.fori_loop(1, 8, scatter, 0)
        return local(rows_at(r, index8), rows_in.at[r, index8], 7 + r)

    def seven(r):
        ref = rows_in.at[r, pl.ds(0, 7)]
        return pltpu.make_async_remote_copy(
            ref, ref, scatter_s.at[r], scatter_r.at[r], to_other, MESH
        )

    def average(r, keep):
        keep.wait()
        seven(r).wait_recv()
        total = rows_in[r, 0].astype(F32)
        for i in range(1, 8):
            total = total + rows_in[r, i].astype(F32)
        total = (total * (1.0 / MEMBERS)).astype(BF16)
        for half in both:
            mean_own[r, half] = total[:, half * 512 : half * 512 + 512]
        misc(mean_own.at[r, tensor], mean_in.at[r, tensor], 19 + 2 * r, {"section": after}).start()
        misc(
            mean_own.at[r, other], mean_in.at[r, tensor], 20 + 2 * r,
            {"section": after, "tensor": other},
        ).start()

    def hopped(r):
        for half, index in ((tensor, 19 + 2 * r), (other, 20 + 2 * r)):
            ref = mean_in.at[r, half]
            pltpu.make_async_remote_copy(
                ref, ref, misc_s.at[index], misc_r.at[index], to_other, MESH
            ).wait_recv()

    def gather_of(r):
        return PlaneGather(
            place,
            lambda part: mean_in.at[r, part],
            lambda part, slot: fin.at[r, slot, part],
            lambda part: fin.at[r, pl.ds(0, 15), part],
            ag_send.at[r],
            ag_recv.at[r],
        )

    collect(ctx_two, 1, 0)
    last_output(0)
    keep_zero = scatter_rows(0, send_stats(0))
    collect(ctx_two, 1, 1)
    last_output(1)
    stats_one = send_stats(1)
    average(0, keep_zero)
    keep_one = scatter_rows(1, stats_one)
    final_zero, final_one = gather_of(0), gather_of(1)
    hopped(0)
    final_zero.begin()
    fin[0, member] = mean_in[0]
    average(1, keep_one)
    final_zero.middle()
    hopped(1)
    final_one.begin()
    fin[1, member] = mean_in[1]
    final_zero.end()

    def place_rows(r):
        for m in range(MEMBERS):
            x, y = m % SIDE, m // SIDE
            side = ((x + 1) // 2) % 2
            lower = r * SEQ + (y * 2 + x // 2) * 16
            for part in both:
                for s in range(4):
                    column = (s // 2 * SIDE + (side if s % 2 == 0 else 3 - side)) * 256 + part * 128
                    out_ref[lower : lower + 16, column : column + 128] = fin[
                        r, m, part, :, s * 128 : s * 128 + 128
                    ]

    final_one.middle()
    place_rows(0)
    final_one.end()
    place_rows(1)

    for wave in (wave_one, wave_two, wave_out):
        wave.sent()
    final_zero.sent()
    final_one.sent()
    for tick, ctx in enumerate((ctx_one, ctx_two)):
        for which in range(3):
            for s in range(4):
                ctx_copy(ctx, tick, s, which).wait_send()
    for n in range(16):
        hop_copy(n).wait_send()
        pass_own(n, to_pair, 0).wait_send()
        pass_own(n, to_other, 1).wait_send()
        pass_pair(n).wait_send()
    for copy in pending:
        copy.wait_send()
    for r in both:
        seven(r).wait_send()


def per_device(
    hidden_input,
    document_index,
    query_key_value_weight,
    output_weight,
    adapter_down,
    adapter_up,
    attention_gain,
    final_norm_gain,
):
    cosine, sine = rope_tables()
    vmem = pl.BlockSpec(memory_space=pltpu.VMEM)
    anywhere = pl.BlockSpec(memory_space=pl.ANY)
    dma = pltpu.SemaphoreType.DMA
    averaged = pl.pallas_call(
        kernel,
        out_shape=jax.ShapeDtypeStruct((ROWS, WIDTH // 2), BF16),
        in_specs=[anywhere, vmem, anywhere, anywhere] + [vmem] * 6,
        out_specs=vmem,
        scratch_shapes=[
            pltpu.VMEM((WIDTH, 768), BF16),
            pltpu.VMEM((8, 2048, 128), BF16),
            pltpu.VMEM((2, 2, SEQ, WIDTH), BF16),
            pltpu.VMEM((2 * ROWS, WIDTH), BF16),
            pltpu.VMEM((2 * ROWS, 768), F32),
            pltpu.VMEM((2 * ROWS, 2048), BF16),
            pltpu.VMEM((2 * ROWS, 2048), BF16),
            pltpu.VMEM((2, 2 * ROWS, 16), BF16),
            pltpu.VMEM((2, SEQ), jnp.int32),
            pltpu.VMEM((2, 1, WIDTH), F32),
            pltpu.VMEM((2, 2, 16, 1024), BF16),
            pltpu.VMEM((2, 16, WIDTH), BF16),
            pltpu.VMEM((2, 2, 1, WIDTH // 2), F32),
            pltpu.VMEM((16, ROWS, 128), BF16),
            pltpu.VMEM((32, 2, ROWS, 128), BF16),
            pltpu.VMEM((2, SIDE, ROWS, 256), BF16),
            pltpu.VMEM((2, ROWS, 128), F32),
            pltpu.VMEM((2, 8, 128), F32),
            pltpu.VMEM((2, 3, 8, 128), F32),
            pltpu.VMEM((2, SEQ, 1024), BF16),
            pltpu.VMEM((2, 8, 16, 1024), BF16),
            pltpu.VMEM((2, 2, 16, 512), BF16),
            pltpu.VMEM((2, 2, 16, 512), BF16),
            pltpu.VMEM((2, MEMBERS, 2, 16, 512), BF16),
            dma((3, 2)),
            dma((3, 2, 7)),
            dma((2, 2)),
            dma((2, 2, 15)),
            dma((9,)),
            dma((2, 3, 4)),
            dma((2, 3, 4)),
            dma((16,)),
            dma((16,)),
            dma((3, 16)),
            dma((3, 16)),
            dma((23,)),
            dma((23,)),
            dma((2,)),
            dma((2,)),
        ],
        compiler_params=pltpu.CompilerParams(
            collective_id=0, has_side_effects=True, vmem_limit_bytes=58 * 1024 * 1024
        ),
        name="relay",
    )(
        hidden_input.reshape(2, SEQ, WIDTH),
        document_index[0],
        query_key_value_weight[0].reshape(256, 1536),
        output_weight[0],
        adapter_down[0, 0].T,
        adapter_up[0, 0],
        attention_gain[0],
        final_norm_gain,
        jnp.asarray(cosine),
        jnp.asarray(sine),
    )
    return averaged.reshape(1, 2, SEQ, WIDTH // 2)


def solution(mesh):
    return jax.shard_map(
        per_device,
        mesh=mesh,
        in_specs=(
            P("member", "section", None, None, None),
            P("section", None, None),
            P("section", "member", "tensor", None),
            P("section", "tensor", "member"),
            P("member", "section", "tensor", None),
            P("member", "section", None, None),
            P("member", "section", None),
            P("member", "tensor"),
        ),
        out_specs=P("section", None, None, "tensor"),
        check_vma=False,
    )
```

```python
import math

import jax
import jax.numpy as jnp
import numpy as np
from jax import lax
from jax.experimental import pallas as pl
from jax.experimental.pallas import tpu as pltpu
from jax.sharding import PartitionSpec as P

HEAD_WIDTH = 128
GROUP = 4
WIDTH = 4096
ROWS = 256
SEQ = 128
MEMBERS = 16
SIDE = 4
EPS = 1e-05
MESH = pl.DeviceIdType.MESH
F32 = jnp.float32
BF16 = jnp.bfloat16


def rope_tables():
    position = np.arange(SEQ, dtype=np.float32)
    frequency = np.exp(
        np.arange(HEAD_WIDTH // 2, dtype=np.float32)
        * np.float32(-2.0 * math.log(500000.0) / HEAD_WIDTH)
    ).astype(np.float32)
    angles = (position[:, None] * frequency[None, :]).astype(np.float32)
    cosine, sine = np.cos(angles), np.sin(angles)
    return (
        np.concatenate([cosine, cosine], axis=1).astype(np.float32),
        np.concatenate([-sine, sine], axis=1).astype(np.float32),
    )


def wrap(value):
    return lax.rem(value + 2 * SIDE, SIDE)


class Torus:
    def __init__(self):
        self.member = lax.axis_index("member")
        self.x = lax.rem(self.member, SIDE)
        self.y = self.member // SIDE

    def at(self, part, du, dv):
        dx, dy = (du, dv) if part == 0 else (dv, du)
        return wrap(self.y + dy) * SIDE + wrap(self.x + dx)


class Place(Torus):
    def __init__(self):
        super().__init__()
        self.kind = lax.rem((self.x + 1) // 2, 2)
        self.parity = lax.rem(self.x, 2)
        self.pair_x = self.x + 1 - 2 * self.parity
        self.pair = self.y * SIDE + self.pair_x
        self.index = self.y * 2 + self.x // 2

    def column(self, f):
        return self.x + f * (3 - 2 * self.x)

    def row(self, dy):
        return wrap(self.y + dy)

    def near(self, f, dy):
        return self.row(dy) * SIDE + self.column(f)

    def pair_near(self, f, dy):
        return self.row(dy) * SIDE + self.pair_x + f * (3 - 2 * self.pair_x)


class PairGather:
    def __init__(self, place, own, slot, whole, send_sem, recv_sem):
        self.place, self.own, self.slot, self.whole = place, own, slot, whole
        self.send_sem, self.recv_sem = send_sem, recv_sem

    def copy(self, src, dst, part, f, dy, index):
        return pltpu.make_async_remote_copy(
            src_ref=src,
            dst_ref=dst,
            send_sem=self.send_sem.at[part],
            recv_sem=self.recv_sem.at[part, index],
            device_id={"member": self.place.near(f, dy)},
            device_id_type=MESH,
        )

    def ref(self, part, f, dy, which=None):
        return self.slot(self.place.column(f), self.place.row(dy), part, which)

    def move(self, part, f, dy, which, to_f, to_dy, index):
        ref = self.ref(part, f, dy, which)
        self.copy(ref, ref, part, to_f, to_dy, index).start()

    def wait(self, part, f, dy, index):
        ref = self.ref(part, f, dy)
        self.copy(ref, ref, part, 1, 0, index).wait_recv()

    def begin(self):
        for part, targets in ((0, ((1, 0), (0, 1), (0, -1))), (1, ((0, 1), (0, -1), (1, 0)))):
            for index, (f, dy) in enumerate(targets):
                self.copy(self.own(part), self.ref(part, 0, 0), part, f, dy, index).start()

    def cross_near(self):
        self.wait(0, 1, 0, 0)
        self.move(0, 1, 0, None, 0, 1, 3)
        self.move(0, 1, 0, None, 0, -1, 4)

    def round_near(self):
        self.wait(1, 0, -1, 0)
        self.move(1, 0, -1, 0, 0, 1, 3)
        self.move(1, 0, -1, None, 1, 0, 4)
        self.wait(1, 0, 1, 1)
        self.move(1, 0, 1, 1, 0, -1, 3)
        self.move(1, 0, 1, None, 1, 0, 5)

    def own_far(self):
        self.wait(0, 0, -1, 1)
        self.move(0, 0, -1, 0, 0, 1, 5)
        self.wait(0, 0, 1, 2)
        self.move(0, 0, 1, 1, 0, -1, 5)

    def round_far(self):
        self.wait(1, 0, 2, 3)
        self.move(1, 0, 2, None, 1, 0, 6)

    def cross_far(self):
        self.wait(0, 1, -1, 3)
        self.move(0, 1, -1, 0, 0, 1, 6)
        self.wait(0, 1, 1, 4)
        self.move(0, 1, 1, 1, 0, -1, 6)

    def middle(self):
        self.cross_near()
        self.round_near()

    def late(self):
        self.own_far()
        self.round_far()
        self.cross_far()

    def end(self, stage):
        if stage == 0:
            self.wait(1, 1, 0, 2)
        elif stage == 1:
            self.wait(1, 1, -1, 4)
            self.wait(1, 1, 1, 5)
        elif stage == 2:
            self.wait(0, 0, 2, 5)
        else:
            self.wait(0, 1, 2, 6)
            self.wait(1, 1, 2, 6)

    def sent(self):
        for part in (0, 1):
            ref = self.whole(part)
            self.copy(ref, ref, part, 1, 0, 0).wait_send()


class PlaneGather:
    order = (0, -1, 1, 2)

    def __init__(self, torus, own, slot, whole, send_sem, recv_sem):
        self.torus, self.own, self.slot, self.whole = torus, own, slot, whole
        self.send_sem, self.recv_sem = send_sem, recv_sem

    def copy(self, src, dst, part, du, dv, index):
        return pltpu.make_async_remote_copy(
            src_ref=src,
            dst_ref=dst,
            send_sem=self.send_sem.at[part],
            recv_sem=self.recv_sem.at[part, index],
            device_id={"member": self.torus.at(part, du, dv)},
            device_id_type=MESH,
        )

    def ref(self, part, du, dv):
        return self.slot(part, self.torus.at(part, du, dv))

    def begin(self):
        for part in (0, 1):
            for k in (1, 2, 3):
                self.copy(self.own(part), self.ref(part, 0, 0), part, -self.order[k], 0, k - 1).start()
        for part in (0, 1):
            self.spread(part, 0)

    def spread(self, part, q):
        here = self.ref(part, self.order[q], 0)
        src = self.own(part) if q == 0 else here
        for k in (1, 2, 3):
            self.copy(src, here, part, 0, -self.order[k], 3 * q + k + 2).start()

    def wait(self, part, du, dv, index):
        ref = self.ref(part, du, dv)
        self.copy(ref, ref, part, 1, 0, index).wait_recv()

    def middle(self):
        for q in (1, 2, 3):
            for part in (0, 1):
                self.wait(part, self.order[q], 0, q - 1)
                self.spread(part, q)

    def end(self):
        for q in range(SIDE):
            for part in (0, 1):
                for k in (1, 2, 3):
                    self.wait(part, self.order[q], self.order[k], 3 * q + k + 2)

    def sent(self):
        for part in (0, 1):
            ref = self.whole(part)
            self.copy(ref, ref, part, 1, 0, 0).wait_send()


def rotate(values, cosine, sine):
    return (values * cosine + pltpu.roll(values, HEAD_WIDTH // 2, 1) * sine).astype(BF16)


QKV_SPLIT = (((0, 144), (0, 80), (80, 64)), ((144, 112), (144, 64), (208, 48)))
OUT_SPLIT = (((0, 1152), (0, 576), (576, 576)), ((1152, 896), (1152, 448), (1600, 448)))


def cut(split, part, which):
    return split[part][0 if which is None else which + 1]


BLOCKS = ((0, 0), (1, 0), (0, -1), (0, 1), (1, -1), (1, 1), (0, 2), (1, 2))


def kernel(
    hidden_in, docs_in, qkv_in, out_in, down_in, up_in, gain_in, final_in, cos_ref, sin_ref,
    out_ref,
    wq, wo, h_all, nrm, proj, ctx_one, ctx_two, low, docs_next, gain_all, down_all, up_all, final_all,
    h_send, h_next, h_last, square, stat_own, stat_in, rows_out, rows_in, mean_own, mean_in, fin,
    pg_send, pg_recv, ag_send, ag_recv, local_sem, ctx_s, ctx_r, hop_s, hop_r, fwd_s, fwd_r,
    misc_s, misc_r, scatter_s, scatter_r,
):
    place = Place()
    member, kind, parity, index8 = place.member, place.kind, place.parity, place.index
    section = lax.axis_index("section")
    tensor = lax.axis_index("tensor")
    other = 1 - tensor
    sections = 8
    after = lax.rem(section + 1, sections)
    before = lax.rem(section + sections - 1, sections)
    both = (0, 1)

    barrier = pltpu.get_barrier_semaphore()

    def signal(device):
        pl.semaphore_signal(barrier, inc=1, device_id=device, device_id_type=MESH)

    def greet(i, carry):
        signal({"member": lax.rem(member + i, MEMBERS)})
        return carry

    lax.fori_loop(1, MEMBERS, greet, 0)
    signal({"tensor": other})
    signal({"member": place.pair, "tensor": other})
    for near in (after, before):
        signal({"section": near})
        signal({"section": near, "tensor": other})

    pending = []

    def local(src, dst, index):
        copy = pltpu.make_async_copy(src, dst, local_sem.at[index])
        copy.start()
        return copy

    def misc(src, dst, index, device):
        copy = pltpu.make_async_remote_copy(
            src, dst, misc_s.at[index], misc_r.at[index], device, MESH
        )
        pending.append(copy)
        return copy

    load_h = local(hidden_in, h_all.at[:, parity], 0)
    loads = [
        local(gain_in, gain_all.at[parity], 1),
        local(down_in, down_all.at[parity, tensor], 2),
        local(up_in, up_all.at[parity], 3),
        local(final_in, final_all.at[parity, tensor], 4),
        local(
            qkv_in.at[:, pl.ds(pl.multiple_of(kind * 768, 256), 768)],
            wq.at[pl.ds(pl.multiple_of(member * 256, 256), 256)],
            5,
        ),
    ]
    load_o = local(
        out_in.at[:, pl.ds(pl.multiple_of(tensor * 128, 128), 128)],
        wo.at[index8, pl.ds(pl.multiple_of(tensor * 1024, 1024), 1024)],
        6,
    )
    pl.semaphore_wait(barrier, MEMBERS - 1 + 6)

    def qkv_slot(of_pair):
        def slot(x, y, part, which):
            if of_pair:
                x = x + 1 - 2 * lax.rem(x, 2)
            lower, size = cut(QKV_SPLIT, part, which)
            return wq.at[pl.ds(pl.multiple_of((y * SIDE + x) * 256 + lower, 16), size)]

        return slot

    def own_qkv(part):
        lower, size = cut(QKV_SPLIT, part, None)
        return qkv_in.at[pl.ds(lower, size), pl.ds(pl.multiple_of(kind * 768, 256), 768)]

    def whole_qkv(part):
        return wq.at[pl.ds(0, 7 * cut(QKV_SPLIT, part, None)[1])]

    def out_slot(x, y, part, which):
        lower, size = cut(OUT_SPLIT, part, which)
        return wo.at[y * 2 + x // 2, pl.ds(lower, size)]

    def whole_out(part):
        return wo.at[pl.ds(0, 7), pl.ds(0, cut(OUT_SPLIT, part, None)[1])]

    wave_one = PairGather(place, own_qkv, qkv_slot(False), whole_qkv, pg_send.at[0], pg_recv.at[0])
    pair_slot = qkv_slot(True)
    wave_two = PairGather(
        place,
        lambda part: pair_slot(place.x, place.y, part, None),
        pair_slot,
        whole_qkv,
        pg_send.at[1],
        pg_recv.at[1],
    )
    wave_out = PairGather(
        place,
        lambda part: out_slot(place.x, place.y, part, None),
        out_slot,
        whole_out,
        pg_send.at[2],
        pg_recv.at[2],
    )

    to_pair = {"member": place.pair}
    to_pair_other = {"member": place.pair, "tensor": other}
    to_other = {"tensor": other}

    rows_of = lambda m: wq.at[pl.ds(pl.multiple_of(m * 256, 256), 256)]
    seed = misc(
        qkv_in.at[:, pl.ds(pl.multiple_of((1 - kind) * 768, 256), 768)], rows_of(member), 0, to_pair
    )
    seed.start()
    wave_one.begin()
    half_of = lambda a, t: h_all.at[t, a]
    share_h = misc(
        hidden_in.at[tensor], half_of(parity, tensor), 1, to_pair
    )
    share_h.start()
    share_out = misc(
        out_in.at[:, pl.ds(pl.multiple_of(other * 128, 128), 128)],
        wo.at[index8, pl.ds(pl.multiple_of(tensor * 1024, 1024), 1024)],
        2,
        to_other,
    )
    share_out.start()
    small = [misc(gain_in, gain_all.at[parity], 3, to_pair), misc(up_in, up_all.at[parity], 4, to_pair)]
    for k, device in enumerate((to_other, to_pair, to_pair_other)):
        small.append(misc(down_in, down_all.at[parity, tensor], 5 + k, device))
        small.append(misc(final_in, final_all.at[parity, tensor], 8 + k, device))
    small.append(misc(docs_in, docs_next, 11, {"section": after}))
    for copy in small:
        copy.start()
    load_h.wait()
    loads[0].wait()

    def norm_first(a):
        def block(i, carry):
            r, j = i // 8, lax.rem(i, 8)
            h = h_all[r, a, pl.ds(pl.multiple_of(j * 16, 16), 16), :].astype(F32)
            scale = lax.rsqrt(jnp.mean(h * h, axis=-1, keepdims=True) + EPS)
            nrm[pl.ds(pl.multiple_of(r * 256 + a * 128 + j * 16, 16), 16), :] = (
                h * scale * gain_all[a]
            ).astype(BF16)
            return carry

        lax.fori_loop(0, ROWS // 16, block, 0)

    norm_first(parity)

    def project(lower, upper):
        def block(n, carry):
            rows = pl.ds(pl.multiple_of(n // 3 * 256, 256), 256)
            columns = pl.ds(pl.multiple_of(lax.rem(n, 3) * 256, 256), 256)
            proj[rows, columns] = jnp.dot(nrm[rows, :], wq[:, columns], preferred_element_type=F32)
            return carry

        lax.fori_loop(lower, upper, block, 0)

    ahead = lax.broadcasted_iota(jnp.int32, (SEQ, SEQ), 0) >= lax.broadcasted_iota(
        jnp.int32, (SEQ, SEQ), 1
    )
    head = 2 * tensor + kind

    def ctx_copy(ctx, tick, s, which):
        owner = 2 * tensor + (1 - kind if which == 2 else kind)
        ref = ctx.at[
            pl.ds(pl.multiple_of(s * SEQ, SEQ), SEQ), pl.ds(pl.multiple_of(owner * 512, 512), 512)
        ]
        return pltpu.make_async_remote_copy(
            ref, ref, ctx_s.at[tick, which, s], ctx_r.at[tick, which, s],
            to_pair if which == 1 else to_other, MESH,
        )

    def ctx_arrived(ctx, tick, s, which):
        t = tensor if which == 1 else other
        owner = 2 * t + (kind if which == 0 else 1 - kind)
        ref = ctx.at[
            pl.ds(pl.multiple_of(s * SEQ, SEQ), SEQ), pl.ds(pl.multiple_of(owner * 512, 512), 512)
        ]
        pltpu.make_async_remote_copy(
            ref, ref, ctx_s.at[tick, which, s], ctx_r.at[tick, which, s], to_other, MESH
        ).wait_recv()

    def attend(docs_ref, ctx, tick, lower, upper):
        def sequence(s, carry):
            rows = pl.ds(pl.multiple_of(s * SEQ, SEQ), SEQ)
            numbers = docs_ref[pl.ds(s // 2, 1), :]
            numbers = jnp.broadcast_to(numbers, (SEQ, SEQ)).astype(F32)
            allowed = ahead & (numbers == numbers.T)
            allowed = jnp.concatenate([allowed.astype(F32)] * GROUP, axis=0) > 0.5
            cosine, sine = cos_ref[...], sin_ref[...]

            def piece(g):
                return proj[rows, g * 128 : g * 128 + 128]

            queries = jnp.concatenate(
                [rotate(piece(g), cosine, sine) for g in range(GROUP)], axis=0
            )
            keys = rotate(piece(GROUP), cosine, sine)
            values = piece(GROUP + 1).astype(BF16)
            scores = lax.dot_general(
                queries, keys, (((1,), (1,)), ((), ())), preferred_element_type=F32
            ) * (1.0 / math.sqrt(HEAD_WIDTH))
            scores = jnp.where(allowed, scores, -1e30)
            weights = jnp.exp(scores - jnp.max(scores, axis=-1, keepdims=True))
            weights = (weights / jnp.sum(weights, axis=-1, keepdims=True)).astype(BF16)
            context = jnp.dot(weights, values, preferred_element_type=F32).astype(BF16)
            for g in range(GROUP):
                columns = pl.ds(pl.multiple_of(head * 512 + g * 128, 128), 128)
                ctx[rows, columns] = context[g * SEQ : (g + 1) * SEQ]
            ctx_copy(ctx, tick, s, 1).start()
            ctx_copy(ctx, tick, s, 0).start()
            return carry

        lax.fori_loop(lower, upper, sequence, 0)

    def collect(ctx, tick, r):
        for a in both:
            ctx_arrived(ctx, tick, 2 * r + a, 1)
            ctx_copy(ctx, tick, 2 * r + a, 2).start()
        for a in both:
            ctx_arrived(ctx, tick, 2 * r + a, 0)
            ctx_arrived(ctx, tick, 2 * r + a, 2)
        for a in both:
            rows = slice((2 * r + a) * SEQ, (2 * r + a + 1) * SEQ)
            for block in both:
                low[block, rows] = lax.dot_general(
                    ctx[rows, block * 1024 : block * 1024 + 1024],
                    down_all[a, block],
                    (((1,), (1,)), ((), ())),
                    preferred_element_type=F32,
                ).astype(BF16)

    wave_one.middle()
    seed_in = pltpu.make_async_remote_copy(
        rows_of(place.pair), rows_of(place.pair), misc_s.at[0], misc_r.at[0], to_pair, MESH
    )
    seed_in.wait_recv()
    wave_two.begin()
    wave_one.late()
    pltpu.make_async_remote_copy(
        half_of(1 - parity, tensor), half_of(1 - parity, tensor), misc_s.at[1], misc_r.at[1],
        to_pair, MESH,
    ).wait_recv()
    pass_h = misc(half_of(1 - parity, tensor), half_of(1 - parity, tensor), 12, to_other)
    pass_h.start()
    wave_two.middle()
    load_o.wait()
    share_in = wo.at[index8, pl.ds(pl.multiple_of(other * 1024, 1024), 1024)]
    pltpu.make_async_remote_copy(
        share_in, share_in, misc_s.at[2], misc_r.at[2], to_other, MESH
    ).wait_recv()
    wave_two.late()
    pltpu.make_async_remote_copy(
        half_of(1 - parity, other), half_of(1 - parity, other), misc_s.at[12], misc_r.at[12],
        to_other, MESH,
    ).wait_recv()
    small[0].wait_recv()
    norm_first(1 - parity)
    wave_out.begin()
    for copy in small[1:]:
        copy.wait_recv()
    for copy in loads[1:]:
        copy.wait()
    for stage in range(4):
        wave_one.end(stage)
        wave_two.end(stage)
    project(0, 3)
    attend(docs_in, ctx_one, 0, 0, 2)
    project(3, 6)
    attend(docs_in, ctx_one, 0, 2, 4)
    wave_out.cross_near()
    wave_out.own_far()
    wave_out.round_near()

    def block_member(i, pair=False):
        f, dy = BLOCKS[i]
        return place.pair_near(f, dy) if pair else place.near(f, dy)

    def columns_of(m):
        return pl.ds(pl.multiple_of(m * 256 + tensor * 128, 128), 128)

    def summed(ctx, r, weights_of, up_of):
        total = None
        rows = slice(r * 256, r * 256 + 256)
        for block in both:
            main = jnp.dot(
                ctx[rows, block * 1024 : block * 1024 + 1024],
                weights_of(block),
                preferred_element_type=F32,
            )
            extra = jnp.concatenate(
                [
                    jnp.dot(
                        low[block, (2 * r + a) * SEQ : (2 * r + a + 1) * SEQ],
                        up_of(a),
                        preferred_element_type=F32,
                    )
                    for a in both
                ],
                axis=0,
            )
            value = (main + extra).astype(BF16).astype(F32)
            total = value if total is None else total + value
        return total

    def block_copy(ref, dst, kind_of, n, device):
        send, recv = (hop_s.at[n], hop_r.at[n]) if kind_of == 3 else (
            fwd_s.at[kind_of, n], fwd_r.at[kind_of, n]
        )
        return pltpu.make_async_remote_copy(ref, dst, send, recv, device, MESH)

    steps = [(i, r) for lower in (0, 4) for r in both for i in range(lower, lower + 4)]

    def own_ref(n):
        i, r = steps[n]
        return h_next.at[block_member(i) * 2 + tensor, r]

    def hop_copy(n):
        return block_copy(h_send.at[n], own_ref(n), 3, n, {"section": after})

    def start_block(n):
        i, r = steps[n]
        f, dy = BLOCKS[i]
        slot = place.row(dy) * 2 + place.column(f) // 2
        columns = columns_of(block_member(i))
        total = summed(
            ctx_one, r, lambda block: wo[slot, block * 1024 : block * 1024 + 1024],
            lambda a: up_all[a, :, columns],
        )
        for a in both:
            rows = slice(a * SEQ, a * SEQ + SEQ)
            h_send[n, rows] = (h_all[r, a, :, columns].astype(F32) + total[rows]).astype(BF16)
        hop_copy(n).start()

    def pair_ref(n):
        i, r = steps[n]
        return h_next.at[block_member(i, True) * 2 + tensor, r]

    def pass_own(n, device, kind_of):
        return block_copy(own_ref(n), own_ref(n), kind_of, n, device)

    def pass_pair(n):
        return block_copy(pair_ref(n), pair_ref(n), 2, n, to_other)

    def arrive(n):
        hop_copy(n).wait_recv()
        pass_own(n, to_pair, 0).start()
        pass_own(n, to_other, 1).start()

    def relay(n):
        block_copy(pair_ref(n), pair_ref(n), 0, n, to_pair).wait_recv()
        pass_pair(n).start()

    def other_ref(n, pair):
        i, r = steps[n]
        return h_next.at[block_member(i, pair) * 2 + other, r]

    def run(lower, upper):
        for n in range(lower, upper):
            start_block(n)
            if n >= 4:
                arrive(n - 4)
            if n >= 7:
                relay(n - 7)

    collect(ctx_one, 0, 0)
    wave_out.end(0)
    run(0, 4)
    wave_out.cross_far()
    collect(ctx_one, 0, 1)
    wave_out.round_far()
    run(4, 8)
    wave_out.end(1)
    run(8, 10)
    wave_out.end(2)
    run(10, 11)
    wave_out.end(3)
    run(11, 16)
    for n in (9, 10, 11):
        relay(n)

    def complete(r):
        for n in range(16):
            if steps[n][1] == r:
                ref = other_ref(n, False)
                block_copy(ref, ref, 1, n, to_other).wait_recv()
                ref = other_ref(n, True)
                block_copy(ref, ref, 2, n, to_other).wait_recv()

    def norm_second(i, carry):
        r, j = i // 8, lax.rem(i, 8)
        a = j // 4
        rows = pl.ds(pl.multiple_of(j * 32, 32), 32)
        total = jnp.zeros((32, 128), F32)
        for block in range(32):
            h = h_next[block, r, rows, :].astype(F32)
            total = total + h * h
        scale = lax.rsqrt(jnp.sum(total, axis=-1, keepdims=True) * (1.0 / WIDTH) + EPS)
        scale = jnp.broadcast_to(scale, (32, 128))
        for block in range(32):
            columns = slice(block * 128, block * 128 + 128)
            h = h_next[block, r, rows, :].astype(F32)
            nrm[pl.ds(pl.multiple_of(i * 32, 32), 32), columns] = (
                h * scale * gain_all[a, :, columns]
            ).astype(BF16)
        return carry

    complete(0)
    arrive(12)
    lax.fori_loop(0, 8, norm_second, 0)
    arrive(13)
    relay(12)
    project(0, 3)
    arrive(14)
    arrive(15)
    relay(13)
    attend(docs_next, ctx_two, 1, 0, 2)
    relay(14)
    relay(15)
    complete(1)
    lax.fori_loop(8, 16, norm_second, 0)
    project(3, 6)
    attend(docs_next, ctx_two, 1, 2, 4)

    def pair_members(y):
        return y * SIDE + kind, y * SIDE + 3 - kind

    def up_pair(a, y):
        return jnp.concatenate([up_all[a, :, columns_of(m)] for m in pair_members(y)], axis=1)

    def last_output(r):
        square[r] = jnp.zeros((ROWS, 128), F32)

        def last_block(y, carry):
            total = summed(
                ctx_two,
                r,
                lambda block: jnp.concatenate(
                    [wo[2 * y + k, block * 1024 : block * 1024 + 1024] for k in both], axis=1
                ),
                lambda a: up_pair(a, y),
            )
            for k, m in enumerate(pair_members(y)):
                columns = slice(k * 128, k * 128 + 128)
                h = h_next[m * 2 + tensor, r].astype(F32) + total[:, columns]
                h = h.astype(BF16)
                h_last[r, y, :, columns] = h
                h = h.astype(F32)
                square[r] += h * h
            return carry

        lax.fori_loop(0, SIDE, last_block, 0)

    def send_stats(r):
        stat_own[r] = jnp.zeros((8, 128), F32)
        for a in both:
            stat_own[r, a : a + 1, :] = jnp.sum(
                square[r, a * SEQ : a * SEQ + SEQ].T, axis=0, keepdims=True
            )
        stats = [
            misc(stat_own.at[r], stat_in.at[r, k], 13 + 3 * r + k, device)
            for k, device in enumerate((to_other, to_pair, to_pair_other))
        ]
        for copy in stats:
            copy.start()
        return stats

    def rows_at(r, i):
        return rows_out.at[r, pl.ds(pl.multiple_of(i * 16, 16), 16)]

    def scatter_rows(r, stats):
        for copy in stats:
            copy.wait_recv()
        total = stat_own[r] + stat_in[r, 0] + stat_in[r, 1] + stat_in[r, 2]
        scales = lax.rsqrt(total * (1.0 / WIDTH) + EPS)
        column_scale = [jnp.broadcast_to(scales[a : a + 1], (128, 128)).T for a in both]
        for y in range(SIDE):
            for k, m in enumerate(pair_members(y)):
                lower = (m - (y // 2) * 8) * 256 + tensor * 128
                gains = [
                    final_all[a, y // 2, :, pl.ds(pl.multiple_of(lower, 128), 128)] for a in both
                ]
                columns = slice(k * 128, k * 128 + 128)
                value = sum(
                    h_last[r, y, a * SEQ : a * SEQ + SEQ, columns].astype(F32)
                    * column_scale[a]
                    * gains[a]
                    for a in both
                )
                rows_out[r, :, (2 * y + k) * 128 : (2 * y + k + 1) * 128] = value.astype(BF16)

        def scatter(i, carry):
            f, dy = lax.rem(i, 2), i // 2
            x, y = place.column(f), place.row(dy)
            pltpu.make_async_remote_copy(
                rows_at(r, y * 2 + x // 2), rows_in.at[r, index8], scatter_s.at[r], scatter_r.at[r],
                {"member": y * SIDE + x}, MESH,
            ).start()
            return carry

        lax.fori_loop(1, 8, scatter, 0)
        return local(rows_at(r, index8), rows_in.at[r, index8], 7 + r)

    def seven(r):
        ref = rows_in.at[r, pl.ds(0, 7)]
        return pltpu.make_async_remote_copy(
            ref, ref, scatter_s.at[r], scatter_r.at[r], to_other, MESH
        )

    def average(r, keep):
        keep.wait()
        seven(r).wait_recv()
        total = rows_in[r, 0].astype(F32)
        for i in range(1, 8):
            total = total + rows_in[r, i].astype(F32)
        total = (total * (1.0 / MEMBERS)).astype(BF16)
        for half in both:
            mean_own[r, half] = total[:, half * 512 : half * 512 + 512]
        misc(mean_own.at[r, tensor], mean_in.at[r, tensor], 19 + 2 * r, {"section": after}).start()
        misc(
            mean_own.at[r, other], mean_in.at[r, tensor], 20 + 2 * r,
            {"section": after, "tensor": other},
        ).start()

    def hopped(r):
        for half, index in ((tensor, 19 + 2 * r), (other, 20 + 2 * r)):
            ref = mean_in.at[r, half]
            pltpu.make_async_remote_copy(
                ref, ref, misc_s.at[index], misc_r.at[index], to_other, MESH
            ).wait_recv()

    def gather_of(r):
        return PlaneGather(
            place,
            lambda part: mean_in.at[r, part],
            lambda part, slot: fin.at[r, slot, part],
            lambda part: fin.at[r, pl.ds(0, 15), part],
            ag_send.at[r],
            ag_recv.at[r],
        )

    collect(ctx_two, 1, 0)
    last_output(0)
    keep_zero = scatter_rows(0, send_stats(0))
    collect(ctx_two, 1, 1)
    last_output(1)
    stats_one = send_stats(1)
    average(0, keep_zero)
    keep_one = scatter_rows(1, stats_one)
    final_zero, final_one = gather_of(0), gather_of(1)
    hopped(0)
    final_zero.begin()
    fin[0, member] = mean_in[0]
    average(1, keep_one)
    final_zero.middle()
    hopped(1)
    final_one.begin()
    fin[1, member] = mean_in[1]
    final_zero.end()

    def place_rows(r):
        for m in range(MEMBERS):
            x, y = m % SIDE, m // SIDE
            side = ((x + 1) // 2) % 2
            lower = r * SEQ + (y * 2 + x // 2) * 16
            for part in both:
                for s in range(4):
                    column = (s // 2 * SIDE + (side if s % 2 == 0 else 3 - side)) * 256 + part * 128
                    out_ref[lower : lower + 16, column : column + 128] = fin[
                        r, m, part, :, s * 128 : s * 128 + 128
                    ]

    final_one.middle()
    place_rows(0)
    final_one.end()
    place_rows(1)

    for wave in (wave_one, wave_two, wave_out):
        wave.sent()
    final_zero.sent()
    final_one.sent()
    for tick, ctx in enumerate((ctx_one, ctx_two)):
        for which in range(3):
            for s in range(4):
                ctx_copy(ctx, tick, s, which).wait_send()
    for n in range(16):
        hop_copy(n).wait_send()
        pass_own(n, to_pair, 0).wait_send()
        pass_own(n, to_other, 1).wait_send()
        pass_pair(n).wait_send()
    for copy in pending:
        copy.wait_send()
    for r in both:
        seven(r).wait_send()


def per_device(
    hidden_input,
    document_index,
    query_key_value_weight,
    output_weight,
    adapter_down,
    adapter_up,
    attention_gain,
    final_norm_gain,
):
    cosine, sine = rope_tables()
    vmem = pl.BlockSpec(memory_space=pltpu.VMEM)
    anywhere = pl.BlockSpec(memory_space=pl.ANY)
    dma = pltpu.SemaphoreType.DMA
    averaged = pl.pallas_call(
        kernel,
        out_shape=jax.ShapeDtypeStruct((ROWS, WIDTH // 2), BF16),
        in_specs=[anywhere, vmem, anywhere, anywhere] + [vmem] * 6,
        out_specs=vmem,
        scratch_shapes=[
            pltpu.VMEM((WIDTH, 768), BF16),
            pltpu.VMEM((8, 2048, 128), BF16),
            pltpu.VMEM((2, 2, SEQ, WIDTH), BF16),
            pltpu.VMEM((2 * ROWS, WIDTH), BF16),
            pltpu.VMEM((2 * ROWS, 768), F32),
            pltpu.VMEM((2 * ROWS, 2048), BF16),
            pltpu.VMEM((2 * ROWS, 2048), BF16),
            pltpu.VMEM((2, 2 * ROWS, 16), BF16),
            pltpu.VMEM((2, SEQ), jnp.int32),
            pltpu.VMEM((2, 1, WIDTH), F32),
            pltpu.VMEM((2, 2, 16, 1024), BF16),
            pltpu.VMEM((2, 16, WIDTH), BF16),
            pltpu.VMEM((2, 2, 1, WIDTH // 2), F32),
            pltpu.VMEM((16, ROWS, 128), BF16),
            pltpu.VMEM((32, 2, ROWS, 128), BF16),
            pltpu.VMEM((2, SIDE, ROWS, 256), BF16),
            pltpu.VMEM((2, ROWS, 128), F32),
            pltpu.VMEM((2, 8, 128), F32),
            pltpu.VMEM((2, 3, 8, 128), F32),
            pltpu.VMEM((2, SEQ, 1024), BF16),
            pltpu.VMEM((2, 8, 16, 1024), BF16),
            pltpu.VMEM((2, 2, 16, 512), BF16),
            pltpu.VMEM((2, 2, 16, 512), BF16),
            pltpu.VMEM((2, MEMBERS, 2, 16, 512), BF16),
            dma((3, 2)),
            dma((3, 2, 7)),
            dma((2, 2)),
            dma((2, 2, 15)),
            dma((9,)),
            dma((2, 3, 4)),
            dma((2, 3, 4)),
            dma((16,)),
            dma((16,)),
            dma((3, 16)),
            dma((3, 16)),
            dma((23,)),
            dma((23,)),
            dma((2,)),
            dma((2,)),
        ],
        compiler_params=pltpu.CompilerParams(
            collective_id=0, has_side_effects=True, vmem_limit_bytes=58 * 1024 * 1024
        ),
        name="relay",
    )(
        hidden_input.reshape(2, SEQ, WIDTH),
        document_index[0],
        query_key_value_weight[0].reshape(256, 1536),
        output_weight[0],
        adapter_down[0, 0].T,
        adapter_up[0, 0],
        attention_gain[0],
        final_norm_gain,
        jnp.asarray(cosine),
        jnp.asarray(sine),
    )
    return averaged.reshape(1, 2, SEQ, WIDTH // 2)


def solution(mesh):
    return jax.shard_map(
        per_device,
        mesh=mesh,
        in_specs=(
            P("member", "section", None, None, None),
            P("section", None, None),
            P("section", "member", "tensor", None),
            P("section", "tensor", "member"),
            P("member", "section", "tensor", None),
            P("member", "section", None, None),
            P("member", "section", None),
            P("member", "tensor"),
        ),
        out_specs=P("section", None, None, "tensor"),
        check_vma=False,
    )
```

```python
import math

import jax
import jax.numpy as jnp
import numpy as np
from jax import lax
from jax.experimental import pallas as pl
from jax.experimental.pallas import tpu as pltpu
from jax.sharding import PartitionSpec as P

HEAD_WIDTH = 128
GROUP = 4
WIDTH = 4096
ROWS = 256
SEQ = 128
MEMBERS = 16
SIDE = 4
EPS = 1e-05
MESH = pl.DeviceIdType.MESH
F32 = jnp.float32
BF16 = jnp.bfloat16


def rope_tables():
    position = np.arange(SEQ, dtype=np.float32)
    frequency = np.exp(
        np.arange(HEAD_WIDTH // 2, dtype=np.float32)
        * np.float32(-2.0 * math.log(500000.0) / HEAD_WIDTH)
    ).astype(np.float32)
    angles = (position[:, None] * frequency[None, :]).astype(np.float32)
    cosine, sine = np.cos(angles), np.sin(angles)
    return (
        np.concatenate([cosine, cosine], axis=1).astype(np.float32),
        np.concatenate([-sine, sine], axis=1).astype(np.float32),
    )


def wrap(value):
    return lax.rem(value + 2 * SIDE, SIDE)


class Torus:
    def __init__(self):
        self.member = lax.axis_index("member")
        self.x = lax.rem(self.member, SIDE)
        self.y = self.member // SIDE

    def at(self, part, du, dv):
        dx, dy = (du, dv) if part == 0 else (dv, du)
        return wrap(self.y + dy) * SIDE + wrap(self.x + dx)


class Place(Torus):
    def __init__(self):
        super().__init__()
        self.kind = lax.rem((self.x + 1) // 2, 2)
        self.parity = lax.rem(self.x, 2)
        self.pair_x = self.x + 1 - 2 * self.parity
        self.pair = self.y * SIDE + self.pair_x
        self.index = self.y * 2 + self.x // 2

    def column(self, f):
        return self.x + f * (3 - 2 * self.x)

    def row(self, dy):
        return wrap(self.y + dy)

    def near(self, f, dy):
        return self.row(dy) * SIDE + self.column(f)

    def pair_near(self, f, dy):
        return self.row(dy) * SIDE + self.pair_x + f * (3 - 2 * self.pair_x)


class PairGather:
    def __init__(self, place, own, slot, whole, send_sem, recv_sem):
        self.place, self.own, self.slot, self.whole = place, own, slot, whole
        self.send_sem, self.recv_sem = send_sem, recv_sem

    def copy(self, src, dst, part, f, dy, index):
        return pltpu.make_async_remote_copy(
            src_ref=src,
            dst_ref=dst,
            send_sem=self.send_sem.at[part],
            recv_sem=self.recv_sem.at[part, index],
            device_id={"member": self.place.near(f, dy)},
            device_id_type=MESH,
        )

    def ref(self, part, f, dy, which=None):
        return self.slot(self.place.column(f), self.place.row(dy), part, which)

    def move(self, part, f, dy, which, to_f, to_dy, index):
        ref = self.ref(part, f, dy, which)
        self.copy(ref, ref, part, to_f, to_dy, index).start()

    def wait(self, part, f, dy, index):
        ref = self.ref(part, f, dy)
        self.copy(ref, ref, part, 1, 0, index).wait_recv()

    def begin(self):
        for part, targets in ((0, ((1, 0), (0, 1), (0, -1))), (1, ((0, 1), (0, -1), (1, 0)))):
            for index, (f, dy) in enumerate(targets):
                self.copy(self.own(part), self.ref(part, 0, 0), part, f, dy, index).start()

    def cross_near(self):
        self.wait(0, 1, 0, 0)
        self.move(0, 1, 0, None, 0, 1, 3)
        self.move(0, 1, 0, None, 0, -1, 4)

    def round_near(self):
        self.wait(1, 0, -1, 0)
        self.move(1, 0, -1, 0, 0, 1, 3)
        self.move(1, 0, -1, None, 1, 0, 4)
        self.wait(1, 0, 1, 1)
        self.move(1, 0, 1, 1, 0, -1, 3)
        self.move(1, 0, 1, None, 1, 0, 5)

    def own_far(self):
        self.wait(0, 0, -1, 1)
        self.move(0, 0, -1, 0, 0, 1, 5)
        self.wait(0, 0, 1, 2)
        self.move(0, 0, 1, 1, 0, -1, 5)

    def round_far(self):
        self.wait(1, 0, 2, 3)
        self.move(1, 0, 2, None, 1, 0, 6)

    def cross_far(self):
        self.wait(0, 1, -1, 3)
        self.move(0, 1, -1, 0, 0, 1, 6)
        self.wait(0, 1, 1, 4)
        self.move(0, 1, 1, 1, 0, -1, 6)

    def middle(self):
        self.cross_near()
        self.round_near()

    def late(self):
        self.own_far()
        self.round_far()
        self.cross_far()

    def end(self, stage):
        if stage == 0:
            self.wait(1, 1, 0, 2)
        elif stage == 1:
            self.wait(1, 1, -1, 4)
            self.wait(1, 1, 1, 5)
        elif stage == 2:
            self.wait(0, 0, 2, 5)
        else:
            self.wait(0, 1, 2, 6)
            self.wait(1, 1, 2, 6)

    def sent(self):
        for part in (0, 1):
            ref = self.whole(part)
            self.copy(ref, ref, part, 1, 0, 0).wait_send()


class PlaneGather:
    order = (0, -1, 1, 2)

    def __init__(self, torus, own, slot, whole, send_sem, recv_sem):
        self.torus, self.own, self.slot, self.whole = torus, own, slot, whole
        self.send_sem, self.recv_sem = send_sem, recv_sem

    def copy(self, src, dst, part, du, dv, index):
        return pltpu.make_async_remote_copy(
            src_ref=src,
            dst_ref=dst,
            send_sem=self.send_sem.at[part],
            recv_sem=self.recv_sem.at[part, index],
            device_id={"member": self.torus.at(part, du, dv)},
            device_id_type=MESH,
        )

    def ref(self, part, du, dv):
        return self.slot(part, self.torus.at(part, du, dv))

    def begin(self):
        for part in (0, 1):
            for k in (1, 2, 3):
                self.copy(self.own(part), self.ref(part, 0, 0), part, -self.order[k], 0, k - 1).start()
        for part in (0, 1):
            self.spread(part, 0)

    def spread(self, part, q):
        here = self.ref(part, self.order[q], 0)
        src = self.own(part) if q == 0 else here
        for k in (1, 2, 3):
            self.copy(src, here, part, 0, -self.order[k], 3 * q + k + 2).start()

    def wait(self, part, du, dv, index):
        ref = self.ref(part, du, dv)
        self.copy(ref, ref, part, 1, 0, index).wait_recv()

    def middle(self):
        for q in (1, 2, 3):
            for part in (0, 1):
                self.wait(part, self.order[q], 0, q - 1)
                self.spread(part, q)

    def end(self):
        for q in range(SIDE):
            for part in (0, 1):
                for k in (1, 2, 3):
                    self.wait(part, self.order[q], self.order[k], 3 * q + k + 2)

    def sent(self):
        for part in (0, 1):
            ref = self.whole(part)
            self.copy(ref, ref, part, 1, 0, 0).wait_send()


def rotate(values, cosine, sine):
    return (values * cosine + pltpu.roll(values, HEAD_WIDTH // 2, 1) * sine).astype(BF16)


QKV_SPLIT = (((0, 144), (0, 80), (80, 64)), ((144, 112), (144, 64), (208, 48)))
OUT_SPLIT = (((0, 1152), (0, 576), (576, 576)), ((1152, 896), (1152, 448), (1600, 448)))


def cut(split, part, which):
    return split[part][0 if which is None else which + 1]


BLOCKS = ((0, 0), (1, 0), (0, -1), (0, 1), (1, -1), (1, 1), (0, 2), (1, 2))


def kernel(
    hidden_in, docs_in, qkv_in, out_in, down_in, up_in, gain_in, final_in, cos_ref, sin_ref,
    out_ref,
    wq, wo, h_all, nrm, proj, ctx_one, ctx_two, held, low, docs_next, gain_all, down_all, up_all, final_all,
    h_send, h_next, h_last, square, stat_own, stat_in, rows_out, rows_in, mean_own, mean_in, fin,
    pg_send, pg_recv, ag_send, ag_recv, local_sem, ctx_s, ctx_r, hop_s, hop_r, fwd_s, fwd_r,
    misc_s, misc_r, scatter_s, scatter_r,
):
    place = Place()
    member, kind, parity, index8 = place.member, place.kind, place.parity, place.index
    section = lax.axis_index("section")
    tensor = lax.axis_index("tensor")
    other = 1 - tensor
    sections = 8
    after = lax.rem(section + 1, sections)
    before = lax.rem(section + sections - 1, sections)
    both = (0, 1)

    barrier = pltpu.get_barrier_semaphore()

    def signal(device):
        pl.semaphore_signal(barrier, inc=1, device_id=device, device_id_type=MESH)

    def greet(i, carry):
        signal({"member": lax.rem(member + i, MEMBERS)})
        return carry

    lax.fori_loop(1, MEMBERS, greet, 0)
    signal({"tensor": other})
    signal({"member": place.pair, "tensor": other})
    for near in (after, before):
        signal({"section": near})
        signal({"section": near, "tensor": other})

    pending = []

    def local(src, dst, index):
        copy = pltpu.make_async_copy(src, dst, local_sem.at[index])
        copy.start()
        return copy

    def misc(src, dst, index, device):
        copy = pltpu.make_async_remote_copy(
            src, dst, misc_s.at[index], misc_r.at[index], device, MESH
        )
        pending.append(copy)
        return copy

    load_h = local(hidden_in, h_all.at[:, parity], 0)
    loads = [
        local(gain_in, gain_all.at[parity], 1),
        local(down_in, down_all.at[parity, tensor], 2),
        local(up_in, up_all.at[parity], 3),
        local(final_in, final_all.at[parity, tensor], 4),
        local(
            qkv_in.at[:, pl.ds(pl.multiple_of(kind * 768, 256), 768)],
            wq.at[pl.ds(pl.multiple_of(member * 256, 256), 256)],
            5,
        ),
    ]
    load_o = local(
        out_in.at[:, pl.ds(pl.multiple_of(tensor * 128, 128), 128)],
        wo.at[index8, pl.ds(pl.multiple_of(tensor * 1024, 1024), 1024)],
        6,
    )
    pl.semaphore_wait(barrier, MEMBERS - 1 + 6)

    COLUMNS = ((0, 512), (512, 256))

    def group_columns(group, base=0):
        lower, size = COLUMNS[group]
        return pl.ds(pl.multiple_of(base + lower, 256), size)

    def qkv_wave(group, of_pair):
        def slot(x, y, part, which):
            if of_pair:
                x = x + 1 - 2 * lax.rem(x, 2)
            lower, size = cut(QKV_SPLIT, part, which)
            rows = pl.ds(pl.multiple_of((y * SIDE + x) * 256 + lower, 16), size)
            return wq.at[rows, group_columns(group)]

        def own(part):
            lower, size = cut(QKV_SPLIT, part, None)
            if of_pair:
                return slot(place.x, place.y, part, None)
            return qkv_in.at[pl.ds(lower, size), group_columns(group, kind * 768)]

        def whole(part):
            return wq.at[pl.ds(0, 7 * cut(QKV_SPLIT, part, None)[1]), group_columns(group)]

        n = 2 * group + of_pair
        return PairGather(place, own, slot, whole, pg_send.at[n], pg_recv.at[n])

    def out_slot(x, y, part, which):
        lower, size = cut(OUT_SPLIT, part, which)
        return wo.at[y * 2 + x // 2, pl.ds(lower, size)]

    def whole_out(part):
        return wo.at[pl.ds(0, 7), pl.ds(0, cut(OUT_SPLIT, part, None)[1])]

    waves = [qkv_wave(group, of_pair) for group in both for of_pair in both]
    wave_out = PairGather(
        place,
        lambda part: out_slot(place.x, place.y, part, None),
        out_slot,
        whole_out,
        pg_send.at[4],
        pg_recv.at[4],
    )

    to_pair = {"member": place.pair}
    to_pair_other = {"member": place.pair, "tensor": other}
    to_other = {"tensor": other}

    def seed_rows(m, group):
        return wq.at[pl.ds(pl.multiple_of(m * 256, 256), 256), group_columns(group)]

    def seed_copy(group):
        return misc(
            qkv_in.at[:, group_columns(group, (1 - kind) * 768)], seed_rows(member, group),
            0 if group == 0 else 23, to_pair,
        )

    def seeded(group):
        ref, index = seed_rows(place.pair, group), 0 if group == 0 else 23
        pltpu.make_async_remote_copy(
            ref, ref, misc_s.at[index], misc_r.at[index], to_pair, MESH
        ).wait_recv()

    seed_copy(0).start()
    waves[0].begin()
    seed_copy(1).start()
    half_of = lambda a, t: h_all.at[t, a]
    share_h = misc(
        hidden_in.at[tensor], half_of(parity, tensor), 1, to_pair
    )
    share_h.start()
    share_out = misc(
        out_in.at[:, pl.ds(pl.multiple_of(other * 128, 128), 128)],
        wo.at[index8, pl.ds(pl.multiple_of(tensor * 1024, 1024), 1024)],
        2,
        to_other,
    )
    share_out.start()
    small = [misc(gain_in, gain_all.at[parity], 3, to_pair), misc(up_in, up_all.at[parity], 4, to_pair)]
    for k, device in enumerate((to_other, to_pair, to_pair_other)):
        small.append(misc(down_in, down_all.at[parity, tensor], 5 + k, device))
        small.append(misc(final_in, final_all.at[parity, tensor], 8 + k, device))
    small.append(misc(docs_in, docs_next, 11, {"section": after}))
    for copy in small:
        copy.start()
    load_h.wait()
    loads[0].wait()

    def norm_first(a):
        def block(i, carry):
            r, j = i // 8, lax.rem(i, 8)
            h = h_all[r, a, pl.ds(pl.multiple_of(j * 16, 16), 16), :].astype(F32)
            scale = lax.rsqrt(jnp.mean(h * h, axis=-1, keepdims=True) + EPS)
            nrm[pl.ds(pl.multiple_of(r * 256 + a * 128 + j * 16, 16), 16), :] = (
                h * scale * gain_all[a]
            ).astype(BF16)
            return carry

        lax.fori_loop(0, ROWS // 16, block, 0)

    norm_first(parity)

    def project(r, group):
        rows = slice(r * 256, r * 256 + 256)

        def block(n, carry):
            columns = pl.ds(pl.multiple_of(n * 256, 256), 256)
            proj[rows, columns] = jnp.dot(nrm[rows, :], wq[:, columns], preferred_element_type=F32)
            return carry

        lax.fori_loop(2 * group, 2 + group, block, 0)

    ahead = lax.broadcasted_iota(jnp.int32, (SEQ, SEQ), 0) >= lax.broadcasted_iota(
        jnp.int32, (SEQ, SEQ), 1
    )
    head = 2 * tensor + kind

    def ctx_part(ctx, s, group, owner):
        return ctx.at[
            pl.ds(pl.multiple_of(s * SEQ, SEQ), SEQ),
            pl.ds(pl.multiple_of(owner * 512 + group * 256, 256), 256),
        ]

    def ctx_copy(ctx, tick, s, group, which):
        ref = ctx_part(ctx, s, group, 2 * tensor + (1 - kind if which == 2 else kind))
        n = 2 * s + group
        return pltpu.make_async_remote_copy(
            ref, ref, ctx_s.at[tick, which, n], ctx_r.at[tick, which, n],
            to_pair if which == 1 else to_other, MESH,
        )

    def ctx_arrived(ctx, tick, s, group, which):
        t = tensor if which == 1 else other
        ref = ctx_part(ctx, s, group, 2 * t + (kind if which == 0 else 1 - kind))
        n = 2 * s + group
        pltpu.make_async_remote_copy(
            ref, ref, ctx_s.at[tick, which, n], ctx_r.at[tick, which, n], to_other, MESH
        ).wait_recv()

    def attend(docs_ref, ctx, tick, r, group):
        def sequence(s, carry):
            rows = pl.ds(pl.multiple_of(s * SEQ, SEQ), SEQ)
            numbers = jnp.broadcast_to(docs_ref[r : r + 1, :], (SEQ, SEQ)).astype(F32)
            allowed = ahead & (numbers == numbers.T)
            allowed = jnp.concatenate([allowed.astype(F32)] * 2, axis=0) > 0.5
            cosine, sine = cos_ref[...], sin_ref[...]

            def piece(g):
                return proj[rows, g * 128 : g * 128 + 128]

            if group == 0:
                held[s, 0] = rotate(piece(0), cosine, sine)
                held[s, 1] = piece(1).astype(BF16)
            queries = jnp.concatenate(
                [rotate(piece(2 + 2 * group + g), cosine, sine) for g in both], axis=0
            )
            scores = lax.dot_general(
                queries, held[s, 0], (((1,), (1,)), ((), ())), preferred_element_type=F32
            ) * (1.0 / math.sqrt(HEAD_WIDTH))
            scores = jnp.where(allowed, scores, -1e30)
            weights = jnp.exp(scores - jnp.max(scores, axis=-1, keepdims=True))
            weights = (weights / jnp.sum(weights, axis=-1, keepdims=True)).astype(BF16)
            context = jnp.dot(weights, held[s, 1], preferred_element_type=F32).astype(BF16)
            for g in both:
                columns = pl.ds(pl.multiple_of(head * 512 + group * 256 + g * 128, 128), 128)
                ctx[rows, columns] = context[g * SEQ : (g + 1) * SEQ]
            ctx_copy(ctx, tick, s, group, 1).start()
            ctx_copy(ctx, tick, s, group, 0).start()
            return carry

        lax.fori_loop(2 * r, 2 * r + 2, sequence, 0)

    def relay_contexts(ctx, tick, r, group):
        for a in both:
            ctx_arrived(ctx, tick, 2 * r + a, group, 1)
            ctx_copy(ctx, tick, 2 * r + a, group, 2).start()

    def collect(ctx, tick, r):
        for a in both:
            for group in both:
                ctx_arrived(ctx, tick, 2 * r + a, group, 0)
                ctx_arrived(ctx, tick, 2 * r + a, group, 2)
        for a in both:
            rows = slice((2 * r + a) * SEQ, (2 * r + a + 1) * SEQ)
            for block in both:
                low[block, rows] = lax.dot_general(
                    ctx[rows, block * 1024 : block * 1024 + 1024],
                    down_all[a, block],
                    (((1,), (1,)), ((), ())),
                    preferred_element_type=F32,
                ).astype(BF16)

    waves[0].middle()
    seeded(0)
    waves[1].begin()
    waves[0].late()
    pltpu.make_async_remote_copy(
        half_of(1 - parity, tensor), half_of(1 - parity, tensor), misc_s.at[1], misc_r.at[1],
        to_pair, MESH,
    ).wait_recv()
    pass_h = misc(half_of(1 - parity, tensor), half_of(1 - parity, tensor), 12, to_other)
    pass_h.start()
    waves[1].middle()
    waves[2].begin()
    waves[1].late()
    pltpu.make_async_remote_copy(
        half_of(1 - parity, other), half_of(1 - parity, other), misc_s.at[12], misc_r.at[12],
        to_other, MESH,
    ).wait_recv()
    small[0].wait_recv()
    norm_first(1 - parity)
    load_o.wait()
    share_in = wo.at[index8, pl.ds(pl.multiple_of(other * 1024, 1024), 1024)]
    pltpu.make_async_remote_copy(
        share_in, share_in, misc_s.at[2], misc_r.at[2], to_other, MESH
    ).wait_recv()
    for copy in small[1:]:
        copy.wait_recv()
    for copy in loads[1:]:
        copy.wait()
    seeded(1)
    waves[2].middle()
    waves[3].begin()
    for stage in range(4):
        waves[0].end(stage)
        waves[1].end(stage)
    waves[2].late()
    project(0, 0)
    attend(docs_in, ctx_one, 0, 0, 0)
    waves[3].middle()
    project(1, 0)
    attend(docs_in, ctx_one, 0, 1, 0)
    waves[3].late()
    wave_out.begin()
    relay_contexts(ctx_one, 0, 0, 0)
    for stage in range(4):
        waves[2].end(stage)
        waves[3].end(stage)
    project(0, 1)
    attend(docs_in, ctx_one, 0, 0, 1)
    project(1, 1)
    attend(docs_in, ctx_one, 0, 1, 1)
    wave_out.cross_near()
    wave_out.own_far()
    relay_contexts(ctx_one, 0, 1, 0)
    relay_contexts(ctx_one, 0, 0, 1)

    def block_member(i, pair=False):
        f, dy = BLOCKS[i]
        return place.pair_near(f, dy) if pair else place.near(f, dy)

    def columns_of(m):
        return pl.ds(pl.multiple_of(m * 256 + tensor * 128, 128), 128)

    def summed(ctx, r, weights_of, up_of):
        total = None
        rows = slice(r * 256, r * 256 + 256)
        for block in both:
            main = jnp.dot(
                ctx[rows, block * 1024 : block * 1024 + 1024],
                weights_of(block),
                preferred_element_type=F32,
            )
            extra = jnp.concatenate(
                [
                    jnp.dot(
                        low[block, (2 * r + a) * SEQ : (2 * r + a + 1) * SEQ],
                        up_of(a),
                        preferred_element_type=F32,
                    )
                    for a in both
                ],
                axis=0,
            )
            value = (main + extra).astype(BF16).astype(F32)
            total = value if total is None else total + value
        return total

    def block_copy(ref, dst, kind_of, n, device):
        send, recv = (hop_s.at[n], hop_r.at[n]) if kind_of == 3 else (
            fwd_s.at[kind_of, n], fwd_r.at[kind_of, n]
        )
        return pltpu.make_async_remote_copy(ref, dst, send, recv, device, MESH)

    steps = [(i, r) for r in both for i in range(4)] + [(i, r) for r in both for i in (4, 5)]
    steps += [(i, r) for i in (6, 7) for r in both]

    def own_ref(n):
        i, r = steps[n]
        return h_next.at[block_member(i) * 2 + tensor, r]

    def hop_copy(n):
        return block_copy(h_send.at[n], own_ref(n), 3, n, {"section": after})

    def start_block(n):
        i, r = steps[n]
        f, dy = BLOCKS[i]
        slot = place.row(dy) * 2 + place.column(f) // 2
        columns = columns_of(block_member(i))
        total = summed(
            ctx_one, r, lambda block: wo[slot, block * 1024 : block * 1024 + 1024],
            lambda a: up_all[a, :, columns],
        )
        for a in both:
            rows = slice(a * SEQ, a * SEQ + SEQ)
            h_send[n, rows] = (h_all[r, a, :, columns].astype(F32) + total[rows]).astype(BF16)
        hop_copy(n).start()

    def pair_ref(n):
        i, r = steps[n]
        return h_next.at[block_member(i, True) * 2 + tensor, r]

    def pass_own(n, device, kind_of):
        return block_copy(own_ref(n), own_ref(n), kind_of, n, device)

    def pass_pair(n):
        return block_copy(pair_ref(n), pair_ref(n), 2, n, to_other)

    def arrive(n):
        hop_copy(n).wait_recv()
        pass_own(n, to_pair, 0).start()
        pass_own(n, to_other, 1).start()

    def relay(n):
        block_copy(pair_ref(n), pair_ref(n), 0, n, to_pair).wait_recv()
        pass_pair(n).start()

    def other_ref(n, pair):
        i, r = steps[n]
        return h_next.at[block_member(i, pair) * 2 + other, r]

    def run(lower, upper):
        for n in range(lower, upper):
            start_block(n)
            if n >= 4:
                arrive(n - 4)
            if n >= 7:
                relay(n - 7)

    collect(ctx_one, 0, 0)
    run(0, 1)
    wave_out.round_near()
    relay_contexts(ctx_one, 0, 1, 1)
    wave_out.end(0)
    run(1, 4)
    wave_out.cross_far()
    collect(ctx_one, 0, 1)
    run(4, 8)
    wave_out.round_far()
    wave_out.end(1)
    run(8, 12)
    wave_out.end(2)
    run(12, 14)
    wave_out.end(3)
    run(14, 16)
    relay(9)
    relay(10)
    for n in range(12, 16):
        arrive(n)
        relay(n - 1)
    relay(15)

    def complete(r):
        for n in range(16):
            if steps[n][1] == r:
                ref = other_ref(n, False)
                block_copy(ref, ref, 1, n, to_other).wait_recv()
                ref = other_ref(n, True)
                block_copy(ref, ref, 2, n, to_other).wait_recv()

    def norm_second(i, carry):
        r, j = i // 8, lax.rem(i, 8)
        a = j // 4
        rows = pl.ds(pl.multiple_of(j * 32, 32), 32)
        total = jnp.zeros((32, 128), F32)
        for block in range(32):
            h = h_next[block, r, rows, :].astype(F32)
            total = total + h * h
        scale = lax.rsqrt(jnp.sum(total, axis=-1, keepdims=True) * (1.0 / WIDTH) + EPS)
        scale = jnp.broadcast_to(scale, (32, 128))
        for block in range(32):
            columns = slice(block * 128, block * 128 + 128)
            h = h_next[block, r, rows, :].astype(F32)
            nrm[pl.ds(pl.multiple_of(i * 32, 32), 32), columns] = (
                h * scale * gain_all[a, :, columns]
            ).astype(BF16)
        return carry

    for r in both:
        complete(r)
        lax.fori_loop(8 * r, 8 * r + 8, norm_second, 0)
        for group in both:
            project(r, group)
            attend(docs_next, ctx_two, 1, r, group)

    def pair_members(y):
        return y * SIDE + kind, y * SIDE + 3 - kind

    def up_pair(a, y):
        return jnp.concatenate([up_all[a, :, columns_of(m)] for m in pair_members(y)], axis=1)

    def last_output(r):
        square[r] = jnp.zeros((ROWS, 128), F32)

        def last_block(y, carry):
            total = summed(
                ctx_two,
                r,
                lambda block: jnp.concatenate(
                    [wo[2 * y + k, block * 1024 : block * 1024 + 1024] for k in both], axis=1
                ),
                lambda a: up_pair(a, y),
            )
            for k, m in enumerate(pair_members(y)):
                columns = slice(k * 128, k * 128 + 128)
                h = h_next[m * 2 + tensor, r].astype(F32) + total[:, columns]
                h = h.astype(BF16)
                h_last[r, y, :, columns] = h
                h = h.astype(F32)
                square[r] += h * h
            return carry

        lax.fori_loop(0, SIDE, last_block, 0)

    def send_stats(r):
        stat_own[r] = jnp.zeros((8, 128), F32)
        for a in both:
            stat_own[r, a : a + 1, :] = jnp.sum(
                square[r, a * SEQ : a * SEQ + SEQ].T, axis=0, keepdims=True
            )
        stats = [
            misc(stat_own.at[r], stat_in.at[r, k], 13 + 3 * r + k, device)
            for k, device in enumerate((to_other, to_pair, to_pair_other))
        ]
        for copy in stats:
            copy.start()
        return stats

    def rows_at(r, i):
        return rows_out.at[r, pl.ds(pl.multiple_of(i * 16, 16), 16)]

    def scatter_rows(r, stats):
        for copy in stats:
            copy.wait_recv()
        total = stat_own[r] + stat_in[r, 0] + stat_in[r, 1] + stat_in[r, 2]
        scales = lax.rsqrt(total * (1.0 / WIDTH) + EPS)
        column_scale = [jnp.broadcast_to(scales[a : a + 1], (128, 128)).T for a in both]
        for y in range(SIDE):
            for k, m in enumerate(pair_members(y)):
                lower = (m - (y // 2) * 8) * 256 + tensor * 128
                gains = [
                    final_all[a, y // 2, :, pl.ds(pl.multiple_of(lower, 128), 128)] for a in both
                ]
                columns = slice(k * 128, k * 128 + 128)
                value = sum(
                    h_last[r, y, a * SEQ : a * SEQ + SEQ, columns].astype(F32)
                    * column_scale[a]
                    * gains[a]
                    for a in both
                )
                rows_out[r, :, (2 * y + k) * 128 : (2 * y + k + 1) * 128] = value.astype(BF16)

        def scatter(i, carry):
            f, dy = lax.rem(i, 2), i // 2
            x, y = place.column(f), place.row(dy)
            pltpu.make_async_remote_copy(
                rows_at(r, y * 2 + x // 2), rows_in.at[r, index8], scatter_s.at[r], scatter_r.at[r],
                {"member": y * SIDE + x}, MESH,
            ).start()
            return carry

        lax.fori_loop(1, 8, scatter, 0)
        return local(rows_at(r, index8), rows_in.at[r, index8], 7 + r)

    def seven(r):
        ref = rows_in.at[r, pl.ds(0, 7)]
        return pltpu.make_async_remote_copy(
            ref, ref, scatter_s.at[r], scatter_r.at[r], to_other, MESH
        )

    def average(r, keep):
        keep.wait()
        seven(r).wait_recv()
        total = rows_in[r, 0].astype(F32)
        for i in range(1, 8):
            total = total + rows_in[r, i].astype(F32)
        total = (total * (1.0 / MEMBERS)).astype(BF16)
        for half in both:
            mean_own[r, half] = total[:, half * 512 : half * 512 + 512]
        misc(mean_own.at[r, tensor], mean_in.at[r, tensor], 19 + 2 * r, {"section": after}).start()
        misc(
            mean_own.at[r, other], mean_in.at[r, tensor], 20 + 2 * r,
            {"section": after, "tensor": other},
        ).start()

    def hopped(r):
        for half, index in ((tensor, 19 + 2 * r), (other, 20 + 2 * r)):
            ref = mean_in.at[r, half]
            pltpu.make_async_remote_copy(
                ref, ref, misc_s.at[index], misc_r.at[index], to_other, MESH
            ).wait_recv()

    def gather_of(r):
        return PlaneGather(
            place,
            lambda part: mean_in.at[r, part],
            lambda part, slot: fin.at[r, slot, part],
            lambda part: fin.at[r, pl.ds(0, 15), part],
            ag_send.at[r],
            ag_recv.at[r],
        )

    relay_contexts(ctx_two, 1, 0, 0)
    relay_contexts(ctx_two, 1, 0, 1)
    collect(ctx_two, 1, 0)
    last_output(0)
    keep_zero = scatter_rows(0, send_stats(0))
    relay_contexts(ctx_two, 1, 1, 0)
    relay_contexts(ctx_two, 1, 1, 1)
    average(0, keep_zero)
    collect(ctx_two, 1, 1)
    last_output(1)
    stats_one = send_stats(1)
    final_zero, final_one = gather_of(0), gather_of(1)
    hopped(0)
    final_zero.begin()
    fin[0, member] = mean_in[0]
    keep_one = scatter_rows(1, stats_one)
    final_zero.middle()
    average(1, keep_one)
    hopped(1)
    final_one.begin()
    fin[1, member] = mean_in[1]
    final_zero.end()

    def place_rows(r):
        for m in range(MEMBERS):
            x, y = m % SIDE, m // SIDE
            side = ((x + 1) // 2) % 2
            lower = r * SEQ + (y * 2 + x // 2) * 16
            for part in both:
                for s in range(4):
                    column = (s // 2 * SIDE + (side if s % 2 == 0 else 3 - side)) * 256 + part * 128
                    out_ref[lower : lower + 16, column : column + 128] = fin[
                        r, m, part, :, s * 128 : s * 128 + 128
                    ]

    final_one.middle()
    place_rows(0)
    final_one.end()
    place_rows(1)

    for wave in waves + [wave_out]:
        wave.sent()
    final_zero.sent()
    final_one.sent()
    for tick, ctx in enumerate((ctx_one, ctx_two)):
        for which in range(3):
            for s in range(4):
                for group in both:
                    ctx_copy(ctx, tick, s, group, which).wait_send()
    for n in range(16):
        hop_copy(n).wait_send()
        pass_own(n, to_pair, 0).wait_send()
        pass_own(n, to_other, 1).wait_send()
        pass_pair(n).wait_send()
    for copy in pending:
        copy.wait_send()
    for r in both:
        seven(r).wait_send()


def per_device(
    hidden_input,
    document_index,
    query_key_value_weight,
    output_weight,
    adapter_down,
    adapter_up,
    attention_gain,
    final_norm_gain,
):
    cosine, sine = rope_tables()
    vmem = pl.BlockSpec(memory_space=pltpu.VMEM)
    anywhere = pl.BlockSpec(memory_space=pl.ANY)
    dma = pltpu.SemaphoreType.DMA
    averaged = pl.pallas_call(
        kernel,
        out_shape=jax.ShapeDtypeStruct((ROWS, WIDTH // 2), BF16),
        in_specs=[anywhere, vmem, anywhere, anywhere] + [vmem] * 6,
        out_specs=vmem,
        scratch_shapes=[
            pltpu.VMEM((WIDTH, 768), BF16),
            pltpu.VMEM((8, 2048, 128), BF16),
            pltpu.VMEM((2, 2, SEQ, WIDTH), BF16),
            pltpu.VMEM((2 * ROWS, WIDTH), BF16),
            pltpu.VMEM((2 * ROWS, 768), F32),
            pltpu.VMEM((2 * ROWS, 2048), BF16),
            pltpu.VMEM((2 * ROWS, 2048), BF16),
            pltpu.VMEM((4, 2, SEQ, HEAD_WIDTH), BF16),
            pltpu.VMEM((2, 2 * ROWS, 16), BF16),
            pltpu.VMEM((2, SEQ), jnp.int32),
            pltpu.VMEM((2, 1, WIDTH), F32),
            pltpu.VMEM((2, 2, 16, 1024), BF16),
            pltpu.VMEM((2, 16, WIDTH), BF16),
            pltpu.VMEM((2, 2, 1, WIDTH // 2), F32),
            pltpu.VMEM((16, ROWS, 128), BF16),
            pltpu.VMEM((32, 2, ROWS, 128), BF16),
            pltpu.VMEM((2, SIDE, ROWS, 256), BF16),
            pltpu.VMEM((2, ROWS, 128), F32),
            pltpu.VMEM((2, 8, 128), F32),
            pltpu.VMEM((2, 3, 8, 128), F32),
            pltpu.VMEM((2, SEQ, 1024), BF16),
            pltpu.VMEM((2, 8, 16, 1024), BF16),
            pltpu.VMEM((2, 2, 16, 512), BF16),
            pltpu.VMEM((2, 2, 16, 512), BF16),
            pltpu.VMEM((2, MEMBERS, 2, 16, 512), BF16),
            dma((5, 2)),
            dma((5, 2, 7)),
            dma((2, 2)),
            dma((2, 2, 15)),
            dma((9,)),
            dma((2, 3, 8)),
            dma((2, 3, 8)),
            dma((16,)),
            dma((16,)),
            dma((3, 16)),
            dma((3, 16)),
            dma((24,)),
            dma((24,)),
            dma((2,)),
            dma((2,)),
        ],
        compiler_params=pltpu.CompilerParams(
            collective_id=0, has_side_effects=True, vmem_limit_bytes=58 * 1024 * 1024
        ),
        name="relay",
    )(
        hidden_input.reshape(2, SEQ, WIDTH),
        document_index[0],
        jnp.concatenate(
            [query_key_value_weight[0, :, :, 512:], query_key_value_weight[0, :, :, :512]], axis=-1
        ).reshape(256, 1536),
        output_weight[0],
        adapter_down[0, 0].T,
        adapter_up[0, 0],
        attention_gain[0],
        final_norm_gain,
        jnp.asarray(cosine),
        jnp.asarray(sine),
    )
    return averaged.reshape(1, 2, SEQ, WIDTH // 2)


def solution(mesh):
    return jax.shard_map(
        per_device,
        mesh=mesh,
        in_specs=(
            P("member", "section", None, None, None),
            P("section", None, None),
            P("section", "member", "tensor", None),
            P("section", "tensor", "member"),
            P("member", "section", "tensor", None),
            P("member", "section", None, None),
            P("member", "section", None),
            P("member", "tensor"),
        ),
        out_specs=P("section", None, None, "tensor"),
        check_vma=False,
    )
```

```python
import math

import jax
import jax.numpy as jnp
import numpy as np
from jax import lax
from jax.experimental import pallas as pl
from jax.experimental.pallas import tpu as pltpu
from jax.sharding import PartitionSpec as P

HEAD_WIDTH = 128
GROUP = 4
WIDTH = 4096
ROWS = 256
SEQ = 128
MEMBERS = 16
SIDE = 4
EPS = 1e-05
MESH = pl.DeviceIdType.MESH
F32 = jnp.float32
BF16 = jnp.bfloat16


def rope_tables():
    position = np.arange(SEQ, dtype=np.float32)
    frequency = np.exp(
        np.arange(HEAD_WIDTH // 2, dtype=np.float32)
        * np.float32(-2.0 * math.log(500000.0) / HEAD_WIDTH)
    ).astype(np.float32)
    angles = (position[:, None] * frequency[None, :]).astype(np.float32)
    cosine, sine = np.cos(angles), np.sin(angles)
    return (
        np.concatenate([cosine, cosine], axis=1).astype(np.float32),
        np.concatenate([-sine, sine], axis=1).astype(np.float32),
    )


def wrap(value):
    return lax.rem(value + 2 * SIDE, SIDE)


class Torus:
    def __init__(self):
        self.member = lax.axis_index("member")
        self.x = lax.rem(self.member, SIDE)
        self.y = self.member // SIDE

    def at(self, part, du, dv):
        dx, dy = (du, dv) if part == 0 else (dv, du)
        return wrap(self.y + dy) * SIDE + wrap(self.x + dx)


class Place(Torus):
    def __init__(self):
        super().__init__()
        self.kind = lax.rem((self.x + 1) // 2, 2)
        self.parity = lax.rem(self.x, 2)
        self.pair_x = self.x + 1 - 2 * self.parity
        self.pair = self.y * SIDE + self.pair_x
        self.index = self.y * 2 + self.x // 2

    def column(self, f):
        return self.x + f * (3 - 2 * self.x)

    def row(self, dy):
        return wrap(self.y + dy)

    def near(self, f, dy):
        return self.row(dy) * SIDE + self.column(f)

    def pair_near(self, f, dy):
        return self.row(dy) * SIDE + self.pair_x + f * (3 - 2 * self.pair_x)


class PairGather:
    def __init__(self, place, own, slot, whole, send_sem, recv_sem):
        self.place, self.own, self.slot, self.whole = place, own, slot, whole
        self.send_sem, self.recv_sem = send_sem, recv_sem

    def copy(self, src, dst, part, f, dy, index):
        return pltpu.make_async_remote_copy(
            src_ref=src,
            dst_ref=dst,
            send_sem=self.send_sem.at[part],
            recv_sem=self.recv_sem.at[part, index],
            device_id={"member": self.place.near(f, dy)},
            device_id_type=MESH,
        )

    def ref(self, part, f, dy, which=None):
        return self.slot(self.place.column(f), self.place.row(dy), part, which)

    def move(self, part, f, dy, which, to_f, to_dy, index):
        ref = self.ref(part, f, dy, which)
        self.copy(ref, ref, part, to_f, to_dy, index).start()

    def wait(self, part, f, dy, index):
        ref = self.ref(part, f, dy)
        self.copy(ref, ref, part, 1, 0, index).wait_recv()

    def begin(self):
        for part, targets in ((0, ((1, 0), (0, 1), (0, -1))), (1, ((0, 1), (0, -1), (1, 0)))):
            for index, (f, dy) in enumerate(targets):
                self.copy(self.own(part), self.ref(part, 0, 0), part, f, dy, index).start()

    def cross_near(self):
        self.wait(0, 1, 0, 0)
        self.move(0, 1, 0, None, 0, 1, 3)
        self.move(0, 1, 0, None, 0, -1, 4)

    def round_near(self):
        self.wait(1, 0, -1, 0)
        self.move(1, 0, -1, 0, 0, 1, 3)
        self.move(1, 0, -1, None, 1, 0, 4)
        self.wait(1, 0, 1, 1)
        self.move(1, 0, 1, 1, 0, -1, 3)
        self.move(1, 0, 1, None, 1, 0, 5)

    def own_far(self):
        self.wait(0, 0, -1, 1)
        self.move(0, 0, -1, 0, 0, 1, 5)
        self.wait(0, 0, 1, 2)
        self.move(0, 0, 1, 1, 0, -1, 5)

    def round_far(self):
        self.wait(1, 0, 2, 3)
        self.move(1, 0, 2, None, 1, 0, 6)

    def cross_far(self):
        self.wait(0, 1, -1, 3)
        self.move(0, 1, -1, 0, 0, 1, 6)
        self.wait(0, 1, 1, 4)
        self.move(0, 1, 1, 1, 0, -1, 6)

    def middle(self):
        self.cross_near()
        self.round_near()

    def late(self):
        self.own_far()
        self.round_far()
        self.cross_far()

    def end(self, stage):
        if stage == 0:
            self.wait(1, 1, 0, 2)
        elif stage == 1:
            self.wait(1, 1, -1, 4)
            self.wait(1, 1, 1, 5)
        elif stage == 2:
            self.wait(0, 0, 2, 5)
        else:
            self.wait(0, 1, 2, 6)
            self.wait(1, 1, 2, 6)

    def sent(self):
        for part in (0, 1):
            ref = self.whole(part)
            self.copy(ref, ref, part, 1, 0, 0).wait_send()


class PlaneGather:
    order = (0, -1, 1, 2)

    def __init__(self, torus, own, slot, whole, send_sem, recv_sem):
        self.torus, self.own, self.slot, self.whole = torus, own, slot, whole
        self.send_sem, self.recv_sem = send_sem, recv_sem

    def copy(self, src, dst, part, du, dv, index):
        return pltpu.make_async_remote_copy(
            src_ref=src,
            dst_ref=dst,
            send_sem=self.send_sem.at[part],
            recv_sem=self.recv_sem.at[part, index],
            device_id={"member": self.torus.at(part, du, dv)},
            device_id_type=MESH,
        )

    def ref(self, part, du, dv):
        return self.slot(part, self.torus.at(part, du, dv))

    def begin(self):
        for part in (0, 1):
            for k in (1, 2, 3):
                self.copy(self.own(part), self.ref(part, 0, 0), part, -self.order[k], 0, k - 1).start()
        for part in (0, 1):
            self.spread(part, 0)

    def spread(self, part, q):
        here = self.ref(part, self.order[q], 0)
        src = self.own(part) if q == 0 else here
        for k in (1, 2, 3):
            self.copy(src, here, part, 0, -self.order[k], 3 * q + k + 2).start()

    def wait(self, part, du, dv, index):
        ref = self.ref(part, du, dv)
        self.copy(ref, ref, part, 1, 0, index).wait_recv()

    def middle(self):
        for q in (1, 2, 3):
            for part in (0, 1):
                self.wait(part, self.order[q], 0, q - 1)
                self.spread(part, q)

    def end(self):
        for q in range(SIDE):
            for part in (0, 1):
                for k in (1, 2, 3):
                    self.wait(part, self.order[q], self.order[k], 3 * q + k + 2)

    def sent(self):
        for part in (0, 1):
            ref = self.whole(part)
            self.copy(ref, ref, part, 1, 0, 0).wait_send()


def rotate(values, cosine, sine):
    return (values * cosine + pltpu.roll(values, HEAD_WIDTH // 2, 1) * sine).astype(BF16)


QKV_SPLIT = (((0, 144), (0, 80), (80, 64)), ((144, 112), (144, 64), (208, 48)))
OUT_SPLIT = (((0, 1152), (0, 576), (576, 576)), ((1152, 896), (1152, 448), (1600, 448)))


def cut(split, part, which):
    return split[part][0 if which is None else which + 1]


BLOCKS = ((0, 0), (1, 0), (0, -1), (0, 1), (1, -1), (1, 1), (0, 2), (1, 2))


def kernel(
    hidden_in, docs_in, qkv_in, out_in, down_in, up_in, gain_in, final_in, cos_ref, sin_ref,
    out_ref,
    wq, wo, h_all, nrm, proj, ctx_one, ctx_two, low, docs_next, gain_all, down_all, up_all, final_all,
    h_send, h_next, h_last, square, stat_own, stat_in, rows_out, rows_in, mean_own, mean_in, fin,
    pg_send, pg_recv, ag_send, ag_recv, local_sem, ctx_s, ctx_r, hop_s, hop_r, fwd_s, fwd_r,
    misc_s, misc_r, scatter_s, scatter_r,
):
    place = Place()
    member, kind, parity, index8 = place.member, place.kind, place.parity, place.index
    section = lax.axis_index("section")
    tensor = lax.axis_index("tensor")
    other = 1 - tensor
    sections = 8
    after = lax.rem(section + 1, sections)
    before = lax.rem(section + sections - 1, sections)
    both = (0, 1)

    barrier = pltpu.get_barrier_semaphore()

    def signal(device):
        pl.semaphore_signal(barrier, inc=1, device_id=device, device_id_type=MESH)

    def greet(i, carry):
        signal({"member": lax.rem(member + i, MEMBERS)})
        return carry

    lax.fori_loop(1, MEMBERS, greet, 0)
    signal({"tensor": other})
    signal({"member": place.pair, "tensor": other})
    for near in (after, before):
        signal({"section": near})
        signal({"section": near, "tensor": other})

    pending = []

    def local(src, dst, index):
        copy = pltpu.make_async_copy(src, dst, local_sem.at[index])
        copy.start()
        return copy

    def misc(src, dst, index, device):
        copy = pltpu.make_async_remote_copy(
            src, dst, misc_s.at[index], misc_r.at[index], device, MESH
        )
        pending.append(copy)
        return copy

    load_h = local(hidden_in, h_all.at[:, parity], 0)
    loads = [
        local(gain_in, gain_all.at[parity], 1),
        local(down_in, down_all.at[parity, tensor], 2),
        local(up_in, up_all.at[parity], 3),
        local(final_in, final_all.at[parity, tensor], 4),
        local(
            qkv_in.at[:, pl.ds(pl.multiple_of(kind * 768, 256), 768)],
            wq.at[pl.ds(pl.multiple_of(member * 256, 256), 256)],
            5,
        ),
    ]
    load_o = local(
        out_in.at[:, pl.ds(pl.multiple_of(tensor * 128, 128), 128)],
        wo.at[index8, pl.ds(pl.multiple_of(tensor * 1024, 1024), 1024)],
        6,
    )
    pl.semaphore_wait(barrier, MEMBERS - 1 + 6)

    def qkv_slot(of_pair):
        def slot(x, y, part, which):
            if of_pair:
                x = x + 1 - 2 * lax.rem(x, 2)
            lower, size = cut(QKV_SPLIT, part, which)
            return wq.at[pl.ds(pl.multiple_of((y * SIDE + x) * 256 + lower, 16), size)]

        return slot

    def own_qkv(part):
        lower, size = cut(QKV_SPLIT, part, None)
        return qkv_in.at[pl.ds(lower, size), pl.ds(pl.multiple_of(kind * 768, 256), 768)]

    def whole_qkv(part):
        return wq.at[pl.ds(0, 7 * cut(QKV_SPLIT, part, None)[1])]

    def out_slot(x, y, part, which):
        lower, size = cut(OUT_SPLIT, part, which)
        return wo.at[y * 2 + x // 2, pl.ds(lower, size)]

    def whole_out(part):
        return wo.at[pl.ds(0, 7), pl.ds(0, cut(OUT_SPLIT, part, None)[1])]

    wave_one = PairGather(place, own_qkv, qkv_slot(False), whole_qkv, pg_send.at[0], pg_recv.at[0])
    pair_slot = qkv_slot(True)
    wave_two = PairGather(
        place,
        lambda part: pair_slot(place.x, place.y, part, None),
        pair_slot,
        whole_qkv,
        pg_send.at[1],
        pg_recv.at[1],
    )
    wave_out = PairGather(
        place,
        lambda part: out_slot(place.x, place.y, part, None),
        out_slot,
        whole_out,
        pg_send.at[2],
        pg_recv.at[2],
    )

    to_pair = {"member": place.pair}
    to_pair_other = {"member": place.pair, "tensor": other}
    to_other = {"tensor": other}

    rows_of = lambda m: wq.at[pl.ds(pl.multiple_of(m * 256, 256), 256)]
    seed = misc(
        qkv_in.at[:, pl.ds(pl.multiple_of((1 - kind) * 768, 256), 768)], rows_of(member), 0, to_pair
    )
    seed.start()
    wave_one.begin()
    half_of = lambda a, t: h_all.at[t, a]
    share_h = misc(
        hidden_in.at[tensor], half_of(parity, tensor), 1, to_pair
    )
    share_out = misc(
        out_in.at[:, pl.ds(pl.multiple_of(other * 128, 128), 128)],
        wo.at[index8, pl.ds(pl.multiple_of(tensor * 1024, 1024), 1024)],
        2,
        to_other,
    )
    share_out.start()
    small = [misc(gain_in, gain_all.at[parity], 3, to_pair), misc(up_in, up_all.at[parity], 4, to_pair)]
    for k, device in enumerate((to_other, to_pair, to_pair_other)):
        small.append(misc(down_in, down_all.at[parity, tensor], 5 + k, device))
        small.append(misc(final_in, final_all.at[parity, tensor], 8 + k, device))
    small.append(misc(docs_in, docs_next, 11, {"section": after}))
    load_h.wait()
    loads[0].wait()

    def norm_first(a):
        def block(i, carry):
            r, j = i // 8, lax.rem(i, 8)
            h = h_all[r, a, pl.ds(pl.multiple_of(j * 16, 16), 16), :].astype(F32)
            scale = lax.rsqrt(jnp.mean(h * h, axis=-1, keepdims=True) + EPS)
            nrm[pl.ds(pl.multiple_of(r * 256 + a * 128 + j * 16, 16), 16), :] = (
                h * scale * gain_all[a]
            ).astype(BF16)
            return carry

        lax.fori_loop(0, ROWS // 16, block, 0)

    norm_first(parity)

    def project(lower, upper):
        def block(n, carry):
            rows = pl.ds(pl.multiple_of(n // 3 * 256, 256), 256)
            columns = pl.ds(pl.multiple_of(lax.rem(n, 3) * 256, 256), 256)
            proj[rows, columns] = jnp.dot(nrm[rows, :], wq[:, columns], preferred_element_type=F32)
            return carry

        lax.fori_loop(lower, upper, block, 0)

    ahead = lax.broadcasted_iota(jnp.int32, (SEQ, SEQ), 0) >= lax.broadcasted_iota(
        jnp.int32, (SEQ, SEQ), 1
    )
    head = 2 * tensor + kind

    def ctx_copy(ctx, tick, s, which):
        owner = 2 * tensor + (1 - kind if which == 2 else kind)
        ref = ctx.at[
            pl.ds(pl.multiple_of(s * SEQ, SEQ), SEQ), pl.ds(pl.multiple_of(owner * 512, 512), 512)
        ]
        return pltpu.make_async_remote_copy(
            ref, ref, ctx_s.at[tick, which, s], ctx_r.at[tick, which, s],
            to_pair if which == 1 else to_other, MESH,
        )

    def ctx_arrived(ctx, tick, s, which):
        t = tensor if which == 1 else other
        owner = 2 * t + (kind if which == 0 else 1 - kind)
        ref = ctx.at[
            pl.ds(pl.multiple_of(s * SEQ, SEQ), SEQ), pl.ds(pl.multiple_of(owner * 512, 512), 512)
        ]
        pltpu.make_async_remote_copy(
            ref, ref, ctx_s.at[tick, which, s], ctx_r.at[tick, which, s], to_other, MESH
        ).wait_recv()

    def attend(docs_ref, ctx, tick, lower, upper):
        def sequence(s, carry):
            rows = pl.ds(pl.multiple_of(s * SEQ, SEQ), SEQ)
            numbers = docs_ref[pl.ds(s // 2, 1), :]
            numbers = jnp.broadcast_to(numbers, (SEQ, SEQ)).astype(F32)
            allowed = ahead & (numbers == numbers.T)
            allowed = jnp.concatenate([allowed.astype(F32)] * GROUP, axis=0) > 0.5
            cosine, sine = cos_ref[...], sin_ref[...]

            def piece(g):
                return proj[rows, g * 128 : g * 128 + 128]

            queries = jnp.concatenate(
                [rotate(piece(g), cosine, sine) for g in range(GROUP)], axis=0
            )
            keys = rotate(piece(GROUP), cosine, sine)
            values = piece(GROUP + 1).astype(BF16)
            scores = lax.dot_general(
                queries, keys, (((1,), (1,)), ((), ())), preferred_element_type=F32
            ) * (1.0 / math.sqrt(HEAD_WIDTH))
            scores = jnp.where(allowed, scores, -1e30)
            weights = jnp.exp(scores - jnp.max(scores, axis=-1, keepdims=True))
            weights = (weights / jnp.sum(weights, axis=-1, keepdims=True)).astype(BF16)
            context = jnp.dot(weights, values, preferred_element_type=F32).astype(BF16)
            for g in range(GROUP):
                columns = pl.ds(pl.multiple_of(head * 512 + g * 128, 128), 128)
                ctx[rows, columns] = context[g * SEQ : (g + 1) * SEQ]
            ctx_copy(ctx, tick, s, 1).start()
            ctx_copy(ctx, tick, s, 0).start()
            return carry

        lax.fori_loop(lower, upper, sequence, 0)

    def collect(ctx, tick, r):
        for a in both:
            ctx_arrived(ctx, tick, 2 * r + a, 1)
            ctx_copy(ctx, tick, 2 * r + a, 2).start()
        for a in both:
            ctx_arrived(ctx, tick, 2 * r + a, 0)
            ctx_arrived(ctx, tick, 2 * r + a, 2)
        for a in both:
            rows = slice((2 * r + a) * SEQ, (2 * r + a + 1) * SEQ)
            for block in both:
                low[block, rows] = lax.dot_general(
                    ctx[rows, block * 1024 : block * 1024 + 1024],
                    down_all[a, block],
                    (((1,), (1,)), ((), ())),
                    preferred_element_type=F32,
                ).astype(BF16)

    wave_one.middle()
    share_h.start()
    for copy in small:
        copy.start()
    seed_in = pltpu.make_async_remote_copy(
        rows_of(place.pair), rows_of(place.pair), misc_s.at[0], misc_r.at[0], to_pair, MESH
    )
    seed_in.wait_recv()
    wave_two.begin()
    wave_one.late()
    wave_two.middle()
    pltpu.make_async_remote_copy(
        half_of(1 - parity, tensor), half_of(1 - parity, tensor), misc_s.at[1], misc_r.at[1],
        to_pair, MESH,
    ).wait_recv()
    pass_h = misc(half_of(1 - parity, tensor), half_of(1 - parity, tensor), 12, to_other)
    pass_h.start()
    load_o.wait()
    share_in = wo.at[index8, pl.ds(pl.multiple_of(other * 1024, 1024), 1024)]
    pltpu.make_async_remote_copy(
        share_in, share_in, misc_s.at[2], misc_r.at[2], to_other, MESH
    ).wait_recv()
    wave_two.late()
    pltpu.make_async_remote_copy(
        half_of(1 - parity, other), half_of(1 - parity, other), misc_s.at[12], misc_r.at[12],
        to_other, MESH,
    ).wait_recv()
    small[0].wait_recv()
    norm_first(1 - parity)
    wave_out.begin()
    for copy in small[1:]:
        copy.wait_recv()
    for copy in loads[1:]:
        copy.wait()
    for stage in range(4):
        wave_one.end(stage)
        wave_two.end(stage)
    project(0, 3)
    attend(docs_in, ctx_one, 0, 0, 2)
    project(3, 6)
    attend(docs_in, ctx_one, 0, 2, 4)
    wave_out.cross_near()
    wave_out.own_far()
    wave_out.round_near()

    def block_member(i, pair=False):
        f, dy = BLOCKS[i]
        return place.pair_near(f, dy) if pair else place.near(f, dy)

    def columns_of(m):
        return pl.ds(pl.multiple_of(m * 256 + tensor * 128, 128), 128)

    def summed(ctx, r, weights_of, up_of):
        total = None
        rows = slice(r * 256, r * 256 + 256)
        for block in both:
            main = jnp.dot(
                ctx[rows, block * 1024 : block * 1024 + 1024],
                weights_of(block),
                preferred_element_type=F32,
            )
            extra = jnp.concatenate(
                [
                    jnp.dot(
                        low[block, (2 * r + a) * SEQ : (2 * r + a + 1) * SEQ],
                        up_of(a),
                        preferred_element_type=F32,
                    )
                    for a in both
                ],
                axis=0,
            )
            value = (main + extra).astype(BF16).astype(F32)
            total = value if total is None else total + value
        return total

    def block_copy(ref, dst, kind_of, n, device):
        send, recv = (hop_s.at[n], hop_r.at[n]) if kind_of == 3 else (
            fwd_s.at[kind_of, n], fwd_r.at[kind_of, n]
        )
        return pltpu.make_async_remote_copy(ref, dst, send, recv, device, MESH)

    steps = [(i, r) for lower in (0, 4) for r in both for i in range(lower, lower + 4)]

    def own_ref(n):
        i, r = steps[n]
        return h_next.at[block_member(i) * 2 + tensor, r]

    def hop_copy(n):
        return block_copy(h_send.at[n], own_ref(n), 3, n, {"section": after})

    def start_block(n):
        i, r = steps[n]
        f, dy = BLOCKS[i]
        slot = place.row(dy) * 2 + place.column(f) // 2
        columns = columns_of(block_member(i))
        total = summed(
            ctx_one, r, lambda block: wo[slot, block * 1024 : block * 1024 + 1024],
            lambda a: up_all[a, :, columns],
        )
        for a in both:
            rows = slice(a * SEQ, a * SEQ + SEQ)
            h_send[n, rows] = (h_all[r, a, :, columns].astype(F32) + total[rows]).astype(BF16)
        hop_copy(n).start()

    def pair_ref(n):
        i, r = steps[n]
        return h_next.at[block_member(i, True) * 2 + tensor, r]

    def pass_own(n, device, kind_of):
        return block_copy(own_ref(n), own_ref(n), kind_of, n, device)

    def pass_pair(n):
        return block_copy(pair_ref(n), pair_ref(n), 2, n, to_other)

    def arrive(n):
        hop_copy(n).wait_recv()
        pass_own(n, to_pair, 0).start()
        pass_own(n, to_other, 1).start()

    def relay(n):
        block_copy(pair_ref(n), pair_ref(n), 0, n, to_pair).wait_recv()
        pass_pair(n).start()

    def other_ref(n, pair):
        i, r = steps[n]
        return h_next.at[block_member(i, pair) * 2 + other, r]

    def run(lower, upper):
        for n in range(lower, upper):
            start_block(n)
            if n >= 4:
                arrive(n - 4)
            if n >= 7:
                relay(n - 7)

    collect(ctx_one, 0, 0)
    wave_out.end(0)
    run(0, 4)
    wave_out.cross_far()
    collect(ctx_one, 0, 1)
    wave_out.round_far()
    run(4, 8)
    wave_out.end(1)
    run(8, 10)
    wave_out.end(2)
    run(10, 11)
    wave_out.end(3)
    run(11, 16)
    for n in (9, 10, 11):
        relay(n)
        arrive(n + 3)

    def complete(r):
        for n in range(16):
            if steps[n][1] == r:
                ref = other_ref(n, False)
                block_copy(ref, ref, 1, n, to_other).wait_recv()
                ref = other_ref(n, True)
                block_copy(ref, ref, 2, n, to_other).wait_recv()

    def norm_second(i, carry):
        r, j = i // 8, lax.rem(i, 8)
        a = j // 4
        rows = pl.ds(pl.multiple_of(j * 32, 32), 32)
        total = jnp.zeros((32, 128), F32)
        for block in range(32):
            h = h_next[block, r, rows, :].astype(F32)
            total = total + h * h
        scale = lax.rsqrt(jnp.sum(total, axis=-1, keepdims=True) * (1.0 / WIDTH) + EPS)
        scale = jnp.broadcast_to(scale, (32, 128))
        for block in range(32):
            columns = slice(block * 128, block * 128 + 128)
            h = h_next[block, r, rows, :].astype(F32)
            nrm[pl.ds(pl.multiple_of(i * 32, 32), 32), columns] = (
                h * scale * gain_all[a, :, columns]
            ).astype(BF16)
        return carry

    complete(0)
    lax.fori_loop(0, 8, norm_second, 0)
    arrive(15)
    relay(12)
    relay(13)
    project(0, 3)
    relay(14)
    relay(15)
    attend(docs_next, ctx_two, 1, 0, 2)
    complete(1)
    lax.fori_loop(8, 16, norm_second, 0)
    project(3, 6)
    attend(docs_next, ctx_two, 1, 2, 4)

    def pair_members(y):
        return y * SIDE + kind, y * SIDE + 3 - kind

    def up_pair(a, y):
        return jnp.concatenate([up_all[a, :, columns_of(m)] for m in pair_members(y)], axis=1)

    def last_output(r):
        square[r] = jnp.zeros((ROWS, 128), F32)

        def last_block(y, carry):
            total = summed(
                ctx_two,
                r,
                lambda block: jnp.concatenate(
                    [wo[2 * y + k, block * 1024 : block * 1024 + 1024] for k in both], axis=1
                ),
                lambda a: up_pair(a, y),
            )
            for k, m in enumerate(pair_members(y)):
                columns = slice(k * 128, k * 128 + 128)
                h = h_next[m * 2 + tensor, r].astype(F32) + total[:, columns]
                h = h.astype(BF16)
                h_last[r, y, :, columns] = h
                h = h.astype(F32)
                square[r] += h * h
            return carry

        lax.fori_loop(0, SIDE, last_block, 0)

    def send_stats(r):
        stat_own[r] = jnp.zeros((8, 128), F32)
        for a in both:
            stat_own[r, a : a + 1, :] = jnp.sum(
                square[r, a * SEQ : a * SEQ + SEQ].T, axis=0, keepdims=True
            )
        stats = [
            misc(stat_own.at[r], stat_in.at[r, k], 13 + 3 * r + k, device)
            for k, device in enumerate((to_other, to_pair, to_pair_other))
        ]
        for copy in stats:
            copy.start()
        return stats

    def rows_at(r, i):
        return rows_out.at[r, pl.ds(pl.multiple_of(i * 16, 16), 16)]

    def scatter_rows(r, stats):
        for copy in stats:
            copy.wait_recv()
        total = stat_own[r] + stat_in[r, 0] + stat_in[r, 1] + stat_in[r, 2]
        scales = lax.rsqrt(total * (1.0 / WIDTH) + EPS)
        column_scale = [jnp.broadcast_to(scales[a : a + 1], (128, 128)).T for a in both]
        for y in range(SIDE):
            for k, m in enumerate(pair_members(y)):
                lower = (m - (y // 2) * 8) * 256 + tensor * 128
                gains = [
                    final_all[a, y // 2, :, pl.ds(pl.multiple_of(lower, 128), 128)] for a in both
                ]
                columns = slice(k * 128, k * 128 + 128)
                value = sum(
                    h_last[r, y, a * SEQ : a * SEQ + SEQ, columns].astype(F32)
                    * column_scale[a]
                    * gains[a]
                    for a in both
                )
                rows_out[r, :, (2 * y + k) * 128 : (2 * y + k + 1) * 128] = value.astype(BF16)

        def scatter(i, carry):
            f, dy = lax.rem(i, 2), i // 2
            x, y = place.column(f), place.row(dy)
            pltpu.make_async_remote_copy(
                rows_at(r, y * 2 + x // 2), rows_in.at[r, index8], scatter_s.at[r], scatter_r.at[r],
                {"member": y * SIDE + x}, MESH,
            ).start()
            return carry

        lax.fori_loop(1, 8, scatter, 0)
        return local(rows_at(r, index8), rows_in.at[r, index8], 7 + r)

    def seven(r):
        ref = rows_in.at[r, pl.ds(0, 7)]
        return pltpu.make_async_remote_copy(
            ref, ref, scatter_s.at[r], scatter_r.at[r], to_other, MESH
        )

    def average(r, keep):
        keep.wait()
        seven(r).wait_recv()
        total = rows_in[r, 0].astype(F32)
        for i in range(1, 8):
            total = total + rows_in[r, i].astype(F32)
        total = (total * (1.0 / MEMBERS)).astype(BF16)
        for half in both:
            mean_own[r, half] = total[:, half * 512 : half * 512 + 512]
        misc(mean_own.at[r, tensor], mean_in.at[r, tensor], 19 + 2 * r, {"section": after}).start()
        misc(
            mean_own.at[r, other], mean_in.at[r, tensor], 20 + 2 * r,
            {"section": after, "tensor": other},
        ).start()

    def hopped(r):
        for half, index in ((tensor, 19 + 2 * r), (other, 20 + 2 * r)):
            ref = mean_in.at[r, half]
            pltpu.make_async_remote_copy(
                ref, ref, misc_s.at[index], misc_r.at[index], to_other, MESH
            ).wait_recv()

    def gather_of(r):
        return PlaneGather(
            place,
            lambda part: mean_in.at[r, part],
            lambda part, slot: fin.at[r, slot, part],
            lambda part: fin.at[r, pl.ds(0, 15), part],
            ag_send.at[r],
            ag_recv.at[r],
        )

    collect(ctx_two, 1, 0)
    last_output(0)
    keep_zero = scatter_rows(0, send_stats(0))
    collect(ctx_two, 1, 1)
    last_output(1)
    stats_one = send_stats(1)
    average(0, keep_zero)
    keep_one = scatter_rows(1, stats_one)
    final_zero, final_one = gather_of(0), gather_of(1)
    hopped(0)
    final_zero.begin()
    fin[0, member] = mean_in[0]
    average(1, keep_one)
    final_zero.middle()
    hopped(1)
    final_one.begin()
    fin[1, member] = mean_in[1]
    final_zero.end()

    def place_rows(r):
        for m in range(MEMBERS):
            x, y = m % SIDE, m // SIDE
            side = ((x + 1) // 2) % 2
            lower = r * SEQ + (y * 2 + x // 2) * 16
            for part in both:
                for s in range(4):
                    column = (s // 2 * SIDE + (side if s % 2 == 0 else 3 - side)) * 256 + part * 128
                    out_ref[lower : lower + 16, column : column + 128] = fin[
                        r, m, part, :, s * 128 : s * 128 + 128
                    ]

    final_one.middle()
    place_rows(0)
    final_one.end()
    place_rows(1)

    for wave in (wave_one, wave_two, wave_out):
        wave.sent()
    final_zero.sent()
    final_one.sent()
    for tick, ctx in enumerate((ctx_one, ctx_two)):
        for which in range(3):
            for s in range(4):
                ctx_copy(ctx, tick, s, which).wait_send()
    for n in range(16):
        hop_copy(n).wait_send()
        pass_own(n, to_pair, 0).wait_send()
        pass_own(n, to_other, 1).wait_send()
        pass_pair(n).wait_send()
    for copy in pending:
        copy.wait_send()
    for r in both:
        seven(r).wait_send()


def per_device(
    hidden_input,
    document_index,
    query_key_value_weight,
    output_weight,
    adapter_down,
    adapter_up,
    attention_gain,
    final_norm_gain,
):
    cosine, sine = rope_tables()
    vmem = pl.BlockSpec(memory_space=pltpu.VMEM)
    anywhere = pl.BlockSpec(memory_space=pl.ANY)
    dma = pltpu.SemaphoreType.DMA
    averaged = pl.pallas_call(
        kernel,
        out_shape=jax.ShapeDtypeStruct((ROWS, WIDTH // 2), BF16),
        in_specs=[anywhere, vmem, anywhere, anywhere] + [vmem] * 6,
        out_specs=vmem,
        scratch_shapes=[
            pltpu.VMEM((WIDTH, 768), BF16),
            pltpu.VMEM((8, 2048, 128), BF16),
            pltpu.VMEM((2, 2, SEQ, WIDTH), BF16),
            pltpu.VMEM((2 * ROWS, WIDTH), BF16),
            pltpu.VMEM((2 * ROWS, 768), F32),
            pltpu.VMEM((2 * ROWS, 2048), BF16),
            pltpu.VMEM((2 * ROWS, 2048), BF16),
            pltpu.VMEM((2, 2 * ROWS, 16), BF16),
            pltpu.VMEM((2, SEQ), jnp.int32),
            pltpu.VMEM((2, 1, WIDTH), F32),
            pltpu.VMEM((2, 2, 16, 1024), BF16),
            pltpu.VMEM((2, 16, WIDTH), BF16),
            pltpu.VMEM((2, 2, 1, WIDTH // 2), F32),
            pltpu.VMEM((16, ROWS, 128), BF16),
            pltpu.VMEM((32, 2, ROWS, 128), BF16),
            pltpu.VMEM((2, SIDE, ROWS, 256), BF16),
            pltpu.VMEM((2, ROWS, 128), F32),
            pltpu.VMEM((2, 8, 128), F32),
            pltpu.VMEM((2, 3, 8, 128), F32),
            pltpu.VMEM((2, SEQ, 1024), BF16),
            pltpu.VMEM((2, 8, 16, 1024), BF16),
            pltpu.VMEM((2, 2, 16, 512), BF16),
            pltpu.VMEM((2, 2, 16, 512), BF16),
            pltpu.VMEM((2, MEMBERS, 2, 16, 512), BF16),
            dma((3, 2)),
            dma((3, 2, 7)),
            dma((2, 2)),
            dma((2, 2, 15)),
            dma((9,)),
            dma((2, 3, 4)),
            dma((2, 3, 4)),
            dma((16,)),
            dma((16,)),
            dma((3, 16)),
            dma((3, 16)),
            dma((23,)),
            dma((23,)),
            dma((2,)),
            dma((2,)),
        ],
        compiler_params=pltpu.CompilerParams(
            collective_id=0, has_side_effects=True, vmem_limit_bytes=58 * 1024 * 1024
        ),
        name="relay",
    )(
        hidden_input.reshape(2, SEQ, WIDTH),
        document_index[0],
        query_key_value_weight[0].reshape(256, 1536),
        output_weight[0],
        adapter_down[0, 0].T,
        adapter_up[0, 0],
        attention_gain[0],
        final_norm_gain,
        jnp.asarray(cosine),
        jnp.asarray(sine),
    )
    return averaged.reshape(1, 2, SEQ, WIDTH // 2)


def solution(mesh):
    return jax.shard_map(
        per_device,
        mesh=mesh,
        in_specs=(
            P("member", "section", None, None, None),
            P("section", None, None),
            P("section", "member", "tensor", None),
            P("section", "tensor", "member"),
            P("member", "section", "tensor", None),
            P("member", "section", None, None),
            P("member", "section", None),
            P("member", "tensor"),
        ),
        out_specs=P("section", None, None, "tensor"),
        check_vma=False,
    )
```

```python
import math

import jax
import jax.numpy as jnp
import numpy as np
from jax import lax
from jax.experimental import pallas as pl
from jax.experimental.pallas import tpu as pltpu
from jax.sharding import PartitionSpec as P

HEAD_WIDTH = 128
GROUP = 4
WIDTH = 4096
ROWS = 256
SEQ = 128
MEMBERS = 16
SIDE = 4
EPS = 1e-05
MESH = pl.DeviceIdType.MESH
F32 = jnp.float32
BF16 = jnp.bfloat16


def rope_tables():
    position = np.arange(SEQ, dtype=np.float32)
    frequency = np.exp(
        np.arange(HEAD_WIDTH // 2, dtype=np.float32)
        * np.float32(-2.0 * math.log(500000.0) / HEAD_WIDTH)
    ).astype(np.float32)
    angles = (position[:, None] * frequency[None, :]).astype(np.float32)
    cosine, sine = np.cos(angles), np.sin(angles)
    return (
        np.concatenate([cosine, cosine], axis=1).astype(np.float32),
        np.concatenate([-sine, sine], axis=1).astype(np.float32),
    )


def wrap(value):
    return lax.rem(value + 2 * SIDE, SIDE)


class Torus:
    def __init__(self):
        self.member = lax.axis_index("member")
        self.x = lax.rem(self.member, SIDE)
        self.y = self.member // SIDE

    def at(self, part, du, dv):
        dx, dy = (du, dv) if part == 0 else (dv, du)
        return wrap(self.y + dy) * SIDE + wrap(self.x + dx)


class Place(Torus):
    def __init__(self):
        super().__init__()
        self.kind = lax.rem((self.x + 1) // 2, 2)
        self.parity = lax.rem(self.x, 2)
        self.pair_x = self.x + 1 - 2 * self.parity
        self.pair = self.y * SIDE + self.pair_x
        self.index = self.y * 2 + self.x // 2

    def column(self, f):
        return self.x + f * (3 - 2 * self.x)

    def row(self, dy):
        return wrap(self.y + dy)

    def near(self, f, dy):
        return self.row(dy) * SIDE + self.column(f)

    def pair_near(self, f, dy):
        return self.row(dy) * SIDE + self.pair_x + f * (3 - 2 * self.pair_x)


class PairGather:
    def __init__(self, place, own, slot, whole, send_sem, recv_sem):
        self.place, self.own, self.slot, self.whole = place, own, slot, whole
        self.send_sem, self.recv_sem = send_sem, recv_sem

    def copy(self, src, dst, part, f, dy, index):
        return pltpu.make_async_remote_copy(
            src_ref=src,
            dst_ref=dst,
            send_sem=self.send_sem.at[part],
            recv_sem=self.recv_sem.at[part, index],
            device_id={"member": self.place.near(f, dy)},
            device_id_type=MESH,
        )

    def ref(self, part, f, dy, which=None):
        return self.slot(self.place.column(f), self.place.row(dy), part, which)

    def move(self, part, f, dy, which, to_f, to_dy, index):
        ref = self.ref(part, f, dy, which)
        self.copy(ref, ref, part, to_f, to_dy, index).start()

    def wait(self, part, f, dy, index):
        ref = self.ref(part, f, dy)
        self.copy(ref, ref, part, 1, 0, index).wait_recv()

    def begin(self):
        for part, targets in ((0, ((1, 0), (0, 1), (0, -1))), (1, ((0, 1), (0, -1), (1, 0)))):
            for index, (f, dy) in enumerate(targets):
                self.copy(self.own(part), self.ref(part, 0, 0), part, f, dy, index).start()

    def cross_near(self):
        self.wait(0, 1, 0, 0)
        self.move(0, 1, 0, None, 0, 1, 3)
        self.move(0, 1, 0, None, 0, -1, 4)

    def round_near(self):
        self.wait(1, 0, -1, 0)
        self.move(1, 0, -1, 0, 0, 1, 3)
        self.move(1, 0, -1, None, 1, 0, 4)
        self.wait(1, 0, 1, 1)
        self.move(1, 0, 1, 1, 0, -1, 3)
        self.move(1, 0, 1, None, 1, 0, 5)

    def own_far(self):
        self.wait(0, 0, -1, 1)
        self.move(0, 0, -1, 0, 0, 1, 5)
        self.wait(0, 0, 1, 2)
        self.move(0, 0, 1, 1, 0, -1, 5)

    def round_far(self):
        self.wait(1, 0, 2, 3)
        self.move(1, 0, 2, None, 1, 0, 6)

    def cross_far(self):
        self.wait(0, 1, -1, 3)
        self.move(0, 1, -1, 0, 0, 1, 6)
        self.wait(0, 1, 1, 4)
        self.move(0, 1, 1, 1, 0, -1, 6)

    def middle(self):
        self.cross_near()
        self.round_near()

    def late(self):
        self.own_far()
        self.round_far()
        self.cross_far()

    def end(self, stage):
        if stage == 0:
            self.wait(1, 1, 0, 2)
        elif stage == 1:
            self.wait(1, 1, -1, 4)
            self.wait(1, 1, 1, 5)
        elif stage == 2:
            self.wait(0, 0, 2, 5)
        else:
            self.wait(0, 1, 2, 6)
            self.wait(1, 1, 2, 6)

    def sent(self):
        for part in (0, 1):
            ref = self.whole(part)
            self.copy(ref, ref, part, 1, 0, 0).wait_send()


class PlaneGather:
    order = (0, -1, 1, 2)

    def __init__(self, torus, own, slot, whole, send_sem, recv_sem):
        self.torus, self.own, self.slot, self.whole = torus, own, slot, whole
        self.send_sem, self.recv_sem = send_sem, recv_sem

    def copy(self, src, dst, part, du, dv, index):
        return pltpu.make_async_remote_copy(
            src_ref=src,
            dst_ref=dst,
            send_sem=self.send_sem.at[part],
            recv_sem=self.recv_sem.at[part, index],
            device_id={"member": self.torus.at(part, du, dv)},
            device_id_type=MESH,
        )

    def ref(self, part, du, dv):
        return self.slot(part, self.torus.at(part, du, dv))

    def begin(self):
        for part in (0, 1):
            for k in (1, 2, 3):
                self.copy(self.own(part), self.ref(part, 0, 0), part, -self.order[k], 0, k - 1).start()
        for part in (0, 1):
            self.spread(part, 0)

    def spread(self, part, q):
        here = self.ref(part, self.order[q], 0)
        src = self.own(part) if q == 0 else here
        for k in (1, 2, 3):
            self.copy(src, here, part, 0, -self.order[k], 3 * q + k + 2).start()

    def wait(self, part, du, dv, index):
        ref = self.ref(part, du, dv)
        self.copy(ref, ref, part, 1, 0, index).wait_recv()

    def middle(self):
        for q in (1, 2, 3):
            for part in (0, 1):
                self.wait(part, self.order[q], 0, q - 1)
                self.spread(part, q)

    def end(self):
        for q in range(SIDE):
            for part in (0, 1):
                for k in (1, 2, 3):
                    self.wait(part, self.order[q], self.order[k], 3 * q + k + 2)

    def sent(self):
        for part in (0, 1):
            ref = self.whole(part)
            self.copy(ref, ref, part, 1, 0, 0).wait_send()


def rotate(values, cosine, sine):
    return (values * cosine + pltpu.roll(values, HEAD_WIDTH // 2, 1) * sine).astype(BF16)


QKV_SPLIT = (((0, 144), (0, 80), (80, 64)), ((144, 112), (144, 64), (208, 48)))
OUT_SPLIT = (((0, 1152), (0, 576), (576, 576)), ((1152, 896), (1152, 448), (1600, 448)))


def cut(split, part, which):
    return split[part][0 if which is None else which + 1]


BLOCKS = ((0, 0), (1, 0), (0, -1), (0, 1), (1, -1), (1, 1), (0, 2), (1, 2))


def kernel(
    hidden_in, docs_in, qkv_in, out_in, down_in, up_in, gain_in, final_in, cos_ref, sin_ref,
    out_ref,
    wq, wo, h_all, nrm, proj, ctx_one, ctx_two, low, docs_next, gain_all, down_all, up_all, final_all,
    h_send, h_next, h_last, square, stat_own, stat_in, rows_out, rows_in, mean_own, mean_in, fin,
    pg_send, pg_recv, ag_send, ag_recv, local_sem, ctx_s, ctx_r, hop_s, hop_r, fwd_s, fwd_r,
    misc_s, misc_r, scatter_s, scatter_r,
):
    place = Place()
    member, kind, parity, index8 = place.member, place.kind, place.parity, place.index
    section = lax.axis_index("section")
    tensor = lax.axis_index("tensor")
    other = 1 - tensor
    sections = 8
    after = lax.rem(section + 1, sections)
    before = lax.rem(section + sections - 1, sections)
    both = (0, 1)

    barrier = pltpu.get_barrier_semaphore()

    def signal(device):
        pl.semaphore_signal(barrier, inc=1, device_id=device, device_id_type=MESH)

    def greet(i, carry):
        signal({"member": lax.rem(member + i, MEMBERS)})
        return carry

    lax.fori_loop(1, MEMBERS, greet, 0)
    signal({"tensor": other})
    signal({"member": place.pair, "tensor": other})
    for near in (after, before):
        signal({"section": near})
        signal({"section": near, "tensor": other})

    pending = []

    def local(src, dst, index):
        copy = pltpu.make_async_copy(src, dst, local_sem.at[index])
        copy.start()
        return copy

    def misc(src, dst, index, device):
        copy = pltpu.make_async_remote_copy(
            src, dst, misc_s.at[index], misc_r.at[index], device, MESH
        )
        pending.append(copy)
        return copy

    load_h = local(hidden_in, h_all.at[:, parity], 0)
    loads = [
        local(gain_in, gain_all.at[parity], 1),
        local(down_in, down_all.at[parity, tensor], 2),
        local(up_in, up_all.at[parity], 3),
        local(final_in, final_all.at[parity, tensor], 4),
        local(
            qkv_in.at[:, pl.ds(pl.multiple_of(kind * 768, 256), 768)],
            wq.at[pl.ds(pl.multiple_of(member * 256, 256), 256)],
            5,
        ),
    ]
    load_o = local(
        out_in.at[:, pl.ds(pl.multiple_of(tensor * 128, 128), 128)],
        wo.at[index8, pl.ds(pl.multiple_of(tensor * 1024, 1024), 1024)],
        6,
    )
    pl.semaphore_wait(barrier, MEMBERS - 1 + 6)

    def qkv_slot(of_pair):
        def slot(x, y, part, which):
            if of_pair:
                x = x + 1 - 2 * lax.rem(x, 2)
            lower, size = cut(QKV_SPLIT, part, which)
            return wq.at[pl.ds(pl.multiple_of((y * SIDE + x) * 256 + lower, 16), size)]

        return slot

    def own_qkv(part):
        lower, size = cut(QKV_SPLIT, part, None)
        return qkv_in.at[pl.ds(lower, size), pl.ds(pl.multiple_of(kind * 768, 256), 768)]

    def whole_qkv(part):
        return wq.at[pl.ds(0, 7 * cut(QKV_SPLIT, part, None)[1])]

    def out_slot(x, y, part, which):
        lower, size = cut(OUT_SPLIT, part, which)
        return wo.at[y * 2 + x // 2, pl.ds(lower, size)]

    def whole_out(part):
        return wo.at[pl.ds(0, 7), pl.ds(0, cut(OUT_SPLIT, part, None)[1])]

    wave_one = PairGather(place, own_qkv, qkv_slot(False), whole_qkv, pg_send.at[0], pg_recv.at[0])
    pair_slot = qkv_slot(True)
    wave_two = PairGather(
        place,
        lambda part: pair_slot(place.x, place.y, part, None),
        pair_slot,
        whole_qkv,
        pg_send.at[1],
        pg_recv.at[1],
    )
    wave_out = PairGather(
        place,
        lambda part: out_slot(place.x, place.y, part, None),
        out_slot,
        whole_out,
        pg_send.at[2],
        pg_recv.at[2],
    )

    to_pair = {"member": place.pair}
    to_pair_other = {"member": place.pair, "tensor": other}
    to_other = {"tensor": other}

    rows_of = lambda m: wq.at[pl.ds(pl.multiple_of(m * 256, 256), 256)]
    seed = misc(
        qkv_in.at[:, pl.ds(pl.multiple_of((1 - kind) * 768, 256), 768)], rows_of(member), 0, to_pair
    )
    seed.start()
    wave_one.begin()
    half_of = lambda a, t: h_all.at[t, a]
    share_h = misc(
        hidden_in.at[tensor], half_of(parity, tensor), 1, to_pair
    )
    share_out = misc(
        out_in.at[:, pl.ds(pl.multiple_of(other * 128, 128), 128)],
        wo.at[index8, pl.ds(pl.multiple_of(tensor * 1024, 1024), 1024)],
        2,
        to_other,
    )
    share_out.start()
    small = [misc(gain_in, gain_all.at[parity], 3, to_pair), misc(up_in, up_all.at[parity], 4, to_pair)]
    for k, device in enumerate((to_other, to_pair, to_pair_other)):
        small.append(misc(down_in, down_all.at[parity, tensor], 5 + k, device))
        small.append(misc(final_in, final_all.at[parity, tensor], 8 + k, device))
    small.append(misc(docs_in, docs_next, 11, {"section": after}))
    load_h.wait()
    loads[0].wait()

    def norm_first(a):
        def block(i, carry):
            r, j = i // 8, lax.rem(i, 8)
            h = h_all[r, a, pl.ds(pl.multiple_of(j * 16, 16), 16), :].astype(F32)
            scale = lax.rsqrt(jnp.mean(h * h, axis=-1, keepdims=True) + EPS)
            nrm[pl.ds(pl.multiple_of(r * 256 + a * 128 + j * 16, 16), 16), :] = (
                h * scale * gain_all[a]
            ).astype(BF16)
            return carry

        lax.fori_loop(0, ROWS // 16, block, 0)

    norm_first(parity)

    def project(lower, upper):
        def block(n, carry):
            rows = pl.ds(pl.multiple_of(n // 3 * 256, 256), 256)
            columns = pl.ds(pl.multiple_of(lax.rem(n, 3) * 256, 256), 256)
            proj[rows, columns] = jnp.dot(nrm[rows, :], wq[:, columns], preferred_element_type=F32)
            return carry

        lax.fori_loop(lower, upper, block, 0)

    ahead = lax.broadcasted_iota(jnp.int32, (SEQ, SEQ), 0) >= lax.broadcasted_iota(
        jnp.int32, (SEQ, SEQ), 1
    )
    head = 2 * tensor + kind

    def ctx_copy(ctx, tick, s, which):
        owner = 2 * tensor + (1 - kind if which == 2 else kind)
        ref = ctx.at[
            pl.ds(pl.multiple_of(s * SEQ, SEQ), SEQ), pl.ds(pl.multiple_of(owner * 512, 512), 512)
        ]
        return pltpu.make_async_remote_copy(
            ref, ref, ctx_s.at[tick, which, s], ctx_r.at[tick, which, s],
            to_pair if which == 1 else to_other, MESH,
        )

    def ctx_arrived(ctx, tick, s, which):
        t = tensor if which == 1 else other
        owner = 2 * t + (kind if which == 0 else 1 - kind)
        ref = ctx.at[
            pl.ds(pl.multiple_of(s * SEQ, SEQ), SEQ), pl.ds(pl.multiple_of(owner * 512, 512), 512)
        ]
        pltpu.make_async_remote_copy(
            ref, ref, ctx_s.at[tick, which, s], ctx_r.at[tick, which, s], to_other, MESH
        ).wait_recv()

    def attend(docs_ref, ctx, tick, lower, upper):
        def sequence(s, carry):
            rows = pl.ds(pl.multiple_of(s * SEQ, SEQ), SEQ)
            numbers = docs_ref[pl.ds(s // 2, 1), :]
            numbers = jnp.broadcast_to(numbers, (SEQ, SEQ)).astype(F32)
            allowed = ahead & (numbers == numbers.T)
            allowed = jnp.concatenate([allowed.astype(F32)] * GROUP, axis=0) > 0.5
            cosine, sine = cos_ref[...], sin_ref[...]

            def piece(g):
                return proj[rows, g * 128 : g * 128 + 128]

            queries = jnp.concatenate(
                [rotate(piece(g), cosine, sine) for g in range(GROUP)], axis=0
            )
            keys = rotate(piece(GROUP), cosine, sine)
            values = piece(GROUP + 1).astype(BF16)
            scores = lax.dot_general(
                queries, keys, (((1,), (1,)), ((), ())), preferred_element_type=F32
            ) * (1.0 / math.sqrt(HEAD_WIDTH))
            scores = jnp.where(allowed, scores, -1e30)
            weights = jnp.exp(scores - jnp.max(scores, axis=-1, keepdims=True))
            weights = (weights / jnp.sum(weights, axis=-1, keepdims=True)).astype(BF16)
            context = jnp.dot(weights, values, preferred_element_type=F32).astype(BF16)
            for g in range(GROUP):
                columns = pl.ds(pl.multiple_of(head * 512 + g * 128, 128), 128)
                ctx[rows, columns] = context[g * SEQ : (g + 1) * SEQ]
            ctx_copy(ctx, tick, s, 1).start()
            ctx_copy(ctx, tick, s, 0).start()
            return carry

        lax.fori_loop(lower, upper, sequence, 0)

    def collect(ctx, tick, r):
        for a in both:
            ctx_arrived(ctx, tick, 2 * r + a, 1)
            ctx_copy(ctx, tick, 2 * r + a, 2).start()
        for a in both:
            ctx_arrived(ctx, tick, 2 * r + a, 0)
            ctx_arrived(ctx, tick, 2 * r + a, 2)
        for a in both:
            rows = slice((2 * r + a) * SEQ, (2 * r + a + 1) * SEQ)
            for block in both:
                low[block, rows] = lax.dot_general(
                    ctx[rows, block * 1024 : block * 1024 + 1024],
                    down_all[a, block],
                    (((1,), (1,)), ((), ())),
                    preferred_element_type=F32,
                ).astype(BF16)

    wave_one.middle()
    share_h.start()
    for copy in small:
        copy.start()
    seed_in = pltpu.make_async_remote_copy(
        rows_of(place.pair), rows_of(place.pair), misc_s.at[0], misc_r.at[0], to_pair, MESH
    )
    seed_in.wait_recv()
    wave_two.begin()
    wave_one.late()
    wave_two.middle()
    pltpu.make_async_remote_copy(
        half_of(1 - parity, tensor), half_of(1 - parity, tensor), misc_s.at[1], misc_r.at[1],
        to_pair, MESH,
    ).wait_recv()
    pass_h = misc(half_of(1 - parity, tensor), half_of(1 - parity, tensor), 12, to_other)
    pass_h.start()
    load_o.wait()
    share_in = wo.at[index8, pl.ds(pl.multiple_of(other * 1024, 1024), 1024)]
    pltpu.make_async_remote_copy(
        share_in, share_in, misc_s.at[2], misc_r.at[2], to_other, MESH
    ).wait_recv()
    wave_two.late()
    pltpu.make_async_remote_copy(
        half_of(1 - parity, other), half_of(1 - parity, other), misc_s.at[12], misc_r.at[12],
        to_other, MESH,
    ).wait_recv()
    small[0].wait_recv()
    norm_first(1 - parity)
    wave_out.begin()
    for copy in small[1:]:
        copy.wait_recv()
    for copy in loads[1:]:
        copy.wait()
    for stage in range(4):
        wave_one.end(stage)
        wave_two.end(stage)
    project(0, 3)
    attend(docs_in, ctx_one, 0, 0, 2)
    project(3, 6)
    attend(docs_in, ctx_one, 0, 2, 4)
    wave_out.cross_near()
    wave_out.own_far()
    wave_out.round_near()

    def block_member(i, pair=False):
        f, dy = BLOCKS[i]
        return place.pair_near(f, dy) if pair else place.near(f, dy)

    def columns_of(m):
        return pl.ds(pl.multiple_of(m * 256 + tensor * 128, 128), 128)

    def summed(ctx, r, weights_of, up_of):
        total = None
        rows = slice(r * 256, r * 256 + 256)
        for block in both:
            main = jnp.dot(
                ctx[rows, block * 1024 : block * 1024 + 1024],
                weights_of(block),
                preferred_element_type=F32,
            )
            extra = jnp.concatenate(
                [
                    jnp.dot(
                        low[block, (2 * r + a) * SEQ : (2 * r + a + 1) * SEQ],
                        up_of(a),
                        preferred_element_type=F32,
                    )
                    for a in both
                ],
                axis=0,
            )
            value = (main + extra).astype(BF16).astype(F32)
            total = value if total is None else total + value
        return total

    def block_copy(ref, dst, kind_of, n, device):
        send, recv = (hop_s.at[n], hop_r.at[n]) if kind_of == 3 else (
            fwd_s.at[kind_of, n], fwd_r.at[kind_of, n]
        )
        return pltpu.make_async_remote_copy(ref, dst, send, recv, device, MESH)

    steps = [(i, r) for lower in (0, 4) for r in both for i in range(lower, lower + 4)]

    def own_ref(n):
        i, r = steps[n]
        return h_next.at[block_member(i) * 2 + tensor, r]

    def hop_copy(n):
        return block_copy(h_send.at[n], own_ref(n), 3, n, {"section": after})

    def start_block(n):
        i, r = steps[n]
        f, dy = BLOCKS[i]
        slot = place.row(dy) * 2 + place.column(f) // 2
        columns = columns_of(block_member(i))
        total = summed(
            ctx_one, r, lambda block: wo[slot, block * 1024 : block * 1024 + 1024],
            lambda a: up_all[a, :, columns],
        )
        for a in both:
            rows = slice(a * SEQ, a * SEQ + SEQ)
            h_send[n, rows] = (h_all[r, a, :, columns].astype(F32) + total[rows]).astype(BF16)
        hop_copy(n).start()

    def pair_ref(n):
        i, r = steps[n]
        return h_next.at[block_member(i, True) * 2 + tensor, r]

    def pass_own(n, device, kind_of):
        return block_copy(own_ref(n), own_ref(n), kind_of, n, device)

    def pass_pair(n):
        return block_copy(pair_ref(n), pair_ref(n), 2, n, to_other)

    def arrive(n):
        hop_copy(n).wait_recv()
        pass_own(n, to_pair, 0).start()
        pass_own(n, to_other, 1).start()

    def relay(n):
        block_copy(pair_ref(n), pair_ref(n), 0, n, to_pair).wait_recv()
        pass_pair(n).start()

    def other_ref(n, pair):
        i, r = steps[n]
        return h_next.at[block_member(i, pair) * 2 + other, r]

    def run(lower, upper):
        for n in range(lower, upper):
            start_block(n)
            if n >= 3:
                arrive(n - 3)
            if n >= 5:
                relay(n - 5)

    collect(ctx_one, 0, 0)
    wave_out.end(0)
    run(0, 4)
    wave_out.cross_far()
    collect(ctx_one, 0, 1)
    wave_out.round_far()
    run(4, 8)
    wave_out.end(1)
    run(8, 10)
    wave_out.end(2)
    run(10, 11)
    wave_out.end(3)
    run(11, 16)
    relay(11)
    arrive(13)
    arrive(14)

    def complete(r):
        for n in range(16):
            if steps[n][1] == r:
                ref = other_ref(n, False)
                block_copy(ref, ref, 1, n, to_other).wait_recv()
                ref = other_ref(n, True)
                block_copy(ref, ref, 2, n, to_other).wait_recv()

    def norm_second(i, carry):
        r, j = i // 8, lax.rem(i, 8)
        a = j // 4
        rows = pl.ds(pl.multiple_of(j * 32, 32), 32)
        total = jnp.zeros((32, 128), F32)
        for block in range(32):
            h = h_next[block, r, rows, :].astype(F32)
            total = total + h * h
        scale = lax.rsqrt(jnp.sum(total, axis=-1, keepdims=True) * (1.0 / WIDTH) + EPS)
        scale = jnp.broadcast_to(scale, (32, 128))
        for block in range(32):
            columns = slice(block * 128, block * 128 + 128)
            h = h_next[block, r, rows, :].astype(F32)
            nrm[pl.ds(pl.multiple_of(i * 32, 32), 32), columns] = (
                h * scale * gain_all[a, :, columns]
            ).astype(BF16)
        return carry

    complete(0)
    lax.fori_loop(0, 8, norm_second, 0)
    arrive(15)
    relay(12)
    relay(13)
    project(0, 3)
    relay(14)
    relay(15)
    attend(docs_next, ctx_two, 1, 0, 2)
    complete(1)
    lax.fori_loop(8, 16, norm_second, 0)
    project(3, 6)
    attend(docs_next, ctx_two, 1, 2, 4)

    def pair_members(y):
        return y * SIDE + kind, y * SIDE + 3 - kind

    def up_pair(a, y):
        return jnp.concatenate([up_all[a, :, columns_of(m)] for m in pair_members(y)], axis=1)

    def last_output(r):
        square[r] = jnp.zeros((ROWS, 128), F32)

        def last_block(y, carry):
            total = summed(
                ctx_two,
                r,
                lambda block: jnp.concatenate(
                    [wo[2 * y + k, block * 1024 : block * 1024 + 1024] for k in both], axis=1
                ),
                lambda a: up_pair(a, y),
            )
            for k, m in enumerate(pair_members(y)):
                columns = slice(k * 128, k * 128 + 128)
                h = h_next[m * 2 + tensor, r].astype(F32) + total[:, columns]
                h = h.astype(BF16)
                h_last[r, y, :, columns] = h
                h = h.astype(F32)
                square[r] += h * h
            return carry

        lax.fori_loop(0, SIDE, last_block, 0)

    def send_stats(r):
        stat_own[r] = jnp.zeros((8, 128), F32)
        for a in both:
            stat_own[r, a : a + 1, :] = jnp.sum(
                square[r, a * SEQ : a * SEQ + SEQ].T, axis=0, keepdims=True
            )
        stats = [
            misc(stat_own.at[r], stat_in.at[r, k], 13 + 3 * r + k, device)
            for k, device in enumerate((to_other, to_pair, to_pair_other))
        ]
        for copy in stats:
            copy.start()
        return stats

    def rows_at(r, i):
        return rows_out.at[r, pl.ds(pl.multiple_of(i * 16, 16), 16)]

    def scatter_rows(r, stats):
        for copy in stats:
            copy.wait_recv()
        total = stat_own[r] + stat_in[r, 0] + stat_in[r, 1] + stat_in[r, 2]
        scales = lax.rsqrt(total * (1.0 / WIDTH) + EPS)
        column_scale = [jnp.broadcast_to(scales[a : a + 1], (128, 128)).T for a in both]
        for y in range(SIDE):
            for k, m in enumerate(pair_members(y)):
                lower = (m - (y // 2) * 8) * 256 + tensor * 128
                gains = [
                    final_all[a, y // 2, :, pl.ds(pl.multiple_of(lower, 128), 128)] for a in both
                ]
                columns = slice(k * 128, k * 128 + 128)
                value = sum(
                    h_last[r, y, a * SEQ : a * SEQ + SEQ, columns].astype(F32)
                    * column_scale[a]
                    * gains[a]
                    for a in both
                )
                rows_out[r, :, (2 * y + k) * 128 : (2 * y + k + 1) * 128] = value.astype(BF16)

        def scatter(i, carry):
            f, dy = lax.rem(i, 2), i // 2
            x, y = place.column(f), place.row(dy)
            pltpu.make_async_remote_copy(
                rows_at(r, y * 2 + x // 2), rows_in.at[r, index8], scatter_s.at[r], scatter_r.at[r],
                {"member": y * SIDE + x}, MESH,
            ).start()
            return carry

        lax.fori_loop(1, 8, scatter, 0)
        return local(rows_at(r, index8), rows_in.at[r, index8], 7 + r)

    def seven(r):
        ref = rows_in.at[r, pl.ds(0, 7)]
        return pltpu.make_async_remote_copy(
            ref, ref, scatter_s.at[r], scatter_r.at[r], to_other, MESH
        )

    def average(r, keep):
        keep.wait()
        seven(r).wait_recv()
        total = rows_in[r, 0].astype(F32)
        for i in range(1, 8):
            total = total + rows_in[r, i].astype(F32)
        total = (total * (1.0 / MEMBERS)).astype(BF16)
        for half in both:
            mean_own[r, half] = total[:, half * 512 : half * 512 + 512]
        misc(mean_own.at[r, tensor], mean_in.at[r, tensor], 19 + 2 * r, {"section": after}).start()
        misc(
            mean_own.at[r, other], mean_in.at[r, tensor], 20 + 2 * r,
            {"section": after, "tensor": other},
        ).start()

    def hopped(r):
        for half, index in ((tensor, 19 + 2 * r), (other, 20 + 2 * r)):
            ref = mean_in.at[r, half]
            pltpu.make_async_remote_copy(
                ref, ref, misc_s.at[index], misc_r.at[index], to_other, MESH
            ).wait_recv()

    def gather_of(r):
        return PlaneGather(
            place,
            lambda part: mean_in.at[r, part],
            lambda part, slot: fin.at[r, slot, part],
            lambda part: fin.at[r, pl.ds(0, 15), part],
            ag_send.at[r],
            ag_recv.at[r],
        )

    collect(ctx_two, 1, 0)
    last_output(0)
    keep_zero = scatter_rows(0, send_stats(0))
    collect(ctx_two, 1, 1)
    last_output(1)
    stats_one = send_stats(1)
    average(0, keep_zero)
    keep_one = scatter_rows(1, stats_one)
    final_zero, final_one = gather_of(0), gather_of(1)
    hopped(0)
    final_zero.begin()
    fin[0, member] = mean_in[0]
    average(1, keep_one)
    final_zero.middle()
    hopped(1)
    final_one.begin()
    fin[1, member] = mean_in[1]
    final_zero.end()

    def place_rows(r):
        for m in range(MEMBERS):
            x, y = m % SIDE, m // SIDE
            side = ((x + 1) // 2) % 2
            lower = r * SEQ + (y * 2 + x // 2) * 16
            for part in both:
                for s in range(4):
                    column = (s // 2 * SIDE + (side if s % 2 == 0 else 3 - side)) * 256 + part * 128
                    out_ref[lower : lower + 16, column : column + 128] = fin[
                        r, m, part, :, s * 128 : s * 128 + 128
                    ]

    final_one.middle()
    place_rows(0)
    final_one.end()
    place_rows(1)

    for wave in (wave_one, wave_two, wave_out):
        wave.sent()
    final_zero.sent()
    final_one.sent()
    for tick, ctx in enumerate((ctx_one, ctx_two)):
        for which in range(3):
            for s in range(4):
                ctx_copy(ctx, tick, s, which).wait_send()
    for n in range(16):
        hop_copy(n).wait_send()
        pass_own(n, to_pair, 0).wait_send()
        pass_own(n, to_other, 1).wait_send()
        pass_pair(n).wait_send()
    for copy in pending:
        copy.wait_send()
    for r in both:
        seven(r).wait_send()


def per_device(
    hidden_input,
    document_index,
    query_key_value_weight,
    output_weight,
    adapter_down,
    adapter_up,
    attention_gain,
    final_norm_gain,
):
    cosine, sine = rope_tables()
    vmem = pl.BlockSpec(memory_space=pltpu.VMEM)
    anywhere = pl.BlockSpec(memory_space=pl.ANY)
    dma = pltpu.SemaphoreType.DMA
    averaged = pl.pallas_call(
        kernel,
        out_shape=jax.ShapeDtypeStruct((ROWS, WIDTH // 2), BF16),
        in_specs=[anywhere, vmem, anywhere, anywhere] + [vmem] * 6,
        out_specs=vmem,
        scratch_shapes=[
            pltpu.VMEM((WIDTH, 768), BF16),
            pltpu.VMEM((8, 2048, 128), BF16),
            pltpu.VMEM((2, 2, SEQ, WIDTH), BF16),
            pltpu.VMEM((2 * ROWS, WIDTH), BF16),
            pltpu.VMEM((2 * ROWS, 768), F32),
            pltpu.VMEM((2 * ROWS, 2048), BF16),
            pltpu.VMEM((2 * ROWS, 2048), BF16),
            pltpu.VMEM((2, 2 * ROWS, 16), BF16),
            pltpu.VMEM((2, SEQ), jnp.int32),
            pltpu.VMEM((2, 1, WIDTH), F32),
            pltpu.VMEM((2, 2, 16, 1024), BF16),
            pltpu.VMEM((2, 16, WIDTH), BF16),
            pltpu.VMEM((2, 2, 1, WIDTH // 2), F32),
            pltpu.VMEM((16, ROWS, 128), BF16),
            pltpu.VMEM((32, 2, ROWS, 128), BF16),
            pltpu.VMEM((2, SIDE, ROWS, 256), BF16),
            pltpu.VMEM((2, ROWS, 128), F32),
            pltpu.VMEM((2, 8, 128), F32),
            pltpu.VMEM((2, 3, 8, 128), F32),
            pltpu.VMEM((2, SEQ, 1024), BF16),
            pltpu.VMEM((2, 8, 16, 1024), BF16),
            pltpu.VMEM((2, 2, 16, 512), BF16),
            pltpu.VMEM((2, 2, 16, 512), BF16),
            pltpu.VMEM((2, MEMBERS, 2, 16, 512), BF16),
            dma((3, 2)),
            dma((3, 2, 7)),
            dma((2, 2)),
            dma((2, 2, 15)),
            dma((9,)),
            dma((2, 3, 4)),
            dma((2, 3, 4)),
            dma((16,)),
            dma((16,)),
            dma((3, 16)),
            dma((3, 16)),
            dma((23,)),
            dma((23,)),
            dma((2,)),
            dma((2,)),
        ],
        compiler_params=pltpu.CompilerParams(
            collective_id=0, has_side_effects=True, vmem_limit_bytes=58 * 1024 * 1024
        ),
        name="relay",
    )(
        hidden_input.reshape(2, SEQ, WIDTH),
        document_index[0],
        query_key_value_weight[0].reshape(256, 1536),
        output_weight[0],
        adapter_down[0, 0].T,
        adapter_up[0, 0],
        attention_gain[0],
        final_norm_gain,
        jnp.asarray(cosine),
        jnp.asarray(sine),
    )
    return averaged.reshape(1, 2, SEQ, WIDTH // 2)


def solution(mesh):
    return jax.shard_map(
        per_device,
        mesh=mesh,
        in_specs=(
            P("member", "section", None, None, None),
            P("section", None, None),
            P("section", "member", "tensor", None),
            P("section", "tensor", "member"),
            P("member", "section", "tensor", None),
            P("member", "section", None, None),
            P("member", "section", None),
            P("member", "tensor"),
        ),
        out_specs=P("section", None, None, "tensor"),
        check_vma=False,
    )
```

```python
import math

import jax
import jax.numpy as jnp
import numpy as np
from jax import lax
from jax.experimental import pallas as pl
from jax.experimental.pallas import tpu as pltpu
from jax.sharding import PartitionSpec as P

HEAD_WIDTH = 128
GROUP = 4
WIDTH = 4096
ROWS = 256
SEQ = 128
MEMBERS = 16
SIDE = 4
EPS = 1e-05
MESH = pl.DeviceIdType.MESH
F32 = jnp.float32
BF16 = jnp.bfloat16


def rope_tables():
    position = np.arange(SEQ, dtype=np.float32)
    frequency = np.exp(
        np.arange(HEAD_WIDTH // 2, dtype=np.float32)
        * np.float32(-2.0 * math.log(500000.0) / HEAD_WIDTH)
    ).astype(np.float32)
    angles = (position[:, None] * frequency[None, :]).astype(np.float32)
    cosine, sine = np.cos(angles), np.sin(angles)
    return (
        np.concatenate([cosine, cosine], axis=1).astype(np.float32),
        np.concatenate([-sine, sine], axis=1).astype(np.float32),
    )


def wrap(value):
    return lax.rem(value + 2 * SIDE, SIDE)


class Torus:
    def __init__(self):
        self.member = lax.axis_index("member")
        self.x = lax.rem(self.member, SIDE)
        self.y = self.member // SIDE

    def at(self, part, du, dv):
        dx, dy = (du, dv) if part == 0 else (dv, du)
        return wrap(self.y + dy) * SIDE + wrap(self.x + dx)


class Place(Torus):
    def __init__(self):
        super().__init__()
        self.kind = lax.rem((self.x + 1) // 2, 2)
        self.parity = lax.rem(self.x, 2)
        self.pair_x = self.x + 1 - 2 * self.parity
        self.pair = self.y * SIDE + self.pair_x
        self.index = self.y * 2 + self.x // 2

    def column(self, f):
        return self.x + f * (3 - 2 * self.x)

    def row(self, dy):
        return wrap(self.y + dy)

    def near(self, f, dy):
        return self.row(dy) * SIDE + self.column(f)

    def pair_near(self, f, dy):
        return self.row(dy) * SIDE + self.pair_x + f * (3 - 2 * self.pair_x)


class PairGather:
    def __init__(self, place, own, slot, whole, send_sem, recv_sem):
        self.place, self.own, self.slot, self.whole = place, own, slot, whole
        self.send_sem, self.recv_sem = send_sem, recv_sem

    def copy(self, src, dst, part, f, dy, index):
        return pltpu.make_async_remote_copy(
            src_ref=src,
            dst_ref=dst,
            send_sem=self.send_sem.at[part],
            recv_sem=self.recv_sem.at[part, index],
            device_id={"member": self.place.near(f, dy)},
            device_id_type=MESH,
        )

    def ref(self, part, f, dy, which=None):
        return self.slot(self.place.column(f), self.place.row(dy), part, which)

    def move(self, part, f, dy, which, to_f, to_dy, index):
        ref = self.ref(part, f, dy, which)
        self.copy(ref, ref, part, to_f, to_dy, index).start()

    def wait(self, part, f, dy, index):
        ref = self.ref(part, f, dy)
        self.copy(ref, ref, part, 1, 0, index).wait_recv()

    def begin(self):
        for part, targets in ((0, ((1, 0), (0, 1), (0, -1))), (1, ((0, 1), (0, -1), (1, 0)))):
            for index, (f, dy) in enumerate(targets):
                self.copy(self.own(part), self.ref(part, 0, 0), part, f, dy, index).start()

    def cross_near(self):
        self.wait(0, 1, 0, 0)
        self.move(0, 1, 0, None, 0, 1, 3)
        self.move(0, 1, 0, None, 0, -1, 4)

    def round_near(self):
        self.wait(1, 0, -1, 0)
        self.move(1, 0, -1, 0, 0, 1, 3)
        self.move(1, 0, -1, None, 1, 0, 4)
        self.wait(1, 0, 1, 1)
        self.move(1, 0, 1, 1, 0, -1, 3)
        self.move(1, 0, 1, None, 1, 0, 5)

    def own_far(self):
        self.wait(0, 0, -1, 1)
        self.move(0, 0, -1, 0, 0, 1, 5)
        self.wait(0, 0, 1, 2)
        self.move(0, 0, 1, 1, 0, -1, 5)

    def round_far(self):
        self.wait(1, 0, 2, 3)
        self.move(1, 0, 2, None, 1, 0, 6)

    def cross_far(self):
        self.wait(0, 1, -1, 3)
        self.move(0, 1, -1, 0, 0, 1, 6)
        self.wait(0, 1, 1, 4)
        self.move(0, 1, 1, 1, 0, -1, 6)

    def middle(self):
        self.cross_near()
        self.round_near()

    def late(self):
        self.own_far()
        self.round_far()
        self.cross_far()

    def end(self, stage):
        if stage == 0:
            self.wait(1, 1, 0, 2)
        elif stage == 1:
            self.wait(1, 1, -1, 4)
            self.wait(1, 1, 1, 5)
        elif stage == 2:
            self.wait(0, 0, 2, 5)
        else:
            self.wait(0, 1, 2, 6)
            self.wait(1, 1, 2, 6)

    def sent(self):
        for part in (0, 1):
            ref = self.whole(part)
            self.copy(ref, ref, part, 1, 0, 0).wait_send()


class PlaneGather:
    order = (0, -1, 1, 2)

    def __init__(self, torus, own, slot, whole, send_sem, recv_sem):
        self.torus, self.own, self.slot, self.whole = torus, own, slot, whole
        self.send_sem, self.recv_sem = send_sem, recv_sem

    def copy(self, src, dst, part, du, dv, index):
        return pltpu.make_async_remote_copy(
            src_ref=src,
            dst_ref=dst,
            send_sem=self.send_sem.at[part],
            recv_sem=self.recv_sem.at[part, index],
            device_id={"member": self.torus.at(part, du, dv)},
            device_id_type=MESH,
        )

    def ref(self, part, du, dv):
        return self.slot(part, self.torus.at(part, du, dv))

    def begin(self):
        for part in (0, 1):
            for k in (1, 2, 3):
                self.copy(self.own(part), self.ref(part, 0, 0), part, -self.order[k], 0, k - 1).start()
        for part in (0, 1):
            self.spread(part, 0)

    def spread(self, part, q):
        here = self.ref(part, self.order[q], 0)
        src = self.own(part) if q == 0 else here
        for k in (1, 2, 3):
            self.copy(src, here, part, 0, -self.order[k], 3 * q + k + 2).start()

    def wait(self, part, du, dv, index):
        ref = self.ref(part, du, dv)
        self.copy(ref, ref, part, 1, 0, index).wait_recv()

    def middle(self):
        for q in (1, 2, 3):
            for part in (0, 1):
                self.wait(part, self.order[q], 0, q - 1)
                self.spread(part, q)

    def end(self):
        for q in range(SIDE):
            for part in (0, 1):
                for k in (1, 2, 3):
                    self.wait(part, self.order[q], self.order[k], 3 * q + k + 2)

    def sent(self):
        for part in (0, 1):
            ref = self.whole(part)
            self.copy(ref, ref, part, 1, 0, 0).wait_send()


def rotate(values, cosine, sine):
    return (values * cosine + pltpu.roll(values, HEAD_WIDTH // 2, 1) * sine).astype(BF16)


QKV_SPLIT = (((0, 144), (0, 80), (80, 64)), ((144, 112), (144, 64), (208, 48)))
OUT_SPLIT = (((0, 1152), (0, 576), (576, 576)), ((1152, 896), (1152, 448), (1600, 448)))


def cut(split, part, which):
    return split[part][0 if which is None else which + 1]


BLOCKS = ((0, 0), (1, 0), (0, -1), (0, 1), (1, -1), (1, 1), (0, 2), (1, 2))


def kernel(
    hidden_in, docs_in, qkv_in, out_in, down_in, up_in, gain_in, final_in, cos_ref, sin_ref,
    out_ref,
    wq, wo, h_all, nrm, proj, ctx_one, ctx_two, low, docs_next, gain_all, down_all, up_all, final_all,
    h_send, h_next, h_last, square, stat_own, stat_in, rows_out, rows_in, mean_own, mean_in, fin,
    pg_send, pg_recv, ag_send, ag_recv, local_sem, ctx_s, ctx_r, hop_s, hop_r, fwd_s, fwd_r,
    misc_s, misc_r, scatter_s, scatter_r,
):
    place = Place()
    member, kind, parity, index8 = place.member, place.kind, place.parity, place.index
    section = lax.axis_index("section")
    tensor = lax.axis_index("tensor")
    other = 1 - tensor
    sections = 8
    after = lax.rem(section + 1, sections)
    before = lax.rem(section + sections - 1, sections)
    both = (0, 1)

    barrier = pltpu.get_barrier_semaphore()

    def signal(device):
        pl.semaphore_signal(barrier, inc=1, device_id=device, device_id_type=MESH)

    def greet(i, carry):
        signal({"member": lax.rem(member + i, MEMBERS)})
        return carry

    lax.fori_loop(1, MEMBERS, greet, 0)
    signal({"tensor": other})
    signal({"member": place.pair, "tensor": other})
    for near in (after, before):
        signal({"section": near})
        signal({"section": near, "tensor": other})

    pending = []

    def local(src, dst, index):
        copy = pltpu.make_async_copy(src, dst, local_sem.at[index])
        copy.start()
        return copy

    def misc(src, dst, index, device):
        copy = pltpu.make_async_remote_copy(
            src, dst, misc_s.at[index], misc_r.at[index], device, MESH
        )
        pending.append(copy)
        return copy

    load_h = local(hidden_in, h_all.at[:, parity], 0)
    loads = [
        local(gain_in, gain_all.at[parity], 1),
        local(down_in, down_all.at[parity, tensor], 2),
        local(up_in, up_all.at[parity], 3),
        local(final_in, final_all.at[parity, tensor], 4),
        local(
            qkv_in.at[:, pl.ds(pl.multiple_of(kind * 768, 256), 768)],
            wq.at[pl.ds(pl.multiple_of(member * 256, 256), 256)],
            5,
        ),
    ]
    load_o = local(
        out_in.at[:, pl.ds(pl.multiple_of(tensor * 128, 128), 128)],
        wo.at[index8, pl.ds(pl.multiple_of(tensor * 1024, 1024), 1024)],
        6,
    )
    pl.semaphore_wait(barrier, MEMBERS - 1 + 6)

    def qkv_slot(of_pair):
        def slot(x, y, part, which):
            if of_pair:
                x = x + 1 - 2 * lax.rem(x, 2)
            lower, size = cut(QKV_SPLIT, part, which)
            return wq.at[pl.ds(pl.multiple_of((y * SIDE + x) * 256 + lower, 16), size)]

        return slot

    def own_qkv(part):
        lower, size = cut(QKV_SPLIT, part, None)
        return qkv_in.at[pl.ds(lower, size), pl.ds(pl.multiple_of(kind * 768, 256), 768)]

    def whole_qkv(part):
        return wq.at[pl.ds(0, 7 * cut(QKV_SPLIT, part, None)[1])]

    def out_slot(x, y, part, which):
        lower, size = cut(OUT_SPLIT, part, which)
        return wo.at[y * 2 + x // 2, pl.ds(lower, size)]

    def whole_out(part):
        return wo.at[pl.ds(0, 7), pl.ds(0, cut(OUT_SPLIT, part, None)[1])]

    wave_one = PairGather(place, own_qkv, qkv_slot(False), whole_qkv, pg_send.at[0], pg_recv.at[0])
    pair_slot = qkv_slot(True)
    wave_two = PairGather(
        place,
        lambda part: pair_slot(place.x, place.y, part, None),
        pair_slot,
        whole_qkv,
        pg_send.at[1],
        pg_recv.at[1],
    )
    wave_out = PairGather(
        place,
        lambda part: out_slot(place.x, place.y, part, None),
        out_slot,
        whole_out,
        pg_send.at[2],
        pg_recv.at[2],
    )

    to_pair = {"member": place.pair}
    to_pair_other = {"member": place.pair, "tensor": other}
    to_other = {"tensor": other}

    rows_of = lambda m: wq.at[pl.ds(pl.multiple_of(m * 256, 256), 256)]
    seed = misc(
        qkv_in.at[:, pl.ds(pl.multiple_of((1 - kind) * 768, 256), 768)], rows_of(member), 0, to_pair
    )
    seed.start()
    wave_one.begin()
    half_of = lambda a, t: h_all.at[t, a]
    share_h = misc(
        hidden_in.at[tensor], half_of(parity, tensor), 1, to_pair
    )
    share_out = misc(
        out_in.at[:, pl.ds(pl.multiple_of(other * 128, 128), 128)],
        wo.at[index8, pl.ds(pl.multiple_of(tensor * 1024, 1024), 1024)],
        2,
        to_other,
    )
    share_out.start()
    small = [misc(gain_in, gain_all.at[parity], 3, to_pair), misc(up_in, up_all.at[parity], 4, to_pair)]
    for k, device in enumerate((to_other, to_pair, to_pair_other)):
        small.append(misc(down_in, down_all.at[parity, tensor], 5 + k, device))
        small.append(misc(final_in, final_all.at[parity, tensor], 8 + k, device))
    small.append(misc(docs_in, docs_next, 11, {"section": after}))
    load_h.wait()
    loads[0].wait()

    def norm_first(a):
        def block(i, carry):
            r, j = i // 8, lax.rem(i, 8)
            h = h_all[r, a, pl.ds(pl.multiple_of(j * 16, 16), 16), :].astype(F32)
            scale = lax.rsqrt(jnp.mean(h * h, axis=-1, keepdims=True) + EPS)
            nrm[pl.ds(pl.multiple_of(r * 256 + a * 128 + j * 16, 16), 16), :] = (
                h * scale * gain_all[a]
            ).astype(BF16)
            return carry

        lax.fori_loop(0, ROWS // 16, block, 0)

    norm_first(parity)

    def project(lower, upper):
        def block(n, carry):
            rows = pl.ds(pl.multiple_of(n // 3 * 256, 256), 256)
            columns = pl.ds(pl.multiple_of(lax.rem(n, 3) * 256, 256), 256)
            proj[rows, columns] = jnp.dot(nrm[rows, :], wq[:, columns], preferred_element_type=F32)
            return carry

        lax.fori_loop(lower, upper, block, 0)

    ahead = lax.broadcasted_iota(jnp.int32, (SEQ, SEQ), 0) >= lax.broadcasted_iota(
        jnp.int32, (SEQ, SEQ), 1
    )
    head = 2 * tensor + kind

    def ctx_copy(ctx, tick, s, which):
        owner = 2 * tensor + (1 - kind if which == 2 else kind)
        ref = ctx.at[
            pl.ds(pl.multiple_of(s * SEQ, SEQ), SEQ), pl.ds(pl.multiple_of(owner * 512, 512), 512)
        ]
        return pltpu.make_async_remote_copy(
            ref, ref, ctx_s.at[tick, which, s], ctx_r.at[tick, which, s],
            to_pair if which == 1 else to_other, MESH,
        )

    def ctx_arrived(ctx, tick, s, which):
        t = tensor if which == 1 else other
        owner = 2 * t + (kind if which == 0 else 1 - kind)
        ref = ctx.at[
            pl.ds(pl.multiple_of(s * SEQ, SEQ), SEQ), pl.ds(pl.multiple_of(owner * 512, 512), 512)
        ]
        pltpu.make_async_remote_copy(
            ref, ref, ctx_s.at[tick, which, s], ctx_r.at[tick, which, s], to_other, MESH
        ).wait_recv()

    def attend(docs_ref, ctx, tick, lower, upper):
        def sequence(s, carry):
            rows = pl.ds(pl.multiple_of(s * SEQ, SEQ), SEQ)
            numbers = docs_ref[pl.ds(s // 2, 1), :]
            numbers = jnp.broadcast_to(numbers, (SEQ, SEQ)).astype(F32)
            allowed = ahead & (numbers == numbers.T)
            allowed = jnp.concatenate([allowed.astype(F32)] * GROUP, axis=0) > 0.5
            cosine, sine = cos_ref[...], sin_ref[...]

            def piece(g):
                return proj[rows, g * 128 : g * 128 + 128]

            queries = jnp.concatenate(
                [rotate(piece(g), cosine, sine) for g in range(GROUP)], axis=0
            )
            keys = rotate(piece(GROUP), cosine, sine)
            values = piece(GROUP + 1).astype(BF16)
            scores = lax.dot_general(
                queries, keys, (((1,), (1,)), ((), ())), preferred_element_type=F32
            ) * (1.0 / math.sqrt(HEAD_WIDTH))
            scores = jnp.where(allowed, scores, -1e30)
            weights = jnp.exp(scores - jnp.max(scores, axis=-1, keepdims=True))
            weights = (weights / jnp.sum(weights, axis=-1, keepdims=True)).astype(BF16)
            context = jnp.dot(weights, values, preferred_element_type=F32).astype(BF16)
            for g in range(GROUP):
                columns = pl.ds(pl.multiple_of(head * 512 + g * 128, 128), 128)
                ctx[rows, columns] = context[g * SEQ : (g + 1) * SEQ]
            ctx_copy(ctx, tick, s, 1).start()
            ctx_copy(ctx, tick, s, 0).start()
            return carry

        lax.fori_loop(lower, upper, sequence, 0)

    def collect(ctx, tick, r):
        for a in both:
            ctx_arrived(ctx, tick, 2 * r + a, 1)
            ctx_copy(ctx, tick, 2 * r + a, 2).start()
        for a in both:
            ctx_arrived(ctx, tick, 2 * r + a, 0)
            ctx_arrived(ctx, tick, 2 * r + a, 2)
        for a in both:
            rows = slice((2 * r + a) * SEQ, (2 * r + a + 1) * SEQ)
            for block in both:
                low[block, rows] = lax.dot_general(
                    ctx[rows, block * 1024 : block * 1024 + 1024],
                    down_all[a, block],
                    (((1,), (1,)), ((), ())),
                    preferred_element_type=F32,
                ).astype(BF16)

    wave_one.middle()
    share_h.start()
    for copy in small:
        copy.start()
    seed_in = pltpu.make_async_remote_copy(
        rows_of(place.pair), rows_of(place.pair), misc_s.at[0], misc_r.at[0], to_pair, MESH
    )
    seed_in.wait_recv()
    wave_two.begin()
    wave_one.late()
    wave_two.middle()
    pltpu.make_async_remote_copy(
        half_of(1 - parity, tensor), half_of(1 - parity, tensor), misc_s.at[1], misc_r.at[1],
        to_pair, MESH,
    ).wait_recv()
    pass_h = misc(half_of(1 - parity, tensor), half_of(1 - parity, tensor), 12, to_other)
    pass_h.start()
    load_o.wait()
    share_in = wo.at[index8, pl.ds(pl.multiple_of(other * 1024, 1024), 1024)]
    pltpu.make_async_remote_copy(
        share_in, share_in, misc_s.at[2], misc_r.at[2], to_other, MESH
    ).wait_recv()
    wave_two.late()
    pltpu.make_async_remote_copy(
        half_of(1 - parity, other), half_of(1 - parity, other), misc_s.at[12], misc_r.at[12],
        to_other, MESH,
    ).wait_recv()
    small[0].wait_recv()
    norm_first(1 - parity)
    wave_out.begin()
    for copy in small[1:]:
        copy.wait_recv()
    for copy in loads[1:]:
        copy.wait()
    for stage in range(4):
        wave_one.end(stage)
        wave_two.end(stage)
    project(0, 3)
    attend(docs_in, ctx_one, 0, 0, 2)
    project(3, 6)
    attend(docs_in, ctx_one, 0, 2, 4)
    wave_out.cross_near()
    wave_out.own_far()
    wave_out.round_near()

    def block_member(i, pair=False):
        f, dy = BLOCKS[i]
        return place.pair_near(f, dy) if pair else place.near(f, dy)

    def columns_of(m):
        return pl.ds(pl.multiple_of(m * 256 + tensor * 128, 128), 128)

    def summed(ctx, r, weights_of, up_of):
        total = None
        rows = slice(r * 256, r * 256 + 256)
        for block in both:
            main = jnp.dot(
                ctx[rows, block * 1024 : block * 1024 + 1024],
                weights_of(block),
                preferred_element_type=F32,
            )
            extra = jnp.concatenate(
                [
                    jnp.dot(
                        low[block, (2 * r + a) * SEQ : (2 * r + a + 1) * SEQ],
                        up_of(a),
                        preferred_element_type=F32,
                    )
                    for a in both
                ],
                axis=0,
            )
            value = (main + extra).astype(BF16).astype(F32)
            total = value if total is None else total + value
        return total

    def block_copy(ref, dst, kind_of, n, device):
        send, recv = (hop_s.at[n], hop_r.at[n]) if kind_of == 3 else (
            fwd_s.at[kind_of, n], fwd_r.at[kind_of, n]
        )
        return pltpu.make_async_remote_copy(ref, dst, send, recv, device, MESH)

    steps = [(i, r) for lower in (0, 4) for r in both for i in range(lower, lower + 4)]

    def own_ref(n):
        i, r = steps[n]
        return h_next.at[block_member(i) * 2 + tensor, r]

    def hop_copy(n):
        return block_copy(h_send.at[n], own_ref(n), 3, n, {"section": after})

    def start_block(n):
        i, r = steps[n]
        f, dy = BLOCKS[i]
        slot = place.row(dy) * 2 + place.column(f) // 2
        columns = columns_of(block_member(i))
        total = summed(
            ctx_one, r, lambda block: wo[slot, block * 1024 : block * 1024 + 1024],
            lambda a: up_all[a, :, columns],
        )
        for a in both:
            rows = slice(a * SEQ, a * SEQ + SEQ)
            h_send[n, rows] = (h_all[r, a, :, columns].astype(F32) + total[rows]).astype(BF16)
        hop_copy(n).start()

    def pair_ref(n):
        i, r = steps[n]
        return h_next.at[block_member(i, True) * 2 + tensor, r]

    def pass_own(n, device, kind_of):
        return block_copy(own_ref(n), own_ref(n), kind_of, n, device)

    def pass_pair(n):
        return block_copy(pair_ref(n), pair_ref(n), 2, n, to_other)

    def arrive(n):
        hop_copy(n).wait_recv()
        pass_own(n, to_pair, 0).start()
        pass_own(n, to_other, 1).start()

    def relay(n):
        block_copy(pair_ref(n), pair_ref(n), 0, n, to_pair).wait_recv()
        pass_pair(n).start()

    def other_ref(n, pair):
        i, r = steps[n]
        return h_next.at[block_member(i, pair) * 2 + other, r]

    def run(lower, upper):
        for n in range(lower, upper):
            start_block(n)
            if n >= 3:
                arrive(n - 3)
            if n >= 5:
                relay(n - 5)

    collect(ctx_one, 0, 0)
    wave_out.end(0)
    run(0, 4)
    wave_out.cross_far()
    collect(ctx_one, 0, 1)
    run(4, 6)
    wave_out.round_far()
    run(6, 8)
    wave_out.end(1)
    run(8, 10)
    wave_out.end(2)
    run(10, 11)
    wave_out.end(3)
    run(11, 16)
    relay(11)
    arrive(13)
    arrive(14)

    def complete(r):
        for n in range(16):
            if steps[n][1] == r:
                ref = other_ref(n, False)
                block_copy(ref, ref, 1, n, to_other).wait_recv()
                ref = other_ref(n, True)
                block_copy(ref, ref, 2, n, to_other).wait_recv()

    def norm_second(i, carry):
        r, j = i // 8, lax.rem(i, 8)
        a = j // 4
        rows = pl.ds(pl.multiple_of(j * 32, 32), 32)
        total = jnp.zeros((32, 128), F32)
        for block in range(32):
            h = h_next[block, r, rows, :].astype(F32)
            total = total + h * h
        scale = lax.rsqrt(jnp.sum(total, axis=-1, keepdims=True) * (1.0 / WIDTH) + EPS)
        scale = jnp.broadcast_to(scale, (32, 128))
        for block in range(32):
            columns = slice(block * 128, block * 128 + 128)
            h = h_next[block, r, rows, :].astype(F32)
            nrm[pl.ds(pl.multiple_of(i * 32, 32), 32), columns] = (
                h * scale * gain_all[a, :, columns]
            ).astype(BF16)
        return carry

    complete(0)
    lax.fori_loop(0, 8, norm_second, 0)
    arrive(15)
    relay(12)
    relay(13)
    project(0, 3)
    relay(14)
    relay(15)
    attend(docs_next, ctx_two, 1, 0, 2)
    complete(1)
    lax.fori_loop(8, 16, norm_second, 0)
    project(3, 6)
    attend(docs_next, ctx_two, 1, 2, 4)

    def pair_members(y):
        return y * SIDE + kind, y * SIDE + 3 - kind

    def up_pair(a, y):
        return jnp.concatenate([up_all[a, :, columns_of(m)] for m in pair_members(y)], axis=1)

    def last_output(r):
        square[r] = jnp.zeros((ROWS, 128), F32)

        def last_block(y, carry):
            total = summed(
                ctx_two,
                r,
                lambda block: jnp.concatenate(
                    [wo[2 * y + k, block * 1024 : block * 1024 + 1024] for k in both], axis=1
                ),
                lambda a: up_pair(a, y),
            )
            for k, m in enumerate(pair_members(y)):
                columns = slice(k * 128, k * 128 + 128)
                h = h_next[m * 2 + tensor, r].astype(F32) + total[:, columns]
                h = h.astype(BF16)
                h_last[r, y, :, columns] = h
                h = h.astype(F32)
                square[r] += h * h
            return carry

        lax.fori_loop(0, SIDE, last_block, 0)

    def send_stats(r):
        stat_own[r] = jnp.zeros((8, 128), F32)
        for a in both:
            stat_own[r, a : a + 1, :] = jnp.sum(
                square[r, a * SEQ : a * SEQ + SEQ].T, axis=0, keepdims=True
            )
        stats = [
            misc(stat_own.at[r], stat_in.at[r, k], 13 + 3 * r + k, device)
            for k, device in enumerate((to_other, to_pair, to_pair_other))
        ]
        for copy in stats:
            copy.start()
        return stats

    def rows_at(r, i):
        return rows_out.at[r, pl.ds(pl.multiple_of(i * 16, 16), 16)]

    def scatter_rows(r, stats):
        for copy in stats:
            copy.wait_recv()
        total = stat_own[r] + stat_in[r, 0] + stat_in[r, 1] + stat_in[r, 2]
        scales = lax.rsqrt(total * (1.0 / WIDTH) + EPS)
        column_scale = [jnp.broadcast_to(scales[a : a + 1], (128, 128)).T for a in both]
        for y in range(SIDE):
            for k, m in enumerate(pair_members(y)):
                lower = (m - (y // 2) * 8) * 256 + tensor * 128
                gains = [
                    final_all[a, y // 2, :, pl.ds(pl.multiple_of(lower, 128), 128)] for a in both
                ]
                columns = slice(k * 128, k * 128 + 128)
                value = sum(
                    h_last[r, y, a * SEQ : a * SEQ + SEQ, columns].astype(F32)
                    * column_scale[a]
                    * gains[a]
                    for a in both
                )
                rows_out[r, :, (2 * y + k) * 128 : (2 * y + k + 1) * 128] = value.astype(BF16)

        def scatter(i, carry):
            f, dy = lax.rem(i, 2), i // 2
            x, y = place.column(f), place.row(dy)
            pltpu.make_async_remote_copy(
                rows_at(r, y * 2 + x // 2), rows_in.at[r, index8], scatter_s.at[r], scatter_r.at[r],
                {"member": y * SIDE + x}, MESH,
            ).start()
            return carry

        lax.fori_loop(1, 8, scatter, 0)
        return local(rows_at(r, index8), rows_in.at[r, index8], 7 + r)

    def seven(r):
        ref = rows_in.at[r, pl.ds(0, 7)]
        return pltpu.make_async_remote_copy(
            ref, ref, scatter_s.at[r], scatter_r.at[r], to_other, MESH
        )

    def average(r, keep):
        keep.wait()
        seven(r).wait_recv()
        total = rows_in[r, 0].astype(F32)
        for i in range(1, 8):
            total = total + rows_in[r, i].astype(F32)
        total = (total * (1.0 / MEMBERS)).astype(BF16)
        for half in both:
            mean_own[r, half] = total[:, half * 512 : half * 512 + 512]
        misc(mean_own.at[r, tensor], mean_in.at[r, tensor], 19 + 2 * r, {"section": after}).start()
        misc(
            mean_own.at[r, other], mean_in.at[r, tensor], 20 + 2 * r,
            {"section": after, "tensor": other},
        ).start()

    def hopped(r):
        for half, index in ((tensor, 19 + 2 * r), (other, 20 + 2 * r)):
            ref = mean_in.at[r, half]
            pltpu.make_async_remote_copy(
                ref, ref, misc_s.at[index], misc_r.at[index], to_other, MESH
            ).wait_recv()

    def gather_of(r):
        return PlaneGather(
            place,
            lambda part: mean_in.at[r, part],
            lambda part, slot: fin.at[r, slot, part],
            lambda part: fin.at[r, pl.ds(0, 15), part],
            ag_send.at[r],
            ag_recv.at[r],
        )

    collect(ctx_two, 1, 0)
    last_output(0)
    keep_zero = scatter_rows(0, send_stats(0))
    collect(ctx_two, 1, 1)
    last_output(1)
    stats_one = send_stats(1)
    average(0, keep_zero)
    keep_one = scatter_rows(1, stats_one)
    final_zero, final_one = gather_of(0), gather_of(1)
    hopped(0)
    final_zero.begin()
    fin[0, member] = mean_in[0]
    average(1, keep_one)
    final_zero.middle()
    hopped(1)
    final_one.begin()
    fin[1, member] = mean_in[1]
    final_zero.end()

    def place_rows(r):
        for m in range(MEMBERS):
            x, y = m % SIDE, m // SIDE
            side = ((x + 1) // 2) % 2
            lower = r * SEQ + (y * 2 + x // 2) * 16
            for part in both:
                for s in range(4):
                    column = (s // 2 * SIDE + (side if s % 2 == 0 else 3 - side)) * 256 + part * 128
                    out_ref[lower : lower + 16, column : column + 128] = fin[
                        r, m, part, :, s * 128 : s * 128 + 128
                    ]

    final_one.middle()
    place_rows(0)
    final_one.end()
    place_rows(1)

    for wave in (wave_one, wave_two, wave_out):
        wave.sent()
    final_zero.sent()
    final_one.sent()
    for tick, ctx in enumerate((ctx_one, ctx_two)):
        for which in range(3):
            for s in range(4):
                ctx_copy(ctx, tick, s, which).wait_send()
    for n in range(16):
        hop_copy(n).wait_send()
        pass_own(n, to_pair, 0).wait_send()
        pass_own(n, to_other, 1).wait_send()
        pass_pair(n).wait_send()
    for copy in pending:
        copy.wait_send()
    for r in both:
        seven(r).wait_send()


def per_device(
    hidden_input,
    document_index,
    query_key_value_weight,
    output_weight,
    adapter_down,
    adapter_up,
    attention_gain,
    final_norm_gain,
):
    cosine, sine = rope_tables()
    vmem = pl.BlockSpec(memory_space=pltpu.VMEM)
    anywhere = pl.BlockSpec(memory_space=pl.ANY)
    dma = pltpu.SemaphoreType.DMA
    averaged = pl.pallas_call(
        kernel,
        out_shape=jax.ShapeDtypeStruct((ROWS, WIDTH // 2), BF16),
        in_specs=[anywhere, vmem, anywhere, anywhere] + [vmem] * 6,
        out_specs=vmem,
        scratch_shapes=[
            pltpu.VMEM((WIDTH, 768), BF16),
            pltpu.VMEM((8, 2048, 128), BF16),
            pltpu.VMEM((2, 2, SEQ, WIDTH), BF16),
            pltpu.VMEM((2 * ROWS, WIDTH), BF16),
            pltpu.VMEM((2 * ROWS, 768), F32),
            pltpu.VMEM((2 * ROWS, 2048), BF16),
            pltpu.VMEM((2 * ROWS, 2048), BF16),
            pltpu.VMEM((2, 2 * ROWS, 16), BF16),
            pltpu.VMEM((2, SEQ), jnp.int32),
            pltpu.VMEM((2, 1, WIDTH), F32),
            pltpu.VMEM((2, 2, 16, 1024), BF16),
            pltpu.VMEM((2, 16, WIDTH), BF16),
            pltpu.VMEM((2, 2, 1, WIDTH // 2), F32),
            pltpu.VMEM((16, ROWS, 128), BF16),
            pltpu.VMEM((32, 2, ROWS, 128), BF16),
            pltpu.VMEM((2, SIDE, ROWS, 256), BF16),
            pltpu.VMEM((2, ROWS, 128), F32),
            pltpu.VMEM((2, 8, 128), F32),
            pltpu.VMEM((2, 3, 8, 128), F32),
            pltpu.VMEM((2, SEQ, 1024), BF16),
            pltpu.VMEM((2, 8, 16, 1024), BF16),
            pltpu.VMEM((2, 2, 16, 512), BF16),
            pltpu.VMEM((2, 2, 16, 512), BF16),
            pltpu.VMEM((2, MEMBERS, 2, 16, 512), BF16),
            dma((3, 2)),
            dma((3, 2, 7)),
            dma((2, 2)),
            dma((2, 2, 15)),
            dma((9,)),
            dma((2, 3, 4)),
            dma((2, 3, 4)),
            dma((16,)),
            dma((16,)),
            dma((3, 16)),
            dma((3, 16)),
            dma((23,)),
            dma((23,)),
            dma((2,)),
            dma((2,)),
        ],
        compiler_params=pltpu.CompilerParams(
            collective_id=0, has_side_effects=True, vmem_limit_bytes=58 * 1024 * 1024
        ),
        name="relay",
    )(
        hidden_input.reshape(2, SEQ, WIDTH),
        document_index[0],
        query_key_value_weight[0].reshape(256, 1536),
        output_weight[0],
        adapter_down[0, 0].T,
        adapter_up[0, 0],
        attention_gain[0],
        final_norm_gain,
        jnp.asarray(cosine),
        jnp.asarray(sine),
    )
    return averaged.reshape(1, 2, SEQ, WIDTH // 2)


def solution(mesh):
    return jax.shard_map(
        per_device,
        mesh=mesh,
        in_specs=(
            P("member", "section", None, None, None),
            P("section", None, None),
            P("section", "member", "tensor", None),
            P("section", "tensor", "member"),
            P("member", "section", "tensor", None),
            P("member", "section", None, None),
            P("member", "section", None),
            P("member", "tensor"),
        ),
        out_specs=P("section", None, None, "tensor"),
        check_vma=False,
    )
```
